32 devices in a mesh: grp: 2 (over core), seq: 8 (over z, x), wsh: 2 (over y).
Axes of the slice: x: 2, y: 2, z: 4, core: 2. Of those that a mesh axis runs over, the one named last changes fastest.
Arguments:
- block_input: bfloat16 [6144, 768], P(('grp', 'seq', 'wsh')), parts along dimension 0, may hold values from -6 to 6
- w_qkv: bfloat16 [3, 768, 768], P(None, ('seq', 'wsh')), may hold values from -0.21875 to 0.21875
- w_attn_out: bfloat16 [768, 768], P(('seq', 'wsh')), may hold values from -4 to 4
- w_router: bfloat16 [768, 16], P(('seq', 'wsh')), may hold values from -0.119628906 to 0.119628906
- gain_attn: bfloat16 [768], P(('seq', 'wsh')), may hold values from 0.25 to 1.75
- gain_moe: bfloat16 [768], P(('seq', 'wsh')), may hold values from 0.25 to 1.75
- rel_bias: bfloat16 [384], P(('seq', 'wsh')), may hold values from -4 to 4
- w_in: bfloat16 [16, 768, 3072], P(('seq', 'wsh')), may hold values from -0.21875 to 0.21875
- w_out: bfloat16 [16, 3072, 768], P(('seq', 'wsh')), may hold values from -0.21875 to 0.21875
- routes: int32 [6144, 2], P(('grp', 'seq', 'wsh')), parts along dimension 0, may hold values from 0 to 15, all different within a row; in each aligned block of 192 rows (0 to 191, 192 to 383, ...) at most 48 rows name the same one
- segment_ids: int32 [6144], P('grp'), parts along dimension 0, may hold values from 0 to 3, as said below
- bucket_table: int32 [2304], replicated, may hold values from 0 to 31, as said below
- out_grad: bfloat16 [6144, 768], P(('grp', 'seq', 'wsh')), parts along dimension 0, may hold values from -6 to 6
Outputs:
- block_output: bfloat16 [6144, 768], P(('grp', 'seq', 'wsh')), parts along dimension 0
- input_grad: float32 [6144, 768], P(('grp', 'seq', 'wsh')), parts along dimension 0
- w_qkv_grad: float32 [6, 768, 768], P('grp', ('seq', 'wsh')), parts along dimension 0
- w_attn_out_grad: float32 [1536, 768], P(('grp', 'seq', 'wsh')), parts along dimension 0
- w_router_grad: float32 [1536, 16], P(('grp', 'seq', 'wsh')), parts along dimension 0
- gain_attn_grad: float32 [1536], P(('grp', 'seq', 'wsh')), parts along dimension 0
- gain_moe_grad: float32 [1536], P(('grp', 'seq', 'wsh')), parts along dimension 0
- rel_bias_grad: float32 [768], P(('grp', 'seq', 'wsh')), parts along dimension 0
- w_in_grad: float32 [32, 768, 3072], P(('grp', 'seq', 'wsh')), parts along dimension 0
- w_out_grad: float32 [32, 3072, 768], P(('grp', 'seq', 'wsh')), parts along dimension 0
The draws below stay inside these ranges and needn't reach their ends.
There are 2 independent parts, one for each index of `grp`. The reference program is written for one: setup_inputs(seed, part) draws one part's arguments, and reference() takes and returns one part's arrays. A program takes and returns all parts, laid end to end along the dimension named above; an argument that names none is the same for every part. Nothing has to cross between parts.
Inputs may be any that keep to these rules, and one draw needn't show every extreme that they name: `segment_ids`: the first 1536 tokens are the prompt, id 0; the rest are the continuations 1 to 3 in order, each one contiguous run of at most 768 tokens, one of exactly 768. `routes`: each row names two different experts; among the rows of one device no expert is named more than 48 times, and in some device one expert exactly 48 times. `bucket_table`: entry d is d for d below 16; beyond that the entries never fall and rise by at most one from one entry to the next, and the last is 31.
All inputs are finite; a program needn't handle non-finite values.
Results may differ from the reference program's by a relative error of at most 0.023.
Values may be sent and summed in bfloat16 or wider, within the bound.
No kernel may reach another device: no remote copies, remote signals or barrier semaphores. Data moves between devices by JAX's collectives and lax.ppermute only.
A program may use at most 256 MiB of HBM per device.

```python
import math
import jax
import jax.numpy as jnp
import numpy as np
from jax import lax

D = 768
HEADS = 12
HEAD_DIM = 64
FF = 3072
NBUCKET = 32
TOK_DEV = 192
TOKENS = 3072
EXPERTS = 16
NCONT = 3
CONT_MOST = 768
MAXREL = 2304
CAP = 48
N_SEQ = 8
N_WSH = 2


def draw_segment_ids(key, part):
    prompt_rows = TOKENS // 2
    other_count = NCONT - 1
    rest_rows = prompt_rows - CONT_MOST
    base_rows = rest_rows // other_count
    spare_rows = rest_rows - base_rows * other_count
    wiggle = base_rows // 4
    shifts = jax.random.randint(jax.random.fold_in(key, 11), (other_count,), 0, wiggle + 1)
    shorter = base_rows + shifts - jnp.roll(shifts, 1)
    shorter = shorter.at[0].add(spare_rows)
    longest = jnp.mod(jnp.asarray(part, jnp.int32), NCONT).astype(jnp.int32)
    places = jnp.arange(NCONT, dtype=jnp.int32)
    pick_at = jnp.clip(places - (places > longest).astype(jnp.int32), 0, other_count - 1)
    lengths = jnp.where(places == longest, CONT_MOST, shorter[pick_at]).astype(jnp.int32)
    finishes = jnp.cumsum(lengths)
    offsets = jnp.arange(prompt_rows, dtype=jnp.int32)
    numbers = 1 + jnp.sum((offsets[:, None] >= finishes[None, :]).astype(jnp.int32), axis=1)
    return jnp.concatenate([jnp.zeros((prompt_rows,), jnp.int32), numbers.astype(jnp.int32)])


def draw_bucket_table(key, part):
    exact_span = 16
    boundary_count = NBUCKET - exact_span - 1
    boundaries = jax.random.permutation(jax.random.fold_in(key, 21), MAXREL - exact_span - 1)[:boundary_count] + exact_span + 1
    distance = jnp.arange(MAXREL, dtype=jnp.int32)
    coarse = exact_span + jnp.sum((distance[:, None] >= boundaries[None, :]).astype(jnp.int32), axis=1)
    return jnp.where(distance < exact_span, distance, coarse).astype(jnp.int32)


def steps_of(rng, extent, shards, least, top_value):
    def one(position, shards_of):
        draws = jax.random.uniform(jax.random.fold_in(jax.random.fold_in(rng, 6), position), (shards_of,), jnp.float32, least / len(shards), top_value / len(shards))
        return jnp.repeat(jnp.exp(draws), extent[position] // shards_of).reshape((-1,) + (1,) * (len(extent) - position - 1))

    factor_of = one(*shards[0])
    for cut in shards[1:]:
        factor_of = factor_of * one(*cut)
    return factor_of


def assign_block(own_key, own, number, rows, count, top, most, slope):
    ranking = jax.random.permutation(own_key, count)
    heavy_load, common = load_shares(count, rows * top, most, slope, True), load_shares(count, rows * top, most, slope, False)
    places = jnp.arange(count)

    def named(tallies, offset_by):
        used = int((tallies > 0).sum())
        fixed = max(1, used // 4)
        moved = fixed + (places - fixed + offset_by * (used - fixed)) % max(1, count - fixed)
        return jnp.zeros((count,), jnp.int32).at[ranking[jnp.where(places < fixed, places, moved)]].set(jnp.asarray(tallies, jnp.int32))

    tallies = jnp.where(number % 4 == 0, named(heavy_load, number // 4), named(common, number - number // 4 - 1))
    mixed = jax.random.permutation(jax.random.fold_in(own, 3), count)
    source_of, receiver = mixed[0:count // 2 * 2:2], mixed[1:count // 2 * 2:2]
    room = jnp.minimum(tallies[source_of] - 1, most - tallies[receiver]) // 2
    room = jnp.where((source_of == ranking[0]) | (receiver == ranking[0]) | (tallies[receiver] == 0), 0, jnp.maximum(room, 0))
    moved = jax.random.randint(jax.random.fold_in(own, 4), (count // 2,), 0, 1 << 20) % (room + 1)
    tallies = tallies.at[source_of].add(-moved).at[receiver].add(moved)
    items = jnp.searchsorted(jnp.cumsum(tallies), jnp.arange(rows * top), side="right").astype(jnp.int32)
    table = items.reshape(top, rows).T
    table = table[jax.random.permutation(jax.random.fold_in(own, 1), rows)]
    offset_by = jax.random.randint(jax.random.fold_in(own, 2), (rows, 1), 0, top)
    return jnp.take_along_axis(table, (jnp.arange(top)[None, :] + offset_by) % top, axis=1)


def load_shares(count, total, reach, skew, full):
    weights = [(1 << 20) // math.isqrt(standing ** skew) + 1 for standing in range(1, count + 1)]
    largest = reach if full else min(reach, max(-(-total // count), total * weights[0] // sum(weights)))
    least = 1 if total - largest >= count - 1 else 0
    given, rest = [largest] + [least] * (count - 1), total - largest - least * (count - 1)
    while rest > 0:
        movable = [i for i in range(1, count) if given[i] < largest] or [i for i in range(1, count) if given[i] < reach]
        mass, left = sum([weights[i] for i in movable]), rest
        for i in movable:
            addition = min(reach - given[i], max(1, left * weights[i] // mass), rest)
            given[i] = given[i] + addition
            rest = rest - addition
    return np.array(given)


def normal_values(key, extent, spread, limit, cuts=(), kind=jnp.bfloat16):
    factor_of = steps_of(key, extent, cuts, -0.22, 0.18) if cuts else 1.0
    array = jax.random.normal(key, extent, jnp.float32) * spread * factor_of
    return jnp.minimum(jnp.maximum(array, -limit), limit).astype(kind)


def setup_inputs(seed: int = 0, part: int = 0) -> dict:
    key_list = jax.random.split(jax.random.key(seed), 14)
    own_keys = jax.random.split(jax.random.fold_in(key_list[13], part), 14)
    block_input = normal_values(own_keys[0], (TOKENS, D), 1.0, 6.0, ((0, 16),))
    w_qkv = normal_values(key_list[1], (3, D, D), D ** -0.5, 0.21875, ((1, 16),))
    w_attn_out = normal_values(key_list[2], (D, D), 1.0, 4.0, ((0, 16),))
    w_router = normal_values(key_list[3], (D, EXPERTS), 0.027, 0.119628906, ((0, 16),))
    gain_attn = jnp.clip(1.0 + 0.15 * jax.random.normal(key_list[4], (D,), jnp.float32), 0.25, 1.75).astype(jnp.bfloat16)
    gain_moe = jnp.clip(1.0 + 0.15 * jax.random.normal(key_list[5], (D,), jnp.float32), 0.25, 1.75).astype(jnp.bfloat16)
    rel_bias = normal_values(key_list[6], (HEADS * NBUCKET,), 1.0, 4.0, ((0, 16),))
    w_in = normal_values(key_list[7], (EXPERTS, D, FF), D ** -0.5, 0.21875, ((0, 16),))
    w_out = normal_values(key_list[8], (EXPERTS, FF, D), (FF // 4) ** -0.5, 0.21875, ((0, 16),))
    routes_keys = jax.random.split(jax.random.fold_in(own_keys[9], 1), TOKENS // TOK_DEV)
    routes_turns = jax.random.permutation(jax.random.fold_in(own_keys[9], 3), TOKENS // TOK_DEV)
    routes = jax.vmap(lambda own, number: assign_block(jax.random.fold_in(own_keys[9], 2), own, number, TOK_DEV, EXPERTS, 2, CAP, 2))(routes_keys, routes_turns).reshape((TOKENS, 2))
    segment_ids = draw_segment_ids(jax.random.fold_in(jax.random.fold_in(key_list[13], part), 71), part)
    bucket_table = draw_bucket_table(jax.random.fold_in(key_list[13], 71), part)
    out_grad = normal_values(own_keys[12], (TOKENS, D), 1.0, 6.0, ((0, 16),))
    return dict(block_input=block_input, w_qkv=w_qkv, w_attn_out=w_attn_out, w_router=w_router, gain_attn=gain_attn, gain_moe=gain_moe, rel_bias=rel_bias, w_in=w_in, w_out=w_out, routes=routes, segment_ids=segment_ids, bucket_table=bucket_table, out_grad=out_grad)


EPSILON = 1e-06
NEGATIVE = -1e+30

@jax.custom_vjp
def low(v):
    return lax.optimization_barrier(v.astype(jnp.bfloat16)).astype(jnp.float32)

@jax.custom_vjp
def low_back(v):
    return v

def low_keep(v):
    return (low(v), None)

def low_pass(kept, grad):
    return (grad,)

def back_keep(v):
    return (v, None)

def back_low(kept, grad):
    return (low(grad),)
low.defvjp(low_keep, low_pass)
low_back.defvjp(back_keep, back_low)

def normalize(values, gain_vec):
    return values * lax.rsqrt(lax.optimization_barrier(jnp.mean(values * values, axis=-1, keepdims=True)) + EPSILON) * gain_vec

def positions_of(segment_ids):
    total_rows = segment_ids.shape[0]
    numbers = jnp.arange(total_rows, dtype=jnp.int32)
    fresh_start = jnp.logical_or(numbers == 0, segment_ids != jnp.roll(segment_ids, 1))
    begins = lax.cummax(jnp.where(fresh_start, numbers, 0), axis=0)
    return jnp.where(segment_ids == 0, numbers, numbers - begins + total_rows // 2).astype(jnp.int32)

def slots_of(routes):
    devices = N_SEQ * N_WSH
    flat_routes = routes.reshape(devices, TOK_DEV * 2)
    route_hits = (flat_routes[:, :, None] == jnp.arange(EXPERTS, dtype=jnp.int32)[None, None, :]).astype(jnp.int32)
    slot_ranks = lax.optimization_barrier(jnp.sum(route_hits * (jnp.cumsum(route_hits, axis=1) - 1), axis=2))
    sources = jnp.arange(devices, dtype=jnp.int32)[:, None]
    return (flat_routes * (devices * CAP) + sources * CAP + slot_ranks).reshape(-1).astype(jnp.int32)

def attention(queries, keys_all, values_all, bias_table, segment_ids, positions, bucket_table):
    total_rows = queries.shape[0]
    block_rows = min(512, total_rows)
    key_heads = keys_all.reshape(total_rows, HEADS, HEAD_DIM)
    value_heads = values_all.reshape(total_rows, HEADS, HEAD_DIM)
    key_index = jnp.arange(total_rows, dtype=jnp.int32)

    def query_block(block_id):
        first_row = block_id * block_rows
        query_rows = lax.dynamic_slice_in_dim(queries, first_row, block_rows).reshape(block_rows, HEADS, HEAD_DIM)
        row_index = first_row + jnp.arange(block_rows, dtype=jnp.int32)
        row_seg = lax.dynamic_slice_in_dim(segment_ids, first_row, block_rows)
        row_pos = lax.dynamic_slice_in_dim(positions, first_row, block_rows)
        raw_scores = low_back(jnp.einsum('qhd,khd->hqk', query_rows, key_heads, precision=lax.Precision.HIGHEST) * 0.125)
        distance = jnp.clip(row_pos[:, None] - positions[None, :], 0, MAXREL - 1)
        buckets = jnp.take(bucket_table, distance)
        scores = raw_scores + jnp.take(bias_table, buckets, axis=1)
        own_part = jnp.logical_or(segment_ids[None, :] == 0, segment_ids[None, :] == row_seg[:, None])
        visible = jnp.logical_and(key_index[None, :] <= row_index[:, None], own_part)
        scores = jnp.where(visible[None], scores, NEGATIVE)
        probs = low(jax.nn.softmax(scores, axis=-1))
        return jnp.einsum('hqk,khd->qhd', probs, value_heads, precision=lax.Precision.HIGHEST).reshape(block_rows, HEADS * HEAD_DIM)
    mixed_rows = lax.map(jax.checkpoint(query_block), jnp.arange(total_rows // block_rows, dtype=jnp.int32))
    return mixed_rows.reshape(total_rows, HEADS * HEAD_DIM)

def forward(block_input, w_qkv, w_attn_out, w_router, gain_attn, gain_moe, rel_bias, w_in, w_out, routes, segment_ids, bucket_table):
    positions = positions_of(segment_ids)
    slot_ids = slots_of(routes)
    attn_in = low(normalize(block_input, gain_attn))
    queries = low_back(low(jnp.dot(attn_in, w_qkv[0], precision=lax.Precision.HIGHEST)))
    keys_all = low_back(low(jnp.dot(attn_in, w_qkv[1], precision=lax.Precision.HIGHEST)))
    values_all = low_back(low(jnp.dot(attn_in, w_qkv[2], precision=lax.Precision.HIGHEST)))
    bias_table = rel_bias.reshape(HEADS, NBUCKET)
    mixed = attention(queries, keys_all, values_all, bias_table, segment_ids, positions, bucket_table)
    mixed = low_back(low(mixed))
    residual = block_input + low_back(jnp.dot(mixed, w_attn_out, precision=lax.Precision.HIGHEST))
    moe_in = low(normalize(residual, gain_moe))
    logits = low_back(jnp.dot(moe_in, w_router, precision=lax.Precision.HIGHEST))
    chosen = jnp.take_along_axis(logits, routes, axis=1)
    gate_probs = jax.nn.softmax(chosen, axis=1)
    rows_in = jnp.repeat(moe_in, 2, axis=0)
    expert_rows = jnp.zeros((EXPERTS * N_SEQ * N_WSH * CAP, D), jnp.float32).at[slot_ids].set(rows_in)
    expert_rows = low_back(expert_rows).reshape(EXPERTS, N_SEQ * N_WSH * CAP, D)
    pre_act = low_back(jnp.einsum('erd,edf->erf', expert_rows, w_in, precision=lax.Precision.HIGHEST))
    hidden = low(jax.nn.gelu(pre_act, approximate=True))
    expert_made = low_back(low(jnp.einsum('erf,efd->erd', hidden, w_out, precision=lax.Precision.HIGHEST)))
    route_rows = expert_made.reshape(-1, D)[slot_ids].reshape(-1, 2, D)
    return residual + lax.optimization_barrier(jnp.sum(gate_probs[:, :, None] * route_rows, axis=1))

def reference(block_input, w_qkv, w_attn_out, w_router, gain_attn, gain_moe, rel_bias, w_in, w_out, routes, segment_ids, bucket_table, out_grad):
    floats = tuple((item.astype(jnp.float32) for item in (block_input, w_qkv, w_attn_out, w_router, gain_attn, gain_moe, rel_bias, w_in, w_out)))

    def run_layer(*values_in):
        return forward(*values_in, routes, segment_ids, bucket_table)
    layer_out, pullback = jax.vjp(run_layer, *floats)
    grads = pullback(out_grad.astype(jnp.float32))
    return (layer_out.astype(jnp.bfloat16), grads[0], grads[1], grads[2], grads[3], grads[4], grads[5], grads[6], grads[7], grads[8])
```

```python
import functools
import math

import jax
import jax.numpy as jnp
from jax import lax
from jax.experimental import pallas as pl
from jax.experimental.pallas import tpu as pltpu
from jax.sharding import Mesh
from jax.sharding import PartitionSpec as P

HEADS = 12
HEAD_DIM = 64
NBUCKET = 32

EPSILON = 1e-06
NEGATIVE = -1e30
LOG2E = 1.4426950408889634
SCALE2 = 0.125 * LOG2E

PLANE = ("fx", "wsh")
ALL = ("pl", "fx", "wsh")
F32 = jnp.float32
BF16 = jnp.bfloat16
I32 = jnp.int32


def positions_of(segment_ids):
    total_rows = segment_ids.shape[0]
    numbers = jnp.arange(total_rows, dtype=jnp.int32)
    fresh_start = jnp.logical_or(numbers == 0, segment_ids != jnp.roll(segment_ids, 1))
    begins = lax.cummax(jnp.where(fresh_start, numbers, 0), axis=0)
    return jnp.where(segment_ids == 0, numbers, numbers - begins + total_rows // 2)


def norm_inverse(values):
    return lax.rsqrt(jnp.mean(values * values, axis=-1, keepdims=True) + EPSILON)


def norm_input_grad(values, inverse, gain_vec, grad_in):
    scaled = grad_in * gain_vec
    inner_mean = jnp.mean(scaled * values, axis=-1, keepdims=True)
    return inverse * scaled - values * inverse * inverse * inverse * inner_mean


BAND = 16


def bucket_kernel(nb, tile, scal, qpos, qseg, kpos, kseg, idx_ref):
    piece = pl.program_id(0)
    n2 = nb * nb
    at = 3 * n2 + nb
    step = 64
    q_first = scal[piece, at + NBUCKET]
    k_first = scal[piece, at + NBUCKET + 1]
    for jb in range(nb):
        for ib in range(nb):
            t = jb * nb + ib

            @pl.when(scal[piece, t] > 0)
            def _(jb=jb, ib=ib, t=t):
                low_bucket = scal[piece, n2 + t]
                high_bucket = scal[piece, 2 * n2 + t]
                cols = slice(ib * tile, (ib + 1) * tile)
                for r in range(tile // step):
                    rows = slice(jb * tile + r * step, jb * tile + (r + 1) * step)
                    distance = qpos[0:1, cols] - kpos[0, rows, :]

                    def more(b, count, distance=distance):
                        return count + (distance >= scal[piece, at + b]).astype(I32)

                    count = lax.fori_loop(
                        low_bucket + 1,
                        high_bucket + 1,
                        more,
                        jnp.full((step, tile), low_bucket, I32),
                    )
                    key_row = lax.broadcasted_iota(I32, (step, tile), 0) + (k_first + rows.start)
                    query_row = lax.broadcasted_iota(I32, (step, tile), 1) + (q_first + cols.start)
                    key_seg = kseg[0, rows, :]
                    own = jnp.logical_or(key_seg == 0, key_seg == qseg[0:1, cols])
                    seen = jnp.logical_and(key_row <= query_row, own)
                    idx_ref[0, rows, cols] = jnp.where(seen, count, NBUCKET)


def forward_kernel(first, nb, tile, *refs):
    if first:
        (scal, q_ref, kv_ref, tbl_ref, idx_ref) = refs[:5]
        (p_ref, m_ref, l_ref, o_ref, s_scr, kvt_scr) = refs[5:]
    else:
        (scal, q_ref, kv_ref, tbl_ref, idx_ref, m_in, l_in, o_in) = refs[:8]
        (p_ref, m_ref, l_ref, o_ref, s_scr, kvt_scr) = refs[8:]
    n2 = nb * nb
    kvt_scr[...] = kv_ref[...].T
    table = jnp.broadcast_to(tbl_ref[0, 0:1, :], (tile, 128))

    def scores_of(rows, cols, query):
        raw = jnp.dot(kv_ref[rows, :], query, preferred_element_type=F32)
        tops = []
        for c in range(tile // 128):
            lanes = slice(c * 128, (c + 1) * 128)
            ids = idx_ref[0, rows, cols.start + c * 128 : cols.start + (c + 1) * 128]
            score = raw[:, lanes] * SCALE2 + jnp.take_along_axis(table, ids, axis=1)
            s_scr[rows, lanes] = score
            tops.append(jnp.max(score, axis=0, keepdims=True))
        return jnp.concatenate(tops, axis=1)

    for ib in range(nb):
        cols = slice(ib * tile, (ib + 1) * tile)
        query = q_ref[:, cols]
        query = jnp.concatenate([query, jnp.zeros_like(query)], axis=0)
        if first:
            m_old = jnp.full((1, tile), -3e38, F32)
            l_old = jnp.zeros((1, tile), F32)
            o_old = jnp.zeros((HEAD_DIM, tile), F32)
        else:
            m_old = m_in[0, 0:1, cols]
            l_old = l_in[0, 0:1, cols]
            o_old = o_in[0, :, cols]
        blocks = ib + 1 if first else nb
        full = scal[3 * n2 + ib] > 0

        @pl.when(full)
        def _():
            m_new = m_old
            for jb in range(blocks):
                rows = slice(jb * tile, (jb + 1) * tile)
                m_new = jnp.maximum(m_new, scores_of(rows, cols, query))
            factor = jnp.exp2(m_old - m_new)
            total = l_old * factor
            for jb in range(blocks):
                rows = slice(jb * tile, (jb + 1) * tile)
                weight = jnp.exp2(s_scr[rows, :] - m_new)
                total = total + jnp.sum(weight, axis=0, keepdims=True)
                p_ref[0, rows, cols] = weight.astype(BF16)
            made = jnp.dot(
                kvt_scr[HEAD_DIM:, : blocks * tile],
                p_ref[0, : blocks * tile, cols],
                preferred_element_type=F32,
            )
            m_ref[0, 0:1, cols] = m_new
            l_ref[0, 0:1, cols] = total
            o_ref[0, :, cols] = o_old * factor + made

        @pl.when(jnp.logical_not(full))
        def _():
            m_ref[0, 0:1, cols] = m_old
            for jb in range(blocks):

                @pl.when(scal[jb * nb + ib] > 0)
                def _(jb=jb):
                    rows = slice(jb * tile, (jb + 1) * tile)
                    m_ref[0, 0:1, cols] = jnp.maximum(
                        m_ref[0, 0:1, cols], scores_of(rows, cols, query)
                    )

            m_new = m_ref[0, 0:1, cols]
            factor = jnp.exp2(m_old - m_new)
            l_ref[0, 0:1, cols] = l_old * factor
            o_ref[0, :, cols] = o_old * factor
            for jb in range(blocks):

                @pl.when(scal[jb * nb + ib] > 0)
                def _(jb=jb):
                    rows = slice(jb * tile, (jb + 1) * tile)
                    weight = jnp.exp2(s_scr[rows, :] - m_new)
                    l_ref[0, 0:1, cols] += jnp.sum(weight, axis=0, keepdims=True)
                    weight_low = weight.astype(BF16)
                    p_ref[0, rows, cols] = weight_low
                    o_ref[0, :, cols] += jnp.dot(
                        kvt_scr[HEAD_DIM:, rows], weight_low, preferred_element_type=F32
                    )


def backward_kernel(start, own, nb, tile, *refs):
    if start:
        (scal, q_ref, do_ref, kv_ref, p_ref, idx_ref, f_ref, delta_ref) = refs[:8]
        (dkv_ref, dq_ref, bias_ref, ds_scr, low_scr, acc_scr, kvt_scr, band_scr) = refs[8:]
    else:
        (scal, q_ref, do_ref, kv_ref, p_ref, idx_ref, f_ref, delta_ref, dq_in) = refs[:9]
        (dkv_ref, dq_ref, bias_ref, ds_scr, low_scr, acc_scr, kvt_scr, band_scr) = refs[9:]
    n2 = nb * nb
    kvt_scr[...] = kv_ref[...].T
    acc_scr[...] = jnp.zeros_like(acc_scr)
    dkv_ref[...] = jnp.zeros_like(dkv_ref)
    band_scr[...] = jnp.zeros_like(band_scr)
    pair = (((1,), (1,)), ((), ()))

    for ib in range(nb):
        cols = slice(ib * tile, (ib + 1) * tile)
        query = q_ref[:, cols]
        query = jnp.concatenate([query, jnp.zeros_like(query)], axis=0)
        out_grad = do_ref[:, cols]
        zeros = jnp.zeros_like(out_grad)
        grad_pad = jnp.concatenate([zeros, out_grad], axis=0)
        factor = f_ref[0, 0:1, cols]
        scaled = (out_grad.astype(F32) * factor).astype(BF16)
        scaled_pad = jnp.concatenate([zeros, scaled], axis=0)
        delta = delta_ref[0, 0:1, cols]
        dq_old = jnp.zeros((HEAD_DIM, tile), F32) if start else dq_in[0, :, cols]
        blocks = ib + 1 if own else nb
        full = scal[3 * n2 + ib] > 0

        def grads_of(rows):
            weight_grad = jnp.dot(kv_ref[rows, :], grad_pad, preferred_element_type=F32)
            score_grad = (p_ref[0, rows, cols].astype(F32) * factor) * (weight_grad - delta)
            ds_scr[rows, :] = score_grad
            low_scr[rows, :] = score_grad.astype(BF16)

        def products_of(rows):
            dkv_ref[rows, :] += lax.dot_general(
                p_ref[0, rows, cols], scaled_pad, pair, preferred_element_type=F32
            ) + lax.dot_general(low_scr[rows, :], query, pair, preferred_element_type=F32)
            return jnp.dot(kvt_scr[:HEAD_DIM, rows], low_scr[rows, :], preferred_element_type=F32)

        @pl.when(full)
        def _():
            for jb in range(blocks):
                grads_of(slice(jb * tile, (jb + 1) * tile))
            dq_ref[0, :, cols] = dq_old + products_of(slice(0, blocks * tile))

        @pl.when(jnp.logical_not(full))
        def _():
            dq_ref[0, :, cols] = dq_old
            for jb in range(blocks):

                @pl.when(scal[jb * nb + ib] > 0)
                def _(jb=jb):
                    rows = slice(jb * tile, (jb + 1) * tile)
                    grads_of(rows)
                    dq_ref[0, :, cols] += products_of(rows)

        for jb in range(blocks):
            t = jb * nb + ib

            @pl.when(scal[t] > 0)
            def _(jb=jb, t=t):
                least = scal[n2 + t]
                if own:
                    least = jnp.maximum(least, BAND)

                @pl.loop(least, scal[2 * n2 + t] + 1)
                def _(b):
                    total = jnp.zeros((8, tile), F32)
                    for r in range(jb * tile, (jb + 1) * tile, 64):
                        hit = idx_ref[0, r : r + 64, cols] == b
                        part = jnp.where(hit, ds_scr[r : r + 64, :], 0.0)
                        total = total + jnp.sum(part.reshape(8, 8, tile), axis=0)
                    acc_scr[b] += total

        if own:
            def band_of(key_at, keys, lane_at):
                here = slice(key_at, key_at + keys)
                lanes = slice(cols.start + lane_at, cols.start + lane_at + 128)
                band_scr[128 - keys :, :] += jnp.where(
                    idx_ref[0, here, lanes] < BAND, ds_scr[here, lane_at : lane_at + 128], 0.0
                )

            for lane_at in range(0, tile, 128):
                band_of(cols.start + lane_at, 128, lane_at)
                if lane_at > 0:
                    band_of(cols.start + lane_at - BAND, BAND, lane_at)
            if ib > 0:

                @pl.when(scal[(ib - 1) * nb + ib] > 0)
                def _():
                    band_of(cols.start - BAND, BAND, 0)

    if own:
        square = (128, 128)
        reverse = (
            lax.broadcasted_iota(I32, square, 0) + lax.broadcasted_iota(I32, square, 1) == 127
        ).astype(BF16)
        band = band_scr[...]
        upper = band.astype(BF16)
        lower = (band - upper.astype(F32)).astype(BF16)
        turned = jnp.dot(reverse, upper, preferred_element_type=F32) + jnp.dot(
            reverse, lower, preferred_element_type=F32
        )
        turned = pltpu.roll(turned, 0, 1, stride=1, stride_axis=0)
        bias_ref[0, NBUCKET:, :] = jnp.sum(turned.reshape(16, 8, 128), axis=0)
    else:
        bias_ref[0, NBUCKET:, :] = jnp.zeros((8, 128), F32)
    folded = jnp.sum(acc_scr[...], axis=1)
    bias = folded[:, :128]
    for c in range(1, tile // 128):
        bias = bias + folded[:, c * 128 : (c + 1) * 128]
    bias_ref[0, :NBUCKET, :] = bias


def buckets_of(scal, qpos, qseg, kpos, kseg, tile):
    planes, rows = kpos.shape[:2]
    nb = rows // tile
    return pl.pallas_call(
        functools.partial(bucket_kernel, nb, tile),
        grid=(planes,),
        in_specs=[
            pl.BlockSpec(memory_space=pltpu.SMEM),
            pl.BlockSpec((1, rows), lambda p: (0, 0)),
            pl.BlockSpec((1, rows), lambda p: (0, 0)),
            pl.BlockSpec((1, rows, 1), lambda p: (p, 0, 0)),
            pl.BlockSpec((1, rows, 1), lambda p: (p, 0, 0)),
        ],
        out_specs=pl.BlockSpec((1, rows, rows), lambda p: (p, 0, 0)),
        out_shape=jax.ShapeDtypeStruct((planes, rows, rows), I32),
        compiler_params=pltpu.CompilerParams(
            dimension_semantics=("arbitrary",), vmem_limit_bytes=40 << 20
        ),
        cost_estimate=pl.CostEstimate(
            flops=planes * rows * rows * 16,
            bytes_accessed=planes * rows * rows * 4,
            transcendentals=0,
        ),
    )(scal, qpos, qseg, kpos, kseg)


def forward_piece(k, scal, q_t, kv, table, idx, state, tile):
    heads = table.shape[0]
    rows = kv.shape[0]
    nb = rows // tile
    by_head = lambda *shape: pl.BlockSpec((1,) + shape, lambda h: (h, 0, 0))
    in_specs = [
        pl.BlockSpec(memory_space=pltpu.SMEM),
        pl.BlockSpec((HEAD_DIM, rows), lambda h: (h, 0)),
        pl.BlockSpec((rows, 2 * HEAD_DIM), lambda h: (0, h)),
        by_head(8, 128),
        pl.BlockSpec((1, rows, rows), lambda h: (k, 0, 0)),
    ]
    args = [scal, q_t, kv, table, idx]
    if k > 0:
        in_specs += [by_head(1, rows), by_head(1, rows), by_head(HEAD_DIM, rows)]
        args += list(state)
    pairs = heads * rows * rows
    return pl.pallas_call(
        functools.partial(forward_kernel, k == 0, nb, tile),
        grid=(heads,),
        in_specs=in_specs,
        out_specs=[
            by_head(rows, rows),
            by_head(1, rows),
            by_head(1, rows),
            by_head(HEAD_DIM, rows),
        ],
        out_shape=[
            jax.ShapeDtypeStruct((heads, rows, rows), BF16),
            jax.ShapeDtypeStruct((heads, 1, rows), F32),
            jax.ShapeDtypeStruct((heads, 1, rows), F32),
            jax.ShapeDtypeStruct((heads, HEAD_DIM, rows), F32),
        ],
        scratch_shapes=[
            pltpu.VMEM((rows, tile), F32),
            pltpu.VMEM((2 * HEAD_DIM, rows), BF16),
        ],
        compiler_params=pltpu.CompilerParams(
            dimension_semantics=("arbitrary",), vmem_limit_bytes=40 << 20
        ),
        cost_estimate=pl.CostEstimate(
            flops=pairs * 4 * 128, bytes_accessed=pairs * 4, transcendentals=pairs
        ),
    )(*args)


def backward_piece(k, scal, q_t, do_t, kv, probs, idx, factor, delta, dq, tile):
    heads = probs.shape[0]
    rows = kv.shape[0]
    nb = rows // tile
    start = dq is None
    by_head = lambda *shape: pl.BlockSpec((1,) + shape, lambda h: (h, 0, 0))
    in_specs = [
        pl.BlockSpec(memory_space=pltpu.SMEM),
        pl.BlockSpec((HEAD_DIM, rows), lambda h: (h, 0)),
        pl.BlockSpec((HEAD_DIM, rows), lambda h: (h, 0)),
        pl.BlockSpec((rows, 2 * HEAD_DIM), lambda h: (0, h)),
        by_head(rows, rows),
        pl.BlockSpec((1, rows, rows), lambda h: (k, 0, 0)),
        by_head(1, rows),
        by_head(1, rows),
    ]
    args = [scal, q_t, do_t, kv, probs, idx, factor, delta]
    if not start:
        in_specs += [by_head(HEAD_DIM, rows)]
        args += [dq]
    pairs = heads * rows * rows
    return pl.pallas_call(
        functools.partial(backward_kernel, start, k == 0, nb, tile),
        grid=(heads,),
        in_specs=in_specs,
        out_specs=[
            pl.BlockSpec((rows, 2 * HEAD_DIM), lambda h: (0, h)),
            by_head(HEAD_DIM, rows),
            by_head(NBUCKET + 8, 128),
        ],
        out_shape=[
            jax.ShapeDtypeStruct((rows, heads * 2 * HEAD_DIM), F32),
            jax.ShapeDtypeStruct((heads, HEAD_DIM, rows), F32),
            jax.ShapeDtypeStruct((heads, NBUCKET + 8, 128), F32),
        ],
        scratch_shapes=[
            pltpu.VMEM((rows, tile), F32),
            pltpu.VMEM((rows, tile), BF16),
            pltpu.VMEM((NBUCKET, 8, tile), F32),
            pltpu.VMEM((2 * HEAD_DIM, rows), BF16),
            pltpu.VMEM((128, 128), F32),
        ],
        compiler_params=pltpu.CompilerParams(
            dimension_semantics=("arbitrary",), vmem_limit_bytes=40 << 20
        ),
        cost_estimate=pl.CostEstimate(
            flops=pairs * 8 * 128, bytes_accessed=pairs * 4, transcendentals=0
        ),
    )(*args)


def shards(
    block_input,
    w_qkv,
    w_attn_out,
    w_router,
    gain_attn,
    gain_moe,
    rel_bias,
    w_in,
    w_out,
    routes,
    segment_ids,
    bucket_table,
    out_grad,
):
    tok_rows, width = block_input.shape
    planes = lax.axis_size("pl")
    group = lax.axis_size("fx") * lax.axis_size("wsh")
    devices = planes * group
    cores = lax.axis_size("grp")
    plane_rank = lax.axis_index("pl")
    place = lax.axis_index(PLANE)
    device_rank = plane_rank * group + place
    core_rank = lax.axis_index("grp")
    heads = HEADS // group
    head_cols = heads * HEAD_DIM
    rows = tok_rows * group
    w_rows = w_qkv.shape[1]
    expert_count = w_router.shape[1]
    bias_share = rel_bias.shape[0]

    split = cores if w_rows % cores == 0 else 1
    part_rows = w_rows // split

    def own_part(array, axis):
        if split == 1:
            return array
        return lax.dynamic_slice_in_dim(array, core_rank * part_rows, part_rows, axis)

    def join_parts(array):
        if split > 1:
            both = lax.all_gather(array, "grp", axis=0, tiled=False)
            array = jnp.transpose(both, (1, 0, 2, 3))
        return array.reshape(devices * w_rows, array.shape[-1])

    def to_all(array, axes, count):
        return lax.all_to_all(
            jnp.broadcast_to(array[None], (count,) + array.shape),
            axes,
            split_axis=0,
            concat_axis=0,
            tiled=True,
        )

    capacity = max(2, 4 * tok_rows // expert_count)
    expert_ids = jnp.arange(expert_count, dtype=I32)
    route_hits = routes[:, :, None] == expert_ids[None, None, :]
    flat_hits = route_hits.reshape(tok_rows * 2, expert_count)
    order = jnp.arange(tok_rows * 2, dtype=I32)
    earlier = (order[:, None] > order[None, :]).astype(BF16)
    ranks = jnp.dot(earlier, flat_hits.astype(BF16), preferred_element_type=F32)
    slot_ranks = jnp.sum(jnp.where(flat_hits, ranks, 0.0), axis=1).astype(I32)
    slot_ids = routes * capacity + slot_ranks.reshape(tok_rows, 2)
    slot_count = expert_count * capacity
    slot_numbers = jnp.arange(slot_count, dtype=I32)
    hit_first = slot_numbers[:, None] == slot_ids[None, :, 0]
    hit_second = slot_numbers[:, None] == slot_ids[None, :, 1]
    table_first = hit_first.astype(BF16)
    table_second = hit_second.astype(BF16)
    slot_table = table_first + table_second
    other_expert = jnp.sum(
        jnp.where(hit_first, routes[None, :, 1], 0) + jnp.where(hit_second, routes[None, :, 0], 0),
        axis=1,
    )

    plane_input = to_all(block_input, PLANE, group).reshape(rows, width)

    qkv_part = own_part(w_qkv, 1)
    q_part = qkv_part[0].reshape(part_rows, group, head_cols)
    kv_part = qkv_part[1:].reshape(2, part_rows, group, heads, HEAD_DIM)
    kv_part = jnp.transpose(kv_part, (1, 2, 3, 0, 4)).reshape(part_rows, group, 2 * head_cols)
    qkv_pay = jnp.transpose(jnp.concatenate([q_part, kv_part], axis=2), (1, 0, 2))
    small = jnp.concatenate([w_router.reshape(-1), gain_attn, gain_moe, rel_bias])
    pay_cols = 3 * head_cols
    small_count = small.shape[0]
    small_rows = -(-(small_count + capacity) // pay_cols)
    small = jnp.concatenate(
        [
            jnp.broadcast_to(small[None], (devices, small_count)),
            other_expert.astype(BF16).reshape(devices, capacity),
        ],
        axis=1,
    )
    small = jnp.pad(small, ((0, 0), (0, small_rows * pay_cols - small_count - capacity)))
    qkv_pay = jnp.broadcast_to(qkv_pay[None], (planes,) + qkv_pay.shape)
    qkv_pay = jnp.concatenate(
        [
            qkv_pay.reshape(devices, part_rows, pay_cols),
            small.reshape(devices, small_rows, pay_cols),
        ],
        axis=1,
    )
    qkv_got = lax.all_to_all(qkv_pay, ALL, split_axis=0, concat_axis=0, tiled=True)
    w_heads = join_parts(qkv_got[:, :part_rows])
    small_got = qkv_got[:, part_rows:].reshape(devices, small_rows * pay_cols)
    router_size = w_rows * expert_count
    full_router = small_got[:, :router_size].reshape(width, expert_count)
    at = router_size
    gain_attn_full = small_got[:, at : at + w_rows].reshape(width).astype(F32)
    at += w_rows
    gain_moe_full = small_got[:, at : at + w_rows].reshape(width).astype(F32)
    at += w_rows
    bias_full = small_got[:, at : at + bias_share].reshape(HEADS, NBUCKET).astype(F32)
    at += bias_share
    other_arrived = small_got[:, at : at + capacity].reshape(slot_count).astype(F32)
    w_query = w_heads[:, :head_cols]
    w_keyval = w_heads[:, head_cols:]

    positions = positions_of(segment_ids)
    bucket_ids = jnp.arange(NBUCKET, dtype=I32)
    edges = jnp.sum((bucket_table[None, :] < bucket_ids[:, None]).astype(I32), axis=1)
    tile = 256 if rows % 256 == 0 else rows
    nb = rows // tile

    def ranges_of(plane):
        first = jnp.maximum(plane, 0) * rows
        pos = lax.dynamic_slice_in_dim(positions, first, rows)
        seg = lax.dynamic_slice_in_dim(segment_ids, first, rows)
        pos_t, seg_t = pos.reshape(nb, tile), seg.reshape(nb, tile)
        limits = (
            jnp.min(pos_t, axis=1),
            jnp.max(pos_t, axis=1),
            jnp.min(seg_t, axis=1),
            jnp.max(seg_t, axis=1),
        )
        return first, pos, seg, limits

    q_first, q_pos, q_seg, (q_pos_min, q_pos_max, q_seg_min, q_seg_max) = ranges_of(plane_rank)
    tile_ids = jnp.arange(nb, dtype=I32)

    def bucket_of(distance):
        return jnp.sum((distance[:, :, None] >= edges[None, None, 1:]).astype(I32), axis=2)

    scal_of, key_info = [], []
    for k in range(planes):
        plane = plane_rank - k
        k_first, k_pos, k_seg, (k_pos_min, k_pos_max, k_seg_min, k_seg_max) = ranges_of(plane)
        causal = (k_first + tile_ids * tile)[:, None] <= (q_first + tile_ids * tile + tile - 1)[
            None, :
        ]
        own = jnp.logical_or(
            (k_seg_min == 0)[:, None],
            jnp.logical_and(
                k_seg_min[:, None] <= q_seg_max[None, :], k_seg_max[:, None] >= q_seg_min[None, :]
            ),
        )
        flags = jnp.logical_and(jnp.logical_and(causal, own), plane >= 0).astype(I32)
        least = bucket_of(jnp.maximum(q_pos_min[None, :] - k_pos_max[:, None], 0))
        most = bucket_of(jnp.maximum(q_pos_max[None, :] - k_pos_min[:, None], 0))
        beyond = jnp.logical_and(k == 0, tile_ids[:, None] > tile_ids[None, :])
        full = jnp.min(jnp.where(beyond, 1, flags), axis=0)
        scal_of.append(
            jnp.concatenate(
                [
                    flags.reshape(-1),
                    least.reshape(-1),
                    most.reshape(-1),
                    full,
                    edges,
                    jnp.stack([q_first, k_first]).astype(I32),
                ]
            )
        )
        key_info.append((k_pos[:, None], k_seg[:, None]))
    bucket_idx = buckets_of(
        jnp.stack(scal_of),
        q_pos[None, :],
        q_seg[None, :],
        jnp.stack([info[0] for info in key_info]),
        jnp.stack([info[1] for info in key_info]),
        tile,
    )

    plane_wide = plane_input.astype(F32)
    plane_inverse = norm_inverse(plane_wide)
    attn_in = (plane_wide * plane_inverse * gain_attn_full).astype(BF16)
    q_t = lax.dot_general(
        w_query, attn_in, (((0,), (1,)), ((), ())), preferred_element_type=F32
    ).astype(BF16)
    keyval = jnp.dot(attn_in, w_keyval, preferred_element_type=F32).astype(BF16)
    bias_local = lax.dynamic_slice_in_dim(bias_full, place * heads, heads, 0) * LOG2E
    bias_table = jnp.concatenate(
        [bias_local, jnp.full((heads, 128 - NBUCKET), NEGATIVE, F32)], axis=1
    )
    bias_table = jnp.broadcast_to(bias_table[:, None, :], (heads, 8, 128))

    upward = [(i, i + 1) for i in range(planes - 1)]
    downward = [(i + 1, i) for i in range(planes - 1)]
    kv_pieces = [keyval]
    for k in range(1, planes):
        kv_pieces.append(lax.ppermute(kv_pieces[-1], "pl", upward))

    grad_send = jnp.dot(slot_table, out_grad, preferred_element_type=F32).astype(BF16)
    out_part = own_part(w_attn_out, 0)
    if planes > 1:
        grad_send, out_part, kv_pieces[1] = lax.optimization_barrier(
            (grad_send, out_part, kv_pieces[1])
        )
    out_got = to_all(out_part, ALL, devices)
    half_width = width // 2
    full_out = jnp.concatenate(
        [join_parts(out_got[:, :, :half_width]), join_parts(out_got[:, :, half_width:])], axis=1
    )
    grad_raw = lax.all_to_all(
        grad_send.reshape(expert_count, capacity, width), ALL, split_axis=0, concat_axis=0, tiled=True
    ).reshape(slot_count, width)
    probs, tops, state = [], [], None
    for k in range(planes):
        made = forward_piece(k, scal_of[k], q_t, kv_pieces[k], bias_table, bucket_idx, state, tile)
        probs.append(made[0])
        state = made[1:]
        tops.append(made[1])
    final_top, final_sum, out_sum = state
    head_out_t = out_sum / final_sum
    mixed_own = head_out_t.astype(BF16).reshape(head_cols, group, tok_rows)
    mixed_t = lax.all_to_all(
        jnp.transpose(mixed_own, (1, 0, 2)), PLANE, split_axis=0, concat_axis=0, tiled=True
    ).reshape(width, tok_rows)

    input_wide = block_input.astype(F32)
    residual = input_wide + lax.dot_general(
        mixed_t, full_out, (((0,), (0,)), ((), ())), preferred_element_type=F32
    )
    inverse_moe = norm_inverse(residual)
    moe_in = (residual * inverse_moe * gain_moe_full).astype(BF16)
    outgoing = jnp.dot(slot_table, moe_in, preferred_element_type=F32).astype(BF16)
    arrived = lax.all_to_all(
        outgoing.reshape(expert_count, capacity, width), ALL, split_axis=0, concat_axis=0, tiled=True
    ).reshape(slot_count, width)
    logits = jnp.dot(moe_in, full_router, preferred_element_type=F32)
    chosen = jnp.sum(jnp.where(route_hits, logits[:, None, :], 0.0), axis=2)
    gate_probs = jax.nn.softmax(chosen, axis=1)

    expert_in = w_in[0]
    expert_out = w_out[0]
    row_logits = jnp.dot(arrived, full_router, preferred_element_type=F32)
    own_logit = jnp.sum(jnp.where(expert_ids[None, :] == device_rank, row_logits, 0.0), axis=1)
    other_logit = jnp.sum(
        jnp.where(expert_ids[None, :].astype(F32) == other_arrived[:, None], row_logits, 0.0), axis=1
    )
    top_logit = jnp.maximum(own_logit, other_logit)
    own_part_exp = jnp.exp(own_logit - top_logit)
    row_gate = own_part_exp / (own_part_exp + jnp.exp(other_logit - top_logit))
    grad_wide = grad_raw.astype(F32)
    made_grad = (row_gate[:, None] * grad_wide).astype(BF16)

    pre_act = jnp.dot(arrived, expert_in, preferred_element_type=F32)
    hidden_wide, gelu_back = jax.vjp(
        lambda inner_vals: jax.nn.gelu(inner_vals, approximate=True), pre_act
    )
    hidden = hidden_wide.astype(BF16)
    hidden_raw = lax.dot_general(
        grad_raw, expert_out, (((1,), (1,)), ((), ())), preferred_element_type=F32
    )
    slot_gate_grad = jnp.sum(hidden_raw * hidden.astype(F32), axis=1)
    pre_grad = gelu_back(hidden_raw * row_gate[:, None])[0].astype(BF16)
    slope = row_gate * (1.0 - row_gate) * slot_gate_grad
    signs = (expert_ids[None, :] == device_rank).astype(F32) - (
        expert_ids[None, :].astype(F32) == other_arrived[:, None]
    ).astype(F32)
    row_logit_grad = slope[:, None] * signs
    logit_high = row_logit_grad.astype(BF16)
    logit_low = (row_logit_grad - logit_high.astype(F32)).astype(BF16)
    row_logit_grad = jnp.concatenate([logit_high, logit_low], axis=1)
    row_grad = lax.dot_general(
        pre_grad, expert_in, (((1,), (1,)), ((), ())), preferred_element_type=F32
    )
    row_grad = (
        row_grad
        + lax.dot_general(
            row_logit_grad,
            jnp.concatenate([full_router, full_router], axis=1),
            (((1,), (1,)), ((), ())),
            preferred_element_type=F32,
        )
    ).astype(BF16)
    returned_grads = lax.all_to_all(
        row_grad.reshape(expert_count, capacity, width),
        ALL,
        split_axis=0,
        concat_axis=0,
        tiled=True,
    ).reshape(slot_count, width)
    hidden_late, made_late, row_grad = lax.optimization_barrier((hidden, made_grad, row_grad))
    expert_made = jnp.dot(hidden_late, expert_out, preferred_element_type=F32).astype(BF16)
    w_out_grad = lax.dot_general(
        hidden_late, made_late, (((0,), (0,)), ((), ())), preferred_element_type=F32
    )[None]
    router_pair = lax.dot_general(
        arrived, row_logit_grad, (((0,), (0,)), ((), ())), preferred_element_type=F32
    )
    router_grad = router_pair[:, :expert_count] + router_pair[:, expert_count:]
    returned_grads, expert_made, w_out_grad = lax.optimization_barrier(
        (returned_grads, expert_made, w_out_grad)
    )

    moe_in_grad = lax.dot_general(
        slot_table, returned_grads, (((0,), (0,)), ((), ())), preferred_element_type=F32
    )
    grad_out = out_grad.astype(F32)
    residual_grad = grad_out + norm_input_grad(residual, inverse_moe, gain_moe_full, moe_in_grad)
    branch_grad = residual_grad.astype(BF16)
    mixed_grad_t = lax.dot_general(
        full_out, branch_grad, (((1,), (1,)), ((), ())), preferred_element_type=F32
    ).astype(BF16)
    grad_t = lax.all_to_all(
        mixed_grad_t.reshape(group, head_cols, tok_rows),
        PLANE,
        split_axis=0,
        concat_axis=0,
        tiled=True,
    )
    grad_t = jnp.transpose(grad_t, (1, 0, 2)).reshape(head_cols, rows)

    delta = jnp.sum(
        grad_t.astype(F32).reshape(heads, HEAD_DIM, rows) * head_out_t, axis=1, keepdims=True
    )
    query_grad, carried, bias_parts = None, None, []
    for k in reversed(range(planes)):
        factor = jnp.exp2(tops[k] - final_top) / final_sum
        dkv, query_grad, bias_part = backward_piece(
            k,
            scal_of[k],
            q_t,
            grad_t,
            kv_pieces[k],
            probs[k],
            bucket_idx,
            factor,
            delta,
            query_grad,
            tile,
        )
        bias_parts.append(bias_part)
        total = dkv if carried is None else dkv + carried.astype(F32)
        if k > 0:
            carried = lax.ppermute(total.astype(BF16), "pl", downward)
        if k == planes - 1:
            made_send, branch_late, query_grad = lax.optimization_barrier(
                (expert_made, branch_grad, query_grad)
            )
            returned = lax.all_to_all(
                made_send.reshape(expert_count, capacity, width),
                ALL,
                split_axis=0,
                concat_axis=0,
                tiled=True,
            ).reshape(slot_count, width)
            attn_out_part = lax.dot_general(
                mixed_t, branch_late, (((1,), (0,)), ((), ())), preferred_element_type=F32
            )
            attn_out_part = jnp.transpose(
                attn_out_part.reshape(planes, group, w_rows, width), (1, 0, 2, 3)
            ).astype(BF16)
            attn_out_part = lax.all_to_all(
                attn_out_part, PLANE, split_axis=0, concat_axis=0, tiled=True
            )
            attn_out_part = jnp.sum(attn_out_part.astype(F32), axis=0).astype(BF16)
            attn_out_part = lax.all_to_all(
                attn_out_part, "pl", split_axis=0, concat_axis=0, tiled=True
            )
            attn_out_grad = jnp.sum(attn_out_part.astype(F32), axis=0)
            gain_moe_grad = jnp.sum(moe_in_grad * residual * inverse_moe, axis=0)
    scale_row = jnp.tile(
        jnp.concatenate([jnp.full((HEAD_DIM,), 0.125, F32), jnp.ones((HEAD_DIM,), F32)]), heads
    )
    keyval_grad = (total * scale_row[None, :]).astype(BF16)
    query_grad_t = (query_grad.reshape(head_cols, rows) * 0.125).astype(BF16)
    bias_rows = sum(bias_parts)
    band_rows = jnp.roll(jnp.sum(bias_rows[:, NBUCKET:], axis=1), 1, axis=1)[:, :BAND]
    bias_grad = jnp.sum(bias_rows[:, :NBUCKET], axis=2) + jnp.pad(
        band_rows, ((0, 0), (0, NBUCKET - BAND))
    )

    attn_in_grad = lax.dot_general(
        query_grad_t, w_query, (((0,), (1,)), ((), ())), preferred_element_type=F32
    ) + lax.dot_general(
        keyval_grad, w_keyval, (((1,), (1,)), ((), ())), preferred_element_type=F32
    )
    gain_attn_grad = jnp.sum(attn_in_grad * plane_wide * plane_inverse, axis=0)
    attn_in_grad = lax.all_to_all(
        attn_in_grad.astype(BF16).reshape(group, tok_rows, width),
        PLANE,
        split_axis=0,
        concat_axis=0,
        tiled=True,
    )
    attn_in_grad = jnp.sum(attn_in_grad.astype(F32), axis=0)
    inverse_attn = norm_inverse(input_wide)
    input_grad = residual_grad + norm_input_grad(
        input_wide, inverse_attn, gain_attn_full, attn_in_grad
    )

    w_query_grad = lax.dot_general(
        attn_in, query_grad_t, (((0,), (1,)), ((), ())), preferred_element_type=F32
    ).astype(BF16)
    w_keyval_grad = lax.dot_general(
        attn_in, keyval_grad, (((0,), (0,)), ((), ())), preferred_element_type=F32
    ).astype(BF16)
    bias_all = lax.dynamic_update_slice_in_dim(
        jnp.zeros((HEADS, NBUCKET), F32), bias_grad, place * heads, 0
    )
    small_grads = jnp.concatenate(
        [
            router_grad.reshape(devices, router_size),
            gain_attn_grad.reshape(devices, w_rows),
            gain_moe_grad.reshape(devices, w_rows),
            bias_all.reshape(devices, bias_share),
        ],
        axis=1,
    )
    small_high = small_grads.astype(BF16)
    small_low = (small_grads - small_high.astype(F32)).astype(BF16)
    pair_rows = -(-2 * small_count // pay_cols)
    small_pair = jnp.pad(
        jnp.concatenate([small_high, small_low], axis=1),
        ((0, 0), (0, pair_rows * pay_cols - 2 * small_count)),
    ).reshape(devices, pair_rows, pay_cols)
    w_parts = jnp.concatenate([w_query_grad, w_keyval_grad], axis=1).reshape(
        devices, w_rows, pay_cols
    )
    w_parts = jnp.concatenate([w_parts, small_pair], axis=1)
    w_got = lax.all_to_all(w_parts, ALL, split_axis=0, concat_axis=0, tiled=True)

    returned, pre_late, w_parts = lax.optimization_barrier((returned, pre_grad, w_parts))
    w_in_grad = lax.dot_general(
        arrived, pre_late, (((0,), (0,)), ((), ())), preferred_element_type=F32
    )[None]
    picked_first = lax.dot_general(
        table_first, returned, (((0,), (0,)), ((), ())), preferred_element_type=F32
    )
    picked_second = lax.dot_general(
        table_second, returned, (((0,), (0,)), ((), ())), preferred_element_type=F32
    )
    block_output = (
        residual + (gate_probs[:, 0:1] * picked_first + gate_probs[:, 1:2] * picked_second)
    ).astype(BF16)
    w_got, w_in_grad, block_output = lax.optimization_barrier((w_got, w_in_grad, block_output))

    w_wide = w_got.astype(F32)
    w_sum = jnp.sum(w_wide[:, :w_rows].reshape(planes, group, w_rows, pay_cols), axis=0)
    q_sum = jnp.transpose(w_sum[:, :, :head_cols], (1, 0, 2)).reshape(1, w_rows, width)
    kv_sum = w_sum[:, :, head_cols:].reshape(group, w_rows, heads, 2, HEAD_DIM)
    kv_sum = jnp.transpose(kv_sum, (3, 1, 0, 2, 4)).reshape(2, w_rows, width)
    qkv_grad = jnp.concatenate([q_sum, kv_sum], axis=0)
    small_sum = jnp.sum(w_wide[:, w_rows:].reshape(devices, -1), axis=0)
    small_sum = small_sum[:small_count] + small_sum[small_count : 2 * small_count]
    at = router_size
    return (
        block_output,
        input_grad,
        qkv_grad,
        attn_out_grad,
        small_sum[:at].reshape(w_rows, expert_count),
        small_sum[at : at + w_rows],
        small_sum[at + w_rows : at + 2 * w_rows],
        small_sum[at + 2 * w_rows : small_count],
        w_in_grad,
        w_out_grad,
    )


def solution(mesh):
    devices = mesh.devices
    grp, seq, wsh = devices.shape
    inner = Mesh(devices.reshape(grp, seq // 2, 2, wsh), ("grp",) + ALL)
    every = ("grp",) + ALL
    in_specs = (
        P(every, None),
        P(None, ALL, None),
        P(ALL, None),
        P(ALL, None),
        P(ALL),
        P(ALL),
        P(ALL),
        P(ALL, None, None),
        P(ALL, None, None),
        P(every, None),
        P("grp"),
        P(),
        P(every, None),
    )
    out_specs = (
        P(every, None),
        P(every, None),
        P("grp", ALL, None),
        P(every, None),
        P(every, None),
        P(every),
        P(every),
        P(every),
        P(every, None, None),
        P(every, None, None),
    )
    return jax.shard_map(
        shards, mesh=inner, in_specs=in_specs, out_specs=out_specs, check_vma=False
    )
```

```python
import functools
import math

import jax
import jax.numpy as jnp
from jax import lax
from jax.experimental import pallas as pl
from jax.experimental.pallas import tpu as pltpu
from jax.sharding import Mesh
from jax.sharding import PartitionSpec as P

HEADS = 12
HEAD_DIM = 64
NBUCKET = 32

EPSILON = 1e-06
NEGATIVE = -1e30
LOG2E = 1.4426950408889634
SCALE2 = 0.125 * LOG2E

PLANE = ("fx", "wsh")
ALL = ("pl", "fx", "wsh")
F32 = jnp.float32
BF16 = jnp.bfloat16
I32 = jnp.int32


def positions_of(segment_ids):
    total_rows = segment_ids.shape[0]
    numbers = jnp.arange(total_rows, dtype=jnp.int32)
    fresh_start = jnp.logical_or(numbers == 0, segment_ids != jnp.roll(segment_ids, 1))
    begins = lax.cummax(jnp.where(fresh_start, numbers, 0), axis=0)
    return jnp.where(segment_ids == 0, numbers, numbers - begins + total_rows // 2)


def norm_inverse(values):
    return lax.rsqrt(jnp.mean(values * values, axis=-1, keepdims=True) + EPSILON)


def norm_input_grad(values, inverse, gain_vec, grad_in):
    scaled = grad_in * gain_vec
    inner_mean = jnp.mean(scaled * values, axis=-1, keepdims=True)
    return inverse * scaled - values * inverse * inverse * inverse * inner_mean


BAND = 16
EDGE_GROUP = 4
EDGES = NBUCKET + EDGE_GROUP
VMEM_LIMIT = 60 << 20


def bucket_kernel(nb, tile, scal, qpos, qseg, kpos, kseg, idx_ref):
    piece = pl.program_id(0)
    n2 = nb * nb
    at = 3 * n2 + nb
    step = 128 if tile % 128 == 0 else tile
    q_first = scal[piece, at + EDGES]
    k_first = scal[piece, at + EDGES + 1]
    for jb in range(nb):
        for ib in range(nb):
            t = jb * nb + ib

            @pl.when(scal[piece, t] > 0)
            def _(jb=jb, ib=ib, t=t):
                low_bucket = scal[piece, n2 + t]
                high_bucket = scal[piece, 2 * n2 + t]
                cols = slice(ib * tile, (ib + 1) * tile)
                for r in range(tile // step):
                    rows = slice(jb * tile + r * step, jb * tile + (r + 1) * step)
                    distance = qpos[0:1, cols] - kpos[0, rows, :]

                    def more(trip, count, distance=distance):
                        start = low_bucket + 1 + trip * EDGE_GROUP
                        for b in range(EDGE_GROUP):
                            count = count + jnp.where(distance >= scal[piece, at + start + b], 1, 0)
                        return count

                    count = more(0, jnp.full((step, tile), low_bucket, I32))
                    trips = lax.div(high_bucket - low_bucket + EDGE_GROUP - 1, EDGE_GROUP)
                    count = lax.fori_loop(1, trips, more, count)
                    key_row = lax.broadcasted_iota(I32, (step, tile), 0) + (k_first + rows.start)
                    query_row = lax.broadcasted_iota(I32, (step, tile), 1) + (q_first + cols.start)
                    key_seg = kseg[0, rows, :]
                    own = jnp.logical_or(key_seg == 0, key_seg == qseg[0:1, cols])
                    seen = jnp.logical_and(key_row <= query_row, own)
                    idx_ref[0, rows, cols] = jnp.where(seen, count, NBUCKET)


def forward_kernel(first, last, nb, tile, *refs):
    if first:
        (scal, q_ref, kv_ref, tbl_ref, idx_ref) = refs[:5]
        refs = refs[5:]
    else:
        (scal, q_ref, kv_ref, tbl_ref, idx_ref, m_in, l_in, o_in) = refs[:8]
        refs = refs[8:]
    if last:
        (p_ref, m_ref, l_ref, o_ref, mixed_ref, s_scr, kvt_scr, mixed_scr) = refs
    else:
        (p_ref, m_ref, l_ref, o_ref, s_scr, kvt_scr) = refs
    n2 = nb * nb
    kvt_scr[...] = kv_ref[...].T
    table = jnp.broadcast_to(tbl_ref[0, 0:1, :], (tile, 128))

    def scores_of(rows, cols, query):
        raw = jnp.dot(kv_ref[rows, :], query, preferred_element_type=F32)
        tops = []
        for c in range(tile // 128):
            lanes = slice(c * 128, (c + 1) * 128)
            ids = idx_ref[0, rows, cols.start + c * 128 : cols.start + (c + 1) * 128]
            score = raw[:, lanes] * SCALE2 + jnp.take_along_axis(table, ids, axis=1)
            s_scr[rows, lanes] = score
            tops.append(jnp.max(score, axis=0, keepdims=True))
        return jnp.concatenate(tops, axis=1)

    for ib in range(nb):
        cols = slice(ib * tile, (ib + 1) * tile)
        query = q_ref[:, cols]
        query = jnp.concatenate([query, jnp.zeros_like(query)], axis=0)
        if first:
            m_old = jnp.full((1, tile), -3e38, F32)
            l_old = jnp.zeros((1, tile), F32)
            o_old = jnp.zeros((HEAD_DIM, tile), F32)
        else:
            m_old = m_in[0, 0:1, cols]
            l_old = l_in[0, 0:1, cols]
            o_old = o_in[0, :, cols]
        blocks = ib + 1 if first else nb
        full = scal[3 * n2 + ib] > 0

        @pl.when(full)
        def _():
            m_new = m_old
            for jb in range(blocks):
                rows = slice(jb * tile, (jb + 1) * tile)
                m_new = jnp.maximum(m_new, scores_of(rows, cols, query))
            factor = jnp.exp2(m_old - m_new)
            total = l_old * factor
            for jb in range(blocks):
                rows = slice(jb * tile, (jb + 1) * tile)
                weight = jnp.exp2(s_scr[rows, :] - m_new)
                total = total + jnp.sum(weight, axis=0, keepdims=True)
                p_ref[0, rows, cols] = weight.astype(BF16)
            made = jnp.dot(
                kvt_scr[HEAD_DIM:, : blocks * tile],
                p_ref[0, : blocks * tile, cols],
                preferred_element_type=F32,
            )
            m_ref[0, 0:1, cols] = m_new
            l_ref[0, 0:1, cols] = total
            o_ref[0, :, cols] = o_old * factor + made

        @pl.when(jnp.logical_not(full))
        def _():
            m_ref[0, 0:1, cols] = m_old
            for jb in range(blocks):

                @pl.when(scal[jb * nb + ib] > 0)
                def _(jb=jb):
                    rows = slice(jb * tile, (jb + 1) * tile)
                    m_ref[0, 0:1, cols] = jnp.maximum(
                        m_ref[0, 0:1, cols], scores_of(rows, cols, query)
                    )

            m_new = m_ref[0, 0:1, cols]
            factor = jnp.exp2(m_old - m_new)
            l_ref[0, 0:1, cols] = l_old * factor
            o_ref[0, :, cols] = o_old * factor
            for jb in range(blocks):

                @pl.when(scal[jb * nb + ib] > 0)
                def _(jb=jb):
                    rows = slice(jb * tile, (jb + 1) * tile)
                    weight = jnp.exp2(s_scr[rows, :] - m_new)
                    l_ref[0, 0:1, cols] += jnp.sum(weight, axis=0, keepdims=True)
                    weight_low = weight.astype(BF16)
                    p_ref[0, rows, cols] = weight_low
                    o_ref[0, :, cols] += jnp.dot(
                        kvt_scr[HEAD_DIM:, rows], weight_low, preferred_element_type=F32
                    )

    if last:
        head = pl.program_id(0)
        at = pl.multiple_of(head * HEAD_DIM, HEAD_DIM)
        mixed_scr[pl.ds(at, HEAD_DIM), :] = (o_ref[0] / l_ref[0, 0:1, :]).astype(BF16)

        @pl.when(head == pl.num_programs(0) - 1)
        def _():
            mixed_ref[...] = mixed_scr[...].T


def backward_kernel(start, own, nb, tile, *refs):
    if start:
        (scal, q_ref, do_ref, kv_ref, p_ref, idx_ref, f_ref, delta_ref) = refs[:8]
        refs = refs[8:]
    else:
        (scal, q_ref, do_ref, kv_ref, p_ref, idx_ref, f_ref, delta_ref, dq_in) = refs[:9]
        refs = refs[9:]
    if own:
        (dkv_ref, dq_ref, bias_ref, ds_scr, low_scr, acc_scr, kvt_scr, band_scr) = refs
    else:
        (dkv_out, dq_ref, bias_ref, ds_scr, low_scr, acc_scr, kvt_scr, band_scr, dkv_ref) = refs
    n2 = nb * nb
    kvt_scr[...] = kv_ref[...].T
    acc_scr[...] = jnp.zeros_like(acc_scr)
    dkv_ref[...] = jnp.zeros_like(dkv_ref)
    band_scr[...] = jnp.zeros_like(band_scr)
    pair = (((1,), (1,)), ((), ()))

    for ib in range(nb):
        cols = slice(ib * tile, (ib + 1) * tile)
        query = q_ref[:, cols]
        query = jnp.concatenate([query, jnp.zeros_like(query)], axis=0)
        out_grad = do_ref[:, cols]
        zeros = jnp.zeros_like(out_grad)
        grad_pad = jnp.concatenate([zeros, out_grad], axis=0)
        factor = f_ref[0, 0:1, cols]
        scaled = (out_grad.astype(F32) * factor).astype(BF16)
        scaled_pad = jnp.concatenate([zeros, scaled], axis=0)
        delta = delta_ref[0, 0:1, cols]
        dq_old = jnp.zeros((HEAD_DIM, tile), F32) if start else dq_in[0, :, cols]
        blocks = ib + 1 if own else nb
        full = scal[3 * n2 + ib] > 0

        def grads_of(rows):
            weight_grad = jnp.dot(kv_ref[rows, :], grad_pad, preferred_element_type=F32)
            score_grad = (p_ref[0, rows, cols].astype(F32) * factor) * (weight_grad - delta)
            ds_scr[rows, :] = score_grad
            low_scr[rows, :] = score_grad.astype(BF16)

        def products_of(rows):
            dkv_ref[rows, :] += lax.dot_general(
                p_ref[0, rows, cols], scaled_pad, pair, preferred_element_type=F32
            ) + lax.dot_general(low_scr[rows, :], query, pair, preferred_element_type=F32)
            return jnp.dot(kvt_scr[:HEAD_DIM, rows], low_scr[rows, :], preferred_element_type=F32)

        @pl.when(full)
        def _():
            for jb in range(blocks):
                grads_of(slice(jb * tile, (jb + 1) * tile))
            dq_ref[0, :, cols] = dq_old + products_of(slice(0, blocks * tile))

        @pl.when(jnp.logical_not(full))
        def _():
            dq_ref[0, :, cols] = dq_old
            for jb in range(blocks):

                @pl.when(scal[jb * nb + ib] > 0)
                def _(jb=jb):
                    rows = slice(jb * tile, (jb + 1) * tile)
                    grads_of(rows)
                    dq_ref[0, :, cols] += products_of(rows)

        for jb in range(blocks):
            t = jb * nb + ib

            @pl.when(scal[t] > 0)
            def _(jb=jb, t=t):
                least = scal[n2 + t]
                if own:
                    least = jnp.maximum(least, BAND)

                spots = range(jb * tile, (jb + 1) * tile, 64)

                def some(b):
                    total = jnp.zeros((8, tile), F32)
                    for r in spots:
                        hit = idx_ref[0, r : r + 64, cols] == b
                        part = jnp.where(hit, ds_scr[r : r + 64, :], 0.0)
                        total = total + jnp.sum(part.reshape(8, 8, tile), axis=0)
                    acc_scr[b] += total
                    return total

                if own:

                    @pl.loop(least, scal[2 * n2 + t] + 1)
                    def _(b):
                        some(b)

                else:
                    rest = jnp.zeros((8, tile), F32)
                    for r in spots:
                        rest = rest + jnp.sum(
                            ds_scr[r : r + 64, :].reshape(8, 8, tile), axis=0
                        )
                    acc_scr[least] += lax.fori_loop(
                        least + 1, scal[2 * n2 + t] + 1, lambda b, left: left - some(b), rest
                    )

        if own:
            def band_of(key_at, keys, lane_at):
                here = slice(key_at, key_at + keys)
                lanes = slice(cols.start + lane_at, cols.start + lane_at + 128)
                band_scr[128 - keys :, :] += jnp.where(
                    idx_ref[0, here, lanes] < BAND, ds_scr[here, lane_at : lane_at + 128], 0.0
                )

            for lane_at in range(0, tile, 128):
                band_of(cols.start + lane_at, 128, lane_at)
                if lane_at > 0:
                    band_of(cols.start + lane_at - BAND, BAND, lane_at)
            if ib > 0:

                @pl.when(scal[(ib - 1) * nb + ib] > 0)
                def _():
                    band_of(cols.start - BAND, BAND, 0)

    if own:
        square = (128, 128)
        reverse = (
            lax.broadcasted_iota(I32, square, 0) + lax.broadcasted_iota(I32, square, 1) == 127
        ).astype(BF16)
        band = band_scr[...]
        upper = band.astype(BF16)
        lower = (band - upper.astype(F32)).astype(BF16)
        turned = jnp.dot(reverse, upper, preferred_element_type=F32) + jnp.dot(
            reverse, lower, preferred_element_type=F32
        )
        turned = pltpu.roll(turned, 0, 1, stride=1, stride_axis=0)
        bias_ref[0, NBUCKET:, :] = jnp.sum(turned.reshape(16, 8, 128), axis=0)
    else:
        bias_ref[0, NBUCKET:, :] = jnp.zeros((8, 128), F32)
    if not own:
        dkv_out[...] = dkv_ref[...].astype(BF16)
    folded = jnp.sum(acc_scr[...], axis=1)
    bias = folded[:, :128]
    for c in range(1, tile // 128):
        bias = bias + folded[:, c * 128 : (c + 1) * 128]
    bias_ref[0, :NBUCKET, :] = bias


def buckets_of(scal, qpos, qseg, kpos, kseg, tile):
    planes, rows = kpos.shape[:2]
    nb = rows // tile
    return pl.pallas_call(
        functools.partial(bucket_kernel, nb, tile),
        grid=(planes,),
        in_specs=[
            pl.BlockSpec(memory_space=pltpu.SMEM),
            pl.BlockSpec((1, rows), lambda p: (0, 0)),
            pl.BlockSpec((1, rows), lambda p: (0, 0)),
            pl.BlockSpec((1, rows, 1), lambda p: (p, 0, 0)),
            pl.BlockSpec((1, rows, 1), lambda p: (p, 0, 0)),
        ],
        out_specs=pl.BlockSpec((1, rows, rows), lambda p: (p, 0, 0)),
        out_shape=jax.ShapeDtypeStruct((planes, rows, rows), I32),
        compiler_params=pltpu.CompilerParams(
            dimension_semantics=("arbitrary",), vmem_limit_bytes=VMEM_LIMIT
        ),
        cost_estimate=pl.CostEstimate(
            flops=planes * rows * rows * 16,
            bytes_accessed=planes * rows * rows * 4,
            transcendentals=0,
        ),
    )(scal, qpos, qseg, kpos, kseg)


def forward_piece(k, last, scal, q_t, kv, table, idx, state, tile):
    heads = table.shape[0]
    rows = kv.shape[0]
    nb = rows // tile
    by_head = lambda *shape: pl.BlockSpec((1,) + shape, lambda h: (h, 0, 0))
    in_specs = [
        pl.BlockSpec(memory_space=pltpu.SMEM),
        pl.BlockSpec((HEAD_DIM, rows), lambda h: (h, 0)),
        pl.BlockSpec((rows, 2 * HEAD_DIM), lambda h: (0, h)),
        by_head(8, 128),
        pl.BlockSpec((1, rows, rows), lambda h: (k, 0, 0)),
    ]
    args = [scal, q_t, kv, table, idx]
    if k > 0:
        in_specs += [by_head(1, rows), by_head(1, rows), by_head(HEAD_DIM, rows)]
        args += list(state)
    pairs = heads * rows * rows
    out_specs = [
        by_head(rows, rows),
        by_head(1, rows),
        by_head(1, rows),
        by_head(HEAD_DIM, rows),
    ]
    out_shape = [
        jax.ShapeDtypeStruct((heads, rows, rows), BF16),
        jax.ShapeDtypeStruct((heads, 1, rows), F32),
        jax.ShapeDtypeStruct((heads, 1, rows), F32),
        jax.ShapeDtypeStruct((heads, HEAD_DIM, rows), F32),
    ]
    scratch_shapes = [
        pltpu.VMEM((rows, tile), F32),
        pltpu.VMEM((2 * HEAD_DIM, rows), BF16),
    ]
    if last:
        head_cols = heads * HEAD_DIM
        out_specs.append(pl.BlockSpec((rows, head_cols), lambda h: (0, 0)))
        out_shape.append(jax.ShapeDtypeStruct((rows, head_cols), BF16))
        scratch_shapes.append(pltpu.VMEM((head_cols, rows), BF16))
    return pl.pallas_call(
        functools.partial(forward_kernel, k == 0, last, nb, tile),
        grid=(heads,),
        in_specs=in_specs,
        out_specs=out_specs,
        out_shape=out_shape,
        scratch_shapes=scratch_shapes,
        compiler_params=pltpu.CompilerParams(
            dimension_semantics=("arbitrary",), vmem_limit_bytes=VMEM_LIMIT
        ),
        cost_estimate=pl.CostEstimate(
            flops=pairs * 4 * 128, bytes_accessed=pairs * 4, transcendentals=pairs
        ),
    )(*args)


def backward_piece(k, scal, q_t, do_t, kv, probs, idx, factor, delta, dq, tile):
    heads = probs.shape[0]
    rows = kv.shape[0]
    nb = rows // tile
    start = dq is None
    by_head = lambda *shape: pl.BlockSpec((1,) + shape, lambda h: (h, 0, 0))
    in_specs = [
        pl.BlockSpec(memory_space=pltpu.SMEM),
        pl.BlockSpec((HEAD_DIM, rows), lambda h: (h, 0)),
        pl.BlockSpec((HEAD_DIM, rows), lambda h: (h, 0)),
        pl.BlockSpec((rows, 2 * HEAD_DIM), lambda h: (0, h)),
        by_head(rows, rows),
        pl.BlockSpec((1, rows, rows), lambda h: (k, 0, 0)),
        by_head(1, rows),
        by_head(1, rows),
    ]
    args = [scal, q_t, do_t, kv, probs, idx, factor, delta]
    if not start:
        in_specs += [by_head(HEAD_DIM, rows)]
        args += [dq]
    pairs = heads * rows * rows
    return pl.pallas_call(
        functools.partial(backward_kernel, start, k == 0, nb, tile),
        grid=(heads,),
        in_specs=in_specs,
        out_specs=[
            pl.BlockSpec((rows, 2 * HEAD_DIM), lambda h: (0, h)),
            by_head(HEAD_DIM, rows),
            by_head(NBUCKET + 8, 128),
        ],
        out_shape=[
            jax.ShapeDtypeStruct((rows, heads * 2 * HEAD_DIM), F32 if k == 0 else BF16),
            jax.ShapeDtypeStruct((heads, HEAD_DIM, rows), F32),
            jax.ShapeDtypeStruct((heads, NBUCKET + 8, 128), F32),
        ],
        scratch_shapes=[
            pltpu.VMEM((rows, tile), F32),
            pltpu.VMEM((rows, tile), BF16),
            pltpu.VMEM((NBUCKET, 8, tile), F32),
            pltpu.VMEM((2 * HEAD_DIM, rows), BF16),
            pltpu.VMEM((128, 128), F32),
        ]
        + ([] if k == 0 else [pltpu.VMEM((rows, 2 * HEAD_DIM), F32)]),
        compiler_params=pltpu.CompilerParams(
            dimension_semantics=("arbitrary",), vmem_limit_bytes=VMEM_LIMIT
        ),
        cost_estimate=pl.CostEstimate(
            flops=pairs * 8 * 128, bytes_accessed=pairs * 4, transcendentals=0
        ),
    )(*args)


def shards(
    block_input,
    w_qkv,
    w_attn_out,
    w_router,
    gain_attn,
    gain_moe,
    rel_bias,
    w_in,
    w_out,
    routes,
    segment_ids,
    bucket_table,
    out_grad,
):
    tok_rows, width = block_input.shape
    planes = lax.axis_size("pl")
    group = lax.axis_size("fx") * lax.axis_size("wsh")
    devices = planes * group
    cores = lax.axis_size("grp")
    plane_rank = lax.axis_index("pl")
    place = lax.axis_index(PLANE)
    device_rank = plane_rank * group + place
    core_rank = lax.axis_index("grp")
    heads = HEADS // group
    head_cols = heads * HEAD_DIM
    rows = tok_rows * group
    w_rows = w_qkv.shape[1]
    expert_count = w_router.shape[1]
    bias_share = rel_bias.shape[0]

    split = cores if w_rows % cores == 0 else 1
    part_rows = w_rows // split

    def own_part(array, axis):
        if split == 1:
            return array
        return lax.dynamic_slice_in_dim(array, core_rank * part_rows, part_rows, axis)

    def join_parts(array):
        if split > 1:
            both = lax.all_gather(array, "grp", axis=0, tiled=False)
            array = jnp.transpose(both, (1, 0, 2, 3))
        return array.reshape(devices * w_rows, array.shape[-1])

    def exchange(array, axes=ALL):
        return lax.all_to_all(array, axes, split_axis=0, concat_axis=0, tiled=True)

    def plane_send(block_of):
        came = [block_of(0)]
        for j in range(1, group):
            onward = [(i, (i + j) % group) for i in range(group)]
            came.append(lax.ppermute(block_of(j), PLANE, onward))
        return [came[-i % group] for i in range(group)]

    def in_place_order(blocks):
        size = blocks[0].shape[0]
        twice = jnp.concatenate(blocks + blocks[:-1], axis=0)
        return lax.dynamic_slice_in_dim(twice, (-place % group) * size, size * group, 0)

    capacity = max(2, 4 * tok_rows // expert_count)
    expert_ids = jnp.arange(expert_count, dtype=I32)
    route_hits = routes[:, :, None] == expert_ids[None, None, :]
    flat_hits = route_hits.reshape(tok_rows * 2, expert_count)
    order = jnp.arange(tok_rows * 2, dtype=I32)
    earlier = (order[:, None] > order[None, :]).astype(BF16)
    ranks = jnp.dot(earlier, flat_hits.astype(BF16), preferred_element_type=F32)
    slot_ranks = jnp.sum(jnp.where(flat_hits, ranks, 0.0), axis=1).astype(I32)
    slot_ids = routes * capacity + slot_ranks.reshape(tok_rows, 2)
    slot_count = expert_count * capacity
    slot_numbers = jnp.arange(slot_count, dtype=I32)
    hit_first = slot_numbers[:, None] == slot_ids[None, :, 0]
    hit_second = slot_numbers[:, None] == slot_ids[None, :, 1]
    table_first = hit_first.astype(BF16)
    table_second = hit_second.astype(BF16)
    slot_table = table_first + table_second
    other_expert = jnp.sum(
        jnp.where(hit_first, routes[None, :, 1], 0) + jnp.where(hit_second, routes[None, :, 0], 0),
        axis=1,
    )

    plane_input = in_place_order(plane_send(lambda j: block_input))
    gathered_out = lax.all_gather(w_attn_out, ALL, axis=0, tiled=True)

    def join_small(rows_of, small_of):
        count, height = rows_of.shape[:2]
        spare = -(-small_of.shape[1] // height)
        small_of = jnp.pad(small_of, ((0, 0), (0, spare * height - small_of.shape[1])))
        return jnp.concatenate([rows_of, small_of.reshape(count, height, spare)], axis=2)

    qkv_part = own_part(w_qkv, 1)
    q_part = qkv_part[0].reshape(part_rows, group, head_cols)
    kv_part = qkv_part[1:].reshape(2, part_rows, group, heads, HEAD_DIM)
    kv_part = jnp.transpose(kv_part, (1, 2, 3, 0, 4)).reshape(part_rows, group, 2 * head_cols)
    qkv_pay = jnp.transpose(jnp.concatenate([q_part, kv_part], axis=2), (1, 0, 2))
    small = jnp.concatenate([w_router.reshape(-1), gain_attn, gain_moe, rel_bias])
    pay_cols = 3 * head_cols
    small_count = small.shape[0]
    small = jnp.concatenate(
        [
            jnp.broadcast_to(small[None], (devices, small_count)),
            other_expert.astype(BF16).reshape(devices, capacity),
        ],
        axis=1,
    )
    qkv_pay = jnp.broadcast_to(qkv_pay[None], (planes,) + qkv_pay.shape)
    qkv_pay = qkv_pay.reshape(devices, part_rows, pay_cols)
    qkv_pay = join_small(qkv_pay, small)
    qkv_got = lax.all_to_all(qkv_pay, ALL, split_axis=0, concat_axis=0, tiled=True)
    positions = positions_of(segment_ids)
    bucket_ids = jnp.arange(NBUCKET, dtype=I32)
    edges = jnp.sum((bucket_table[None, :] < bucket_ids[:, None]).astype(I32), axis=1)
    tile = 256 if rows % 256 == 0 else rows
    nb = rows // tile

    def ranges_of(plane):
        first = jnp.maximum(plane, 0) * rows
        pos = lax.dynamic_slice_in_dim(positions, first, rows)
        seg = lax.dynamic_slice_in_dim(segment_ids, first, rows)
        pos_t, seg_t = pos.reshape(nb, tile), seg.reshape(nb, tile)
        limits = (
            jnp.min(pos_t, axis=1),
            jnp.max(pos_t, axis=1),
            jnp.min(seg_t, axis=1),
            jnp.max(seg_t, axis=1),
        )
        return first, pos, seg, limits

    q_first, q_pos, q_seg, (q_pos_min, q_pos_max, q_seg_min, q_seg_max) = ranges_of(plane_rank)
    tile_ids = jnp.arange(nb, dtype=I32)

    def bucket_of(distance):
        return jnp.sum((distance[:, :, None] >= edges[None, None, 1:]).astype(I32), axis=2)

    scal_of, key_info = [], []
    for k in range(planes):
        plane = plane_rank - k
        k_first, k_pos, k_seg, (k_pos_min, k_pos_max, k_seg_min, k_seg_max) = ranges_of(plane)
        causal = (k_first + tile_ids * tile)[:, None] <= (q_first + tile_ids * tile + tile - 1)[
            None, :
        ]
        own = jnp.logical_or(
            (k_seg_min == 0)[:, None],
            jnp.logical_and(
                k_seg_min[:, None] <= q_seg_max[None, :], k_seg_max[:, None] >= q_seg_min[None, :]
            ),
        )
        flags = jnp.logical_and(jnp.logical_and(causal, own), plane >= 0).astype(I32)
        least = bucket_of(jnp.maximum(q_pos_min[None, :] - k_pos_max[:, None], 0))
        most = bucket_of(jnp.maximum(q_pos_max[None, :] - k_pos_min[:, None], 0))
        beyond = jnp.logical_and(k == 0, tile_ids[:, None] > tile_ids[None, :])
        full = jnp.min(jnp.where(beyond, 1, flags), axis=0)
        scal_of.append(
            jnp.concatenate(
                [
                    flags.reshape(-1),
                    least.reshape(-1),
                    most.reshape(-1),
                    full,
                    edges,
                    jnp.full((EDGE_GROUP,), 1 << 30, I32),
                    jnp.stack([q_first, k_first]).astype(I32),
                ]
            )
        )
        key_info.append((k_pos[:, None], k_seg[:, None]))
    bucket_idx = buckets_of(
        jnp.stack(scal_of),
        q_pos[None, :],
        q_seg[None, :],
        jnp.stack([info[0] for info in key_info]),
        jnp.stack([info[1] for info in key_info]),
        tile,
    )

    qkv_got, bucket_idx = lax.optimization_barrier((qkv_got, bucket_idx))
    w_heads = join_parts(qkv_got[:, :, :pay_cols])
    small_got = qkv_got[:, :, pay_cols:].reshape(devices, -1)
    router_size = w_rows * expert_count
    full_router = small_got[:, :router_size].reshape(width, expert_count)
    at = router_size
    gain_attn_full = small_got[:, at : at + w_rows].reshape(width).astype(F32)
    at += w_rows
    gain_moe_full = small_got[:, at : at + w_rows].reshape(width).astype(F32)
    at += w_rows
    bias_full = small_got[:, at : at + bias_share].reshape(HEADS, NBUCKET).astype(F32)
    at += bias_share
    other_arrived = small_got[:, at : at + capacity].reshape(slot_count).astype(F32)
    w_query = w_heads[:, :head_cols]
    w_keyval = w_heads[:, head_cols:]

    plane_wide = plane_input.astype(F32)
    plane_inverse = norm_inverse(plane_wide)
    attn_in = (plane_wide * plane_inverse * gain_attn_full).astype(BF16)
    q_t = lax.dot_general(
        w_query, attn_in, (((0,), (1,)), ((), ())), preferred_element_type=F32
    ).astype(BF16)
    keyval = jnp.dot(attn_in, w_keyval, preferred_element_type=F32).astype(BF16)
    bias_local = lax.dynamic_slice_in_dim(bias_full, place * heads, heads, 0) * LOG2E
    bias_table = jnp.concatenate(
        [bias_local, jnp.full((heads, 128 - NBUCKET), NEGATIVE, F32)], axis=1
    )
    bias_table = jnp.broadcast_to(bias_table[:, None, :], (heads, 8, 128))

    upward = [(i, i + 1) for i in range(planes - 1)]
    downward = [(i + 1, i) for i in range(planes - 1)]
    grad_send = jnp.dot(slot_table, out_grad, preferred_element_type=F32).astype(BF16)
    kv_pieces, probs, tops, state = [keyval], [], [], None
    travelling = lax.ppermute(keyval, "pl", upward) if planes > 1 else None
    for k in range(planes):
        made = forward_piece(
            k,
            k == planes - 1,
            scal_of[k],
            q_t,
            kv_pieces[k],
            bias_table,
            bucket_idx,
            state,
            tile,
        )
        probs.append(made[0])
        state = made[1:4]
        tops.append(made[1])
        if k == planes - 1:
            break
        if k == planes - 2:
            travelling, state, grad_send, gathered_out = lax.optimization_barrier(
                (travelling, state, grad_send, gathered_out)
            )
        else:
            travelling, state = lax.optimization_barrier((travelling, state))
        kv_pieces.append(travelling)
        if k + 2 < planes:
            travelling = lax.ppermute(travelling, "pl", upward)
    grad_raw = exchange(grad_send.reshape(expert_count, capacity, width)).reshape(
        slot_count, width
    )
    final_top, final_sum, out_sum = state
    mixed_own = made[4].reshape(group, tok_rows, head_cols)
    mixed = jnp.concatenate(
        plane_send(lambda j: lax.dynamic_index_in_dim(mixed_own, (place + j) % group, 0, False)),
        axis=1,
    )
    turned_out = lax.dynamic_slice_in_dim(
        jnp.concatenate([gathered_out, gathered_out], axis=0), place * head_cols, width, 0
    )

    input_wide = block_input.astype(F32)
    residual = input_wide + jnp.dot(mixed, turned_out, preferred_element_type=F32)
    inverse_moe = norm_inverse(residual)
    moe_in = (residual * inverse_moe * gain_moe_full).astype(BF16)
    outgoing = jnp.dot(slot_table, moe_in, preferred_element_type=F32).astype(BF16)
    outgoing, grad_raw = lax.optimization_barrier((outgoing, grad_raw))
    arrived = lax.all_to_all(
        outgoing.reshape(expert_count, capacity, width), ALL, split_axis=0, concat_axis=0, tiled=True
    ).reshape(slot_count, width)
    logits = jnp.dot(moe_in, full_router, preferred_element_type=F32)
    chosen = jnp.sum(jnp.where(route_hits, logits[:, None, :], 0.0), axis=2)
    gate_probs = jax.nn.softmax(chosen, axis=1)

    expert_in = w_in[0]
    expert_out = w_out[0]
    row_logits = jnp.dot(arrived, full_router, preferred_element_type=F32)
    own_logit = jnp.sum(jnp.where(expert_ids[None, :] == device_rank, row_logits, 0.0), axis=1)
    other_logit = jnp.sum(
        jnp.where(expert_ids[None, :].astype(F32) == other_arrived[:, None], row_logits, 0.0), axis=1
    )
    top_logit = jnp.maximum(own_logit, other_logit)
    own_part_exp = jnp.exp(own_logit - top_logit)
    row_gate = own_part_exp / (own_part_exp + jnp.exp(other_logit - top_logit))
    grad_wide = grad_raw.astype(F32)
    made_grad = (row_gate[:, None] * grad_wide).astype(BF16)

    pre_act = jnp.dot(arrived, expert_in, preferred_element_type=F32)
    hidden_wide, gelu_back = jax.vjp(
        lambda inner_vals: jax.nn.gelu(inner_vals, approximate=True), pre_act
    )
    hidden = hidden_wide.astype(BF16)
    hidden_raw = lax.dot_general(
        grad_raw, expert_out, (((1,), (1,)), ((), ())), preferred_element_type=F32
    )
    slot_gate_grad = jnp.sum(hidden_raw * hidden.astype(F32), axis=1)
    pre_grad = gelu_back(hidden_raw * row_gate[:, None])[0].astype(BF16)
    slope = row_gate * (1.0 - row_gate) * slot_gate_grad
    signs = (expert_ids[None, :] == device_rank).astype(F32) - (
        expert_ids[None, :].astype(F32) == other_arrived[:, None]
    ).astype(F32)
    row_logit_grad = slope[:, None] * signs
    logit_high = row_logit_grad.astype(BF16)
    logit_low = (row_logit_grad - logit_high.astype(F32)).astype(BF16)
    row_logit_grad = jnp.concatenate([logit_high, logit_low], axis=1)
    row_grad = lax.dot_general(
        pre_grad, expert_in, (((1,), (1,)), ((), ())), preferred_element_type=F32
    )
    row_grad = (
        row_grad
        + lax.dot_general(
            row_logit_grad,
            jnp.concatenate([full_router, full_router], axis=1),
            (((1,), (1,)), ((), ())),
            preferred_element_type=F32,
        )
    ).astype(BF16)
    returned_grads = lax.all_to_all(
        row_grad.reshape(expert_count, capacity, width),
        ALL,
        split_axis=0,
        concat_axis=0,
        tiled=True,
    ).reshape(slot_count, width)
    hidden_late, made_late, row_grad = lax.optimization_barrier((hidden, made_grad, row_grad))
    expert_made = jnp.dot(hidden_late, expert_out, preferred_element_type=F32).astype(BF16)
    w_out_grad = lax.dot_general(
        hidden_late, made_late, (((0,), (0,)), ((), ())), preferred_element_type=F32
    )[None]
    router_pair = lax.dot_general(
        arrived, row_logit_grad, (((0,), (0,)), ((), ())), preferred_element_type=F32
    )
    router_grad = router_pair[:, :expert_count] + router_pair[:, expert_count:]
    returned_grads, expert_made, w_out_grad = lax.optimization_barrier(
        (returned_grads, expert_made, w_out_grad)
    )
    returned = exchange(expert_made.reshape(expert_count, capacity, width)).reshape(
        slot_count, width
    )

    moe_in_grad = lax.dot_general(
        slot_table, returned_grads, (((0,), (0,)), ((), ())), preferred_element_type=F32
    )
    grad_out = out_grad.astype(F32)
    residual_grad = grad_out + norm_input_grad(residual, inverse_moe, gain_moe_full, moe_in_grad)
    branch_grad = residual_grad.astype(BF16)
    mixed_grad = lax.dot_general(
        branch_grad, turned_out, (((1,), (1,)), ((), ())), preferred_element_type=F32
    ).astype(BF16)
    grad_t = in_place_order(
        plane_send(lambda j: mixed_grad[:, j * head_cols : (j + 1) * head_cols])
    ).T

    head_out_t = out_sum / final_sum
    delta = jnp.sum(
        grad_t.astype(F32).reshape(heads, HEAD_DIM, rows) * head_out_t, axis=1, keepdims=True
    )
    query_grad, carried, bias_parts = None, None, []
    for k in reversed(range(planes)):
        factor = jnp.exp2(tops[k] - final_top) / final_sum
        dkv, query_grad, bias_part = backward_piece(
            k,
            scal_of[k],
            q_t,
            grad_t,
            kv_pieces[k],
            probs[k],
            bucket_idx,
            factor,
            delta,
            query_grad,
            tile,
        )
        bias_parts.append(bias_part)
        if carried is None:
            total = dkv
        else:
            carried, dkv, query_grad = lax.optimization_barrier((carried, dkv, query_grad))
            total = dkv.astype(F32) + carried.astype(F32)
        if k == 0:
            break
        sent = total.astype(BF16)
        if k == planes - 1:
            sent, query_grad, returned, branch_late = lax.optimization_barrier(
                (sent, query_grad, returned, branch_grad)
            )
        carried = lax.ppermute(sent, "pl", downward)
        if k == planes - 1:
            attn_out_part = lax.dot_general(
                mixed, branch_late, (((0,), (0,)), ((), ())), preferred_element_type=F32
            )
            attn_out_part = lax.dynamic_slice_in_dim(
                jnp.concatenate([attn_out_part, attn_out_part], axis=0),
                width - place * head_cols,
                width,
                0,
            )
            attn_out_part = attn_out_part.astype(BF16).reshape(planes, group, w_rows, width)
            attn_out_part = sum(
                block.astype(F32)
                for block in plane_send(
                    lambda j: lax.dynamic_index_in_dim(
                        attn_out_part, (place + j) % group, 1, False
                    )
                )
            ).astype(BF16)
            gain_moe_grad = jnp.sum(moe_in_grad * residual * inverse_moe, axis=0)
    scale_row = jnp.tile(
        jnp.concatenate([jnp.full((HEAD_DIM,), 0.125, F32), jnp.ones((HEAD_DIM,), F32)]), heads
    )
    keyval_grad = (total * scale_row[None, :]).astype(BF16)
    query_grad = (query_grad.reshape(head_cols, rows) * 0.125).astype(BF16).T
    head_grads = jnp.concatenate([query_grad, keyval_grad], axis=1)
    bias_rows = sum(bias_parts)
    band_rows = jnp.roll(jnp.sum(bias_rows[:, NBUCKET:], axis=1), 1, axis=1)[:, :BAND]
    bias_grad = jnp.sum(bias_rows[:, :NBUCKET], axis=2) + jnp.pad(
        band_rows, ((0, 0), (0, NBUCKET - BAND))
    )

    attn_in_grad = lax.dot_general(
        head_grads, w_heads, (((1,), (1,)), ((), ())), preferred_element_type=F32
    )
    gain_attn_grad = jnp.sum(attn_in_grad * plane_wide * plane_inverse, axis=0)
    w_parts = lax.dot_general(
        attn_in, head_grads, (((0,), (0,)), ((), ())), preferred_element_type=F32
    ).astype(BF16)
    bias_all = lax.dynamic_update_slice_in_dim(
        jnp.zeros((HEADS, NBUCKET), F32), bias_grad, place * heads, 0
    )
    small_grads = jnp.concatenate(
        [
            router_grad.reshape(devices, router_size),
            gain_attn_grad.reshape(devices, w_rows),
            gain_moe_grad.reshape(devices, w_rows),
            bias_all.reshape(devices, bias_share),
        ],
        axis=1,
    )
    small_high = small_grads.astype(BF16)
    small_low = (small_grads - small_high.astype(F32)).astype(BF16)
    w_parts = join_small(
        w_parts.reshape(devices, w_rows, pay_cols),
        jnp.concatenate([small_high, small_low], axis=1),
    )
    w_parts, attn_in_grad = lax.optimization_barrier((w_parts, attn_in_grad))
    w_got = exchange(w_parts)

    attn_in_grad = attn_in_grad.reshape(group, tok_rows, width)
    attn_in_grad = sum(
        block.astype(F32)
        for block in plane_send(
            lambda j: lax.dynamic_index_in_dim(
                attn_in_grad, (place + j) % group, 0, False
            ).astype(BF16)
        )
    )
    inverse_attn = norm_inverse(input_wide)
    input_grad = residual_grad + norm_input_grad(
        input_wide, inverse_attn, gain_attn_full, attn_in_grad
    )


    returned, pre_late, attn_out_part, w_parts = lax.optimization_barrier(
        (returned, pre_grad, attn_out_part, w_parts)
    )
    attn_out_grad = lax.dynamic_index_in_dim(
        attn_out_part, plane_rank, 0, False
    ).astype(F32)
    for j in range(1, planes):
        onward = [(i, (i + j) % planes) for i in range(planes)]
        block = lax.dynamic_index_in_dim(attn_out_part, (plane_rank + j) % planes, 0, False)
        attn_out_grad = attn_out_grad + lax.ppermute(block, "pl", onward).astype(F32)
    w_in_grad = lax.dot_general(
        arrived, pre_late, (((0,), (0,)), ((), ())), preferred_element_type=F32
    )[None]
    picked_first = lax.dot_general(
        table_first, returned, (((0,), (0,)), ((), ())), preferred_element_type=F32
    )
    picked_second = lax.dot_general(
        table_second, returned, (((0,), (0,)), ((), ())), preferred_element_type=F32
    )
    block_output = (
        residual + (gate_probs[:, 0:1] * picked_first + gate_probs[:, 1:2] * picked_second)
    ).astype(BF16)
    w_got, w_in_grad, block_output = lax.optimization_barrier((w_got, w_in_grad, block_output))

    w_wide = w_got.astype(F32)
    w_sum = jnp.sum(w_wide[:, :, :pay_cols].reshape(planes, group, w_rows, pay_cols), axis=0)
    q_sum = jnp.transpose(w_sum[:, :, :head_cols], (1, 0, 2)).reshape(1, w_rows, width)
    kv_sum = w_sum[:, :, head_cols:].reshape(group, w_rows, heads, 2, HEAD_DIM)
    kv_sum = jnp.transpose(kv_sum, (3, 1, 0, 2, 4)).reshape(2, w_rows, width)
    qkv_grad = jnp.concatenate([q_sum, kv_sum], axis=0)
    small_sum = jnp.sum(w_wide[:, :, pay_cols:].reshape(devices, -1), axis=0)
    small_sum = small_sum[:small_count] + small_sum[small_count : 2 * small_count]
    at = router_size
    return (
        block_output,
        input_grad,
        qkv_grad,
        attn_out_grad,
        small_sum[:at].reshape(w_rows, expert_count),
        small_sum[at : at + w_rows],
        small_sum[at + w_rows : at + 2 * w_rows],
        small_sum[at + 2 * w_rows : small_count],
        w_in_grad,
        w_out_grad,
    )


def solution(mesh):
    devices = mesh.devices
    grp, seq, wsh = devices.shape
    inner = Mesh(devices.reshape(grp, seq // 2, 2, wsh), ("grp",) + ALL)
    every = ("grp",) + ALL
    in_specs = (
        P(every, None),
        P(None, ALL, None),
        P(ALL, None),
        P(ALL, None),
        P(ALL),
        P(ALL),
        P(ALL),
        P(ALL, None, None),
        P(ALL, None, None),
        P(every, None),
        P("grp"),
        P(),
        P(every, None),
    )
    out_specs = (
        P(every, None),
        P(every, None),
        P("grp", ALL, None),
        P(every, None),
        P(every, None),
        P(every),
        P(every),
        P(every),
        P(every, None, None),
        P(every, None, None),
    )
    return jax.shard_map(
        shards, mesh=inner, in_specs=in_specs, out_specs=out_specs, check_vma=False
    )
```

```python
import functools
import math

import jax
import jax.numpy as jnp
from jax import lax
from jax.experimental import pallas as pl
from jax.experimental.pallas import tpu as pltpu
from jax.sharding import Mesh
from jax.sharding import PartitionSpec as P

HEADS = 12
HEAD_DIM = 64
NBUCKET = 32

EPSILON = 1e-06
NEGATIVE = -1e30
LOG2E = 1.4426950408889634
SCALE2 = 0.125 * LOG2E

PLANE = ("fx", "wsh")
ALL = ("pl", "fx", "wsh")
F32 = jnp.float32
BF16 = jnp.bfloat16
I32 = jnp.int32


def positions_of(segment_ids):
    total_rows = segment_ids.shape[0]
    numbers = jnp.arange(total_rows, dtype=jnp.int32)
    fresh_start = jnp.logical_or(numbers == 0, segment_ids != jnp.roll(segment_ids, 1))
    begins = lax.cummax(jnp.where(fresh_start, numbers, 0), axis=0)
    return jnp.where(segment_ids == 0, numbers, numbers - begins + total_rows // 2)


def norm_inverse(values):
    return lax.rsqrt(jnp.mean(values * values, axis=-1, keepdims=True) + EPSILON)


def norm_input_grad(values, inverse, gain_vec, grad_in):
    scaled = grad_in * gain_vec
    inner_mean = jnp.mean(scaled * values, axis=-1, keepdims=True)
    return inverse * scaled - values * inverse * inverse * inverse * inner_mean


BAND = 16
EDGE_GROUP = 4
EDGES = NBUCKET + EDGE_GROUP
VMEM_LIMIT = 60 << 20


def bucket_kernel(nb, tile, scal, qpos, qseg, kpos, kseg, idx_ref):
    piece = pl.program_id(0)
    n2 = nb * nb
    at = 3 * n2 + nb
    step = 128 if tile % 128 == 0 else tile
    q_first = scal[piece, at + EDGES]
    k_first = scal[piece, at + EDGES + 1]
    for jb in range(nb):
        for ib in range(nb):
            t = jb * nb + ib

            @pl.when(scal[piece, t] > 0)
            def _(jb=jb, ib=ib, t=t):
                low_bucket = scal[piece, n2 + t]
                high_bucket = scal[piece, 2 * n2 + t]
                cols = slice(ib * tile, (ib + 1) * tile)
                for r in range(tile // step):
                    rows = slice(jb * tile + r * step, jb * tile + (r + 1) * step)
                    key_pos = jnp.concatenate([kpos[0, rows, :]] * (tile // 128), axis=1)
                    key_seg = jnp.concatenate([kseg[0, rows, :]] * (tile // 128), axis=1)
                    distance = qpos[0:1, cols] - key_pos

                    def more(trip, count, distance=distance):
                        start = low_bucket + 1 + trip * EDGE_GROUP
                        for b in range(EDGE_GROUP):
                            count = count + jnp.where(distance >= scal[piece, at + start + b], 1, 0)
                        return count

                    count = more(0, jnp.full((step, tile), low_bucket, I32))
                    trips = lax.div(high_bucket - low_bucket + EDGE_GROUP - 1, EDGE_GROUP)
                    count = lax.fori_loop(1, trips, more, count)
                    key_row = lax.broadcasted_iota(I32, (step, tile), 0) + (k_first + rows.start)
                    query_row = lax.broadcasted_iota(I32, (step, tile), 1) + (q_first + cols.start)
                    own = jnp.logical_or(key_seg == 0, key_seg == qseg[0:1, cols])
                    seen = jnp.logical_and(key_row <= query_row, own)
                    idx_ref[0, rows, cols] = jnp.where(seen, count, NBUCKET)


def forward_kernel(first, last, nb, tile, *refs):
    if first:
        (scal, q_ref, kv_ref, tbl_ref, idx_ref) = refs[:5]
        refs = refs[5:]
    else:
        (scal, q_ref, kv_ref, tbl_ref, idx_ref, m_in, l_in, o_in) = refs[:8]
        refs = refs[8:]
    if last:
        (p_ref, m_ref, l_ref, o_ref, mixed_ref, s_scr, kvt_scr, mixed_scr) = refs
    else:
        (p_ref, m_ref, l_ref, o_ref, s_scr, kvt_scr) = refs
    n2 = nb * nb
    kvt_scr[...] = kv_ref[...].T
    table = jnp.broadcast_to(tbl_ref[0, 0:1, :], (tile, 128))

    def scores_of(rows, cols, query):
        raw = jnp.dot(kv_ref[rows, :], query, preferred_element_type=F32)
        tops = []
        for c in range(tile // 128):
            lanes = slice(c * 128, (c + 1) * 128)
            ids = idx_ref[0, rows, cols.start + c * 128 : cols.start + (c + 1) * 128]
            score = raw[:, lanes] * SCALE2 + jnp.take_along_axis(table, ids, axis=1)
            s_scr[rows, lanes] = score
            tops.append(jnp.max(score, axis=0, keepdims=True))
        return jnp.concatenate(tops, axis=1)

    for ib in range(nb):
        cols = slice(ib * tile, (ib + 1) * tile)
        query = q_ref[:, cols]
        query = jnp.concatenate([query, jnp.zeros_like(query)], axis=0)
        if first:
            m_old = jnp.full((1, tile), -3e38, F32)
            l_old = jnp.zeros((1, tile), F32)
            o_old = jnp.zeros((HEAD_DIM, tile), F32)
        else:
            m_old = m_in[0, 0:1, cols]
            l_old = l_in[0, 0:1, cols]
            o_old = o_in[0, :, cols]
        blocks = ib + 1 if first else nb
        full = scal[3 * n2 + ib] > 0

        @pl.when(full)
        def _():
            m_new = m_old
            for jb in range(blocks):
                rows = slice(jb * tile, (jb + 1) * tile)
                m_new = jnp.maximum(m_new, scores_of(rows, cols, query))
            factor = jnp.exp2(m_old - m_new)
            total = l_old * factor
            for jb in range(blocks):
                rows = slice(jb * tile, (jb + 1) * tile)
                weight = jnp.exp2(s_scr[rows, :] - m_new)
                total = total + jnp.sum(weight, axis=0, keepdims=True)
                p_ref[0, rows, cols] = weight.astype(BF16)
            made = jnp.dot(
                kvt_scr[HEAD_DIM:, : blocks * tile],
                p_ref[0, : blocks * tile, cols],
                preferred_element_type=F32,
            )
            m_ref[0, 0:1, cols] = m_new
            l_ref[0, 0:1, cols] = total
            o_ref[0, :, cols] = o_old * factor + made

        @pl.when(jnp.logical_not(full))
        def _():
            m_ref[0, 0:1, cols] = m_old
            for jb in range(blocks):

                @pl.when(scal[jb * nb + ib] > 0)
                def _(jb=jb):
                    rows = slice(jb * tile, (jb + 1) * tile)
                    m_ref[0, 0:1, cols] = jnp.maximum(
                        m_ref[0, 0:1, cols], scores_of(rows, cols, query)
                    )

            m_new = m_ref[0, 0:1, cols]
            factor = jnp.exp2(m_old - m_new)
            l_ref[0, 0:1, cols] = l_old * factor
            o_ref[0, :, cols] = o_old * factor
            for jb in range(blocks):

                @pl.when(scal[jb * nb + ib] > 0)
                def _(jb=jb):
                    rows = slice(jb * tile, (jb + 1) * tile)
                    weight = jnp.exp2(s_scr[rows, :] - m_new)
                    l_ref[0, 0:1, cols] += jnp.sum(weight, axis=0, keepdims=True)
                    weight_low = weight.astype(BF16)
                    p_ref[0, rows, cols] = weight_low
                    o_ref[0, :, cols] += jnp.dot(
                        kvt_scr[HEAD_DIM:, rows], weight_low, preferred_element_type=F32
                    )

    if last:
        head = pl.program_id(0)
        at = pl.multiple_of(head * HEAD_DIM, HEAD_DIM)
        mixed_scr[pl.ds(at, HEAD_DIM), :] = (o_ref[0] / l_ref[0, 0:1, :]).astype(BF16)

        @pl.when(head == pl.num_programs(0) - 1)
        def _():
            mixed_ref[...] = mixed_scr[...].T


def backward_kernel(start, own, nb, tile, *refs):
    if start:
        (scal, q_ref, do_ref, kv_ref, p_ref, idx_ref, f_ref, delta_ref) = refs[:8]
        refs = refs[8:]
    else:
        (scal, q_ref, do_ref, kv_ref, p_ref, idx_ref, f_ref, delta_ref, dq_in) = refs[:9]
        refs = refs[9:]
    if own:
        (dkv_ref, dq_ref, bias_ref, qg_ref, ds_scr, low_scr, acc_scr, kvt_scr, band_scr) = refs[:9]
        qg_scr = refs[9]
    else:
        (dkv_out, dq_ref, bias_ref, ds_scr, low_scr, acc_scr, kvt_scr, band_scr, dkv_ref) = refs
    n2 = nb * nb
    kvt_scr[...] = kv_ref[...].T
    acc_scr[...] = jnp.zeros_like(acc_scr)
    dkv_ref[...] = jnp.zeros_like(dkv_ref)
    band_scr[...] = jnp.zeros_like(band_scr)
    pair = (((1,), (1,)), ((), ()))

    for ib in range(nb):
        cols = slice(ib * tile, (ib + 1) * tile)
        query = q_ref[:, cols]
        query = jnp.concatenate([query, jnp.zeros_like(query)], axis=0)
        out_grad = do_ref[:, cols]
        zeros = jnp.zeros_like(out_grad)
        grad_pad = jnp.concatenate([zeros, out_grad], axis=0)
        factor = f_ref[0, 0:1, cols]
        scaled = (out_grad.astype(F32) * factor).astype(BF16)
        scaled_pad = jnp.concatenate([zeros, scaled], axis=0)
        delta = delta_ref[0, 0:1, cols]
        dq_old = jnp.zeros((HEAD_DIM, tile), F32) if start else dq_in[0, :, cols]
        blocks = ib + 1 if own else nb
        full = scal[3 * n2 + ib] > 0

        def grads_of(rows):
            weight_grad = jnp.dot(kv_ref[rows, :], grad_pad, preferred_element_type=F32)
            score_grad = (p_ref[0, rows, cols].astype(F32) * factor) * (weight_grad - delta)
            ds_scr[rows, :] = score_grad
            low_scr[rows, :] = score_grad.astype(BF16)

        def products_of(rows):
            dkv_ref[rows, :] += lax.dot_general(
                p_ref[0, rows, cols], scaled_pad, pair, preferred_element_type=F32
            ) + lax.dot_general(low_scr[rows, :], query, pair, preferred_element_type=F32)
            return jnp.dot(kvt_scr[:HEAD_DIM, rows], low_scr[rows, :], preferred_element_type=F32)

        @pl.when(full)
        def _():
            for jb in range(blocks):
                grads_of(slice(jb * tile, (jb + 1) * tile))
            dq_ref[0, :, cols] = dq_old + products_of(slice(0, blocks * tile))

        @pl.when(jnp.logical_not(full))
        def _():
            dq_ref[0, :, cols] = dq_old
            for jb in range(blocks):

                @pl.when(scal[jb * nb + ib] > 0)
                def _(jb=jb):
                    rows = slice(jb * tile, (jb + 1) * tile)
                    grads_of(rows)
                    dq_ref[0, :, cols] += products_of(rows)

        for jb in range(blocks):
            t = jb * nb + ib

            @pl.when(scal[t] > 0)
            def _(jb=jb, t=t):
                least = scal[n2 + t]
                if own:
                    least = jnp.maximum(least, BAND)

                spots = range(jb * tile, (jb + 1) * tile, 64)

                def some(b):
                    total = jnp.zeros((8, tile), F32)
                    for r in spots:
                        hit = idx_ref[0, r : r + 64, cols] == b
                        part = jnp.where(hit, ds_scr[r : r + 64, :], 0.0)
                        total = total + jnp.sum(part.reshape(8, 8, tile), axis=0)
                    acc_scr[b] += total
                    return total

                if own:

                    @pl.loop(least, scal[2 * n2 + t] + 1)
                    def _(b):
                        some(b)

                else:
                    rest = jnp.zeros((8, tile), F32)
                    for r in spots:
                        rest = rest + jnp.sum(
                            ds_scr[r : r + 64, :].reshape(8, 8, tile), axis=0
                        )
                    acc_scr[least] += lax.fori_loop(
                        least + 1, scal[2 * n2 + t] + 1, lambda b, left: left - some(b), rest
                    )

        if own:
            def band_of(key_at, keys, lane_at):
                here = slice(key_at, key_at + keys)
                lanes = slice(cols.start + lane_at, cols.start + lane_at + 128)
                band_scr[128 - keys :, :] += jnp.where(
                    idx_ref[0, here, lanes] < BAND, ds_scr[here, lane_at : lane_at + 128], 0.0
                )

            for lane_at in range(0, tile, 128):
                band_of(cols.start + lane_at, 128, lane_at)
                if lane_at > 0:
                    band_of(cols.start + lane_at - BAND, BAND, lane_at)
            if ib > 0:

                @pl.when(scal[(ib - 1) * nb + ib] > 0)
                def _():
                    band_of(cols.start - BAND, BAND, 0)

    if own:
        square = (128, 128)
        reverse = (
            lax.broadcasted_iota(I32, square, 0) + lax.broadcasted_iota(I32, square, 1) == 127
        ).astype(BF16)
        band = band_scr[...]
        upper = band.astype(BF16)
        lower = (band - upper.astype(F32)).astype(BF16)
        turned = jnp.dot(reverse, upper, preferred_element_type=F32) + jnp.dot(
            reverse, lower, preferred_element_type=F32
        )
        turned = pltpu.roll(turned, 0, 1, stride=1, stride_axis=0)
        bias_ref[0, NBUCKET:, :] = jnp.sum(turned.reshape(16, 8, 128), axis=0)
    else:
        bias_ref[0, NBUCKET:, :] = jnp.zeros((8, 128), F32)
    if own:
        head = pl.program_id(0)
        at = pl.multiple_of(head * HEAD_DIM, HEAD_DIM)
        qg_scr[pl.ds(at, HEAD_DIM), :] = (dq_ref[0] * 0.125).astype(BF16)

        @pl.when(head == pl.num_programs(0) - 1)
        def _():
            qg_ref[...] = qg_scr[...].T
    else:
        dkv_out[...] = dkv_ref[...].astype(BF16)
    folded = jnp.sum(acc_scr[...], axis=1)
    bias = folded[:, :128]
    for c in range(1, tile // 128):
        bias = bias + folded[:, c * 128 : (c + 1) * 128]
    bias_ref[0, :NBUCKET, :] = bias


def buckets_of(scal, qpos, qseg, kpos, kseg, tile):
    planes, rows = kpos.shape[:2]
    nb = rows // tile
    return pl.pallas_call(
        functools.partial(bucket_kernel, nb, tile),
        grid=(planes,),
        in_specs=[
            pl.BlockSpec(memory_space=pltpu.SMEM),
            pl.BlockSpec((1, rows), lambda p: (0, 0)),
            pl.BlockSpec((1, rows), lambda p: (0, 0)),
            pl.BlockSpec((1, rows, 128), lambda p: (p, 0, 0)),
            pl.BlockSpec((1, rows, 128), lambda p: (p, 0, 0)),
        ],
        out_specs=pl.BlockSpec((1, rows, rows), lambda p: (p, 0, 0)),
        out_shape=jax.ShapeDtypeStruct((planes, rows, rows), I32),
        compiler_params=pltpu.CompilerParams(
            dimension_semantics=("arbitrary",), vmem_limit_bytes=VMEM_LIMIT
        ),
        cost_estimate=pl.CostEstimate(
            flops=planes * rows * rows * 16,
            bytes_accessed=planes * rows * rows * 4,
            transcendentals=0,
        ),
    )(scal, qpos, qseg, kpos, kseg)


def forward_piece(k, last, scal, q_t, kv, table, idx, state, tile):
    heads = table.shape[0]
    rows = kv.shape[0]
    nb = rows // tile
    by_head = lambda *shape: pl.BlockSpec((1,) + shape, lambda h: (h, 0, 0))
    in_specs = [
        pl.BlockSpec(memory_space=pltpu.SMEM),
        pl.BlockSpec((HEAD_DIM, rows), lambda h: (h, 0)),
        pl.BlockSpec((rows, 2 * HEAD_DIM), lambda h: (0, h)),
        by_head(8, 128),
        pl.BlockSpec((1, rows, rows), lambda h: (k, 0, 0)),
    ]
    args = [scal, q_t, kv, table, idx]
    if k > 0:
        in_specs += [by_head(1, rows), by_head(1, rows), by_head(HEAD_DIM, rows)]
        args += list(state)
    pairs = heads * rows * rows
    out_specs = [
        by_head(rows, rows),
        by_head(1, rows),
        by_head(1, rows),
        by_head(HEAD_DIM, rows),
    ]
    out_shape = [
        jax.ShapeDtypeStruct((heads, rows, rows), BF16),
        jax.ShapeDtypeStruct((heads, 1, rows), F32),
        jax.ShapeDtypeStruct((heads, 1, rows), F32),
        jax.ShapeDtypeStruct((heads, HEAD_DIM, rows), F32),
    ]
    scratch_shapes = [
        pltpu.VMEM((rows, tile), F32),
        pltpu.VMEM((2 * HEAD_DIM, rows), BF16),
    ]
    if last:
        head_cols = heads * HEAD_DIM
        out_specs.append(pl.BlockSpec((rows, head_cols), lambda h: (0, 0)))
        out_shape.append(jax.ShapeDtypeStruct((rows, head_cols), BF16))
        scratch_shapes.append(pltpu.VMEM((head_cols, rows), BF16))
    return pl.pallas_call(
        functools.partial(forward_kernel, k == 0, last, nb, tile),
        grid=(heads,),
        in_specs=in_specs,
        out_specs=out_specs,
        out_shape=out_shape,
        scratch_shapes=scratch_shapes,
        compiler_params=pltpu.CompilerParams(
            dimension_semantics=("arbitrary",), vmem_limit_bytes=VMEM_LIMIT
        ),
        cost_estimate=pl.CostEstimate(
            flops=pairs * 4 * 128, bytes_accessed=pairs * 4, transcendentals=pairs
        ),
    )(*args)


def backward_piece(k, scal, q_t, do_t, kv, probs, idx, factor, delta, dq, tile):
    heads = probs.shape[0]
    rows = kv.shape[0]
    nb = rows // tile
    start = dq is None
    by_head = lambda *shape: pl.BlockSpec((1,) + shape, lambda h: (h, 0, 0))
    in_specs = [
        pl.BlockSpec(memory_space=pltpu.SMEM),
        pl.BlockSpec((HEAD_DIM, rows), lambda h: (h, 0)),
        pl.BlockSpec((HEAD_DIM, rows), lambda h: (h, 0)),
        pl.BlockSpec((rows, 2 * HEAD_DIM), lambda h: (0, h)),
        by_head(rows, rows),
        pl.BlockSpec((1, rows, rows), lambda h: (k, 0, 0)),
        by_head(1, rows),
        by_head(1, rows),
    ]
    args = [scal, q_t, do_t, kv, probs, idx, factor, delta]
    if not start:
        in_specs += [by_head(HEAD_DIM, rows)]
        args += [dq]
    pairs = heads * rows * rows
    own = k == 0
    head_cols = heads * HEAD_DIM
    out_specs = [
        pl.BlockSpec((rows, 2 * HEAD_DIM), lambda h: (0, h)),
        by_head(HEAD_DIM, rows),
        by_head(NBUCKET + 8, 128),
    ]
    out_shape = [
        jax.ShapeDtypeStruct((rows, heads * 2 * HEAD_DIM), F32 if own else BF16),
        jax.ShapeDtypeStruct((heads, HEAD_DIM, rows), F32),
        jax.ShapeDtypeStruct((heads, NBUCKET + 8, 128), F32),
    ]
    scratch_shapes = [
        pltpu.VMEM((rows, tile), F32),
        pltpu.VMEM((rows, tile), BF16),
        pltpu.VMEM((NBUCKET, 8, tile), F32),
        pltpu.VMEM((2 * HEAD_DIM, rows), BF16),
        pltpu.VMEM((128, 128), F32),
    ]
    if own:
        out_specs.append(pl.BlockSpec((rows, head_cols), lambda h: (0, 0)))
        out_shape.append(jax.ShapeDtypeStruct((rows, head_cols), BF16))
        scratch_shapes.append(pltpu.VMEM((head_cols, rows), BF16))
    else:
        scratch_shapes.append(pltpu.VMEM((rows, 2 * HEAD_DIM), F32))
    return pl.pallas_call(
        functools.partial(backward_kernel, start, own, nb, tile),
        grid=(heads,),
        in_specs=in_specs,
        out_specs=out_specs,
        out_shape=out_shape,
        scratch_shapes=scratch_shapes,
        compiler_params=pltpu.CompilerParams(
            dimension_semantics=("arbitrary",), vmem_limit_bytes=VMEM_LIMIT
        ),
        cost_estimate=pl.CostEstimate(
            flops=pairs * 8 * 128, bytes_accessed=pairs * 4, transcendentals=0
        ),
    )(*args)


GELU_SCALE = 0.7978845608028654
GELU_CUBE = 0.044715


def expert_kernel(
    steps,
    blocks,
    rows_ref,
    grads_ref,
    gate_ref,
    signs_ref,
    router_ref,
    win_ref,
    wout_ref,
    hidden_ref,
    pre_ref,
    row_ref,
    slope_ref,
    acc_scr,
    gate_scr,
):
    step = pl.program_id(0)

    @pl.when(step == 0)
    def _():
        acc_scr[...] = jnp.zeros_like(acc_scr)
        gate_scr[...] = jnp.zeros_like(gate_scr)

    size = rows_ref.shape[0] // blocks
    pair = (((1,), (1,)), ((), ()))
    for block in range(blocks):
        here = slice(block * size, (block + 1) * size)
        pre = jnp.dot(rows_ref[here, :], win_ref[...], preferred_element_type=F32)
        raw = lax.dot_general(
            grads_ref[here, :], wout_ref[...], pair, preferred_element_type=F32
        )
        square = pre * pre
        turn = jnp.tanh(GELU_SCALE * pre * (1.0 + GELU_CUBE * square))
        half = 0.5 + 0.5 * turn
        hidden = (pre * half).astype(BF16)
        hidden_ref[here, :] = hidden
        gate_scr[here, :] += jnp.sum(raw * hidden.astype(F32), axis=1, keepdims=True)
        slope = half + (0.5 * GELU_SCALE) * pre * (1.0 - turn * turn) * (
            1.0 + (3.0 * GELU_CUBE) * square
        )
        pre_grad = (raw * gate_ref[here, :] * slope).astype(BF16)
        pre_ref[here, :] = pre_grad
        acc_scr[here, :] += lax.dot_general(
            pre_grad, win_ref[...], pair, preferred_element_type=F32
        )

    @pl.when(step == steps - 1)
    def _():
        gate = gate_ref[...]
        slope = gate * (1.0 - gate) * gate_scr[...]
        logit = slope * signs_ref[...]
        high = logit.astype(BF16)
        low = (logit - high.astype(F32)).astype(BF16)
        routed = lax.dot_general(high, router_ref[...], pair, preferred_element_type=F32)
        routed += lax.dot_general(low, router_ref[...], pair, preferred_element_type=F32)
        row_ref[...] = (acc_scr[...] + routed).astype(BF16)
        slope_ref[...] = slope


def expert_pass(rows, grads, gate, signs, router, w_in, w_out):
    count, width = rows.shape
    units = w_in.shape[1]
    experts = router.shape[1]
    tile = 512 if units % 512 == 0 else units
    steps = units // tile
    blocks = 3 if count % 48 == 0 else 1
    whole = lambda *shape: pl.BlockSpec(shape, lambda f: (0,) * len(shape))
    return pl.pallas_call(
        functools.partial(expert_kernel, steps, blocks),
        grid=(steps,),
        in_specs=[
            whole(count, width),
            whole(count, width),
            whole(count, 1),
            whole(count, experts),
            whole(width, experts),
            pl.BlockSpec((width, tile), lambda f: (0, f)),
            pl.BlockSpec((tile, width), lambda f: (f, 0)),
        ],
        out_specs=[
            pl.BlockSpec((count, tile), lambda f: (0, f)),
            pl.BlockSpec((count, tile), lambda f: (0, f)),
            whole(count, width),
            whole(count, 1),
        ],
        out_shape=[
            jax.ShapeDtypeStruct((count, units), BF16),
            jax.ShapeDtypeStruct((count, units), BF16),
            jax.ShapeDtypeStruct((count, width), BF16),
            jax.ShapeDtypeStruct((count, 1), F32),
        ],
        scratch_shapes=[pltpu.VMEM((count, width), F32), pltpu.VMEM((count, 1), F32)],
        compiler_params=pltpu.CompilerParams(
            dimension_semantics=("arbitrary",), vmem_limit_bytes=VMEM_LIMIT
        ),
        cost_estimate=pl.CostEstimate(
            flops=6 * count * width * units,
            bytes_accessed=4 * width * units + 4 * count * units + 6 * count * width,
            transcendentals=count * units,
        ),
    )(rows, grads, gate, signs, router, w_in, w_out)


def shards(
    block_input,
    w_qkv,
    w_attn_out,
    w_router,
    gain_attn,
    gain_moe,
    rel_bias,
    w_in,
    w_out,
    routes,
    segment_ids,
    bucket_table,
    out_grad,
):
    tok_rows, width = block_input.shape
    planes = lax.axis_size("pl")
    group = lax.axis_size("fx") * lax.axis_size("wsh")
    devices = planes * group
    cores = lax.axis_size("grp")
    plane_rank = lax.axis_index("pl")
    place = lax.axis_index(PLANE)
    device_rank = plane_rank * group + place
    core_rank = lax.axis_index("grp")
    heads = HEADS // group
    head_cols = heads * HEAD_DIM
    rows = tok_rows * group
    w_rows = w_qkv.shape[1]
    expert_count = w_router.shape[1]
    bias_share = rel_bias.shape[0]

    split = cores if w_rows % cores == 0 else 1
    part_rows = w_rows // split

    def own_part(array, axis):
        if split == 1:
            return array
        return lax.dynamic_slice_in_dim(array, core_rank * part_rows, part_rows, axis)

    def join_parts(array):
        if split > 1:
            both = lax.all_gather(array, "grp", axis=0, tiled=False)
            array = jnp.transpose(both, (1, 0, 2, 3))
        return array.reshape(devices * w_rows, array.shape[-1])

    def exchange(array, axes=ALL):
        return lax.all_to_all(array, axes, split_axis=0, concat_axis=0, tiled=True)

    def plane_send(block_of):
        came = [block_of(0)]
        for j in range(1, group):
            onward = [(i, (i + j) % group) for i in range(group)]
            came.append(lax.ppermute(block_of(j), PLANE, onward))
        return [came[-i % group] for i in range(group)]

    def in_place_order(blocks):
        size = blocks[0].shape[0]
        twice = jnp.concatenate(blocks + blocks[:-1], axis=0)
        return lax.dynamic_slice_in_dim(twice, (-place % group) * size, size * group, 0)

    capacity = max(2, 4 * tok_rows // expert_count)
    expert_ids = jnp.arange(expert_count, dtype=I32)
    route_hits = routes[:, :, None] == expert_ids[None, None, :]
    flat_hits = route_hits.reshape(tok_rows * 2, expert_count)
    order = jnp.arange(tok_rows * 2, dtype=I32)
    earlier = (order[:, None] > order[None, :]).astype(BF16)
    ranks = jnp.dot(earlier, flat_hits.astype(BF16), preferred_element_type=F32)
    slot_ranks = jnp.sum(jnp.where(flat_hits, ranks, 0.0), axis=1).astype(I32)
    slot_ids = routes * capacity + slot_ranks.reshape(tok_rows, 2)
    slot_count = expert_count * capacity
    slot_numbers = jnp.arange(slot_count, dtype=I32)
    hit_first = slot_numbers[:, None] == slot_ids[None, :, 0]
    hit_second = slot_numbers[:, None] == slot_ids[None, :, 1]
    table_first = hit_first.astype(BF16)
    table_second = hit_second.astype(BF16)
    slot_table = table_first + table_second
    other_expert = jnp.sum(
        jnp.where(hit_first, routes[None, :, 1], 0) + jnp.where(hit_second, routes[None, :, 0], 0),
        axis=1,
    )

    plane_input = in_place_order(plane_send(lambda j: block_input))

    def join_small(rows_of, small_of):
        count, height = rows_of.shape[:2]
        spare = -(-small_of.shape[1] // height)
        small_of = jnp.pad(small_of, ((0, 0), (0, spare * height - small_of.shape[1])))
        return jnp.concatenate([rows_of, small_of.reshape(count, height, spare)], axis=2)

    qkv_part = own_part(w_qkv, 1)
    q_part = qkv_part[0].reshape(part_rows, group, head_cols)
    kv_part = qkv_part[1:].reshape(2, part_rows, group, heads, HEAD_DIM)
    kv_part = jnp.transpose(kv_part, (1, 2, 3, 0, 4)).reshape(part_rows, group, 2 * head_cols)
    qkv_pay = jnp.transpose(jnp.concatenate([q_part, kv_part], axis=2), (1, 0, 2))
    small = jnp.concatenate([w_router.reshape(-1), gain_attn, gain_moe, rel_bias])
    pay_cols = 3 * head_cols
    small_count = small.shape[0]
    small = jnp.concatenate(
        [
            jnp.broadcast_to(small[None], (devices, small_count)),
            other_expert.astype(BF16).reshape(devices, capacity),
        ],
        axis=1,
    )
    qkv_pay = jnp.broadcast_to(qkv_pay[None], (planes,) + qkv_pay.shape)
    qkv_pay = qkv_pay.reshape(devices, part_rows, pay_cols)
    out_pay = jnp.broadcast_to(own_part(w_attn_out, 0)[None], (devices, part_rows, width))
    qkv_pay = join_small(jnp.concatenate([qkv_pay, out_pay], axis=2), small)
    qkv_got = lax.all_to_all(qkv_pay, ALL, split_axis=0, concat_axis=0, tiled=True)
    positions = positions_of(segment_ids)
    bucket_ids = jnp.arange(NBUCKET, dtype=I32)
    edges = jnp.sum((bucket_table[None, :] < bucket_ids[:, None]).astype(I32), axis=1)
    tile = 256 if rows % 256 == 0 else rows
    nb = rows // tile

    def ranges_of(plane):
        first = jnp.maximum(plane, 0) * rows
        pos = lax.dynamic_slice_in_dim(positions, first, rows)
        seg = lax.dynamic_slice_in_dim(segment_ids, first, rows)
        pos_t, seg_t = pos.reshape(nb, tile), seg.reshape(nb, tile)
        limits = (
            jnp.min(pos_t, axis=1),
            jnp.max(pos_t, axis=1),
            jnp.min(seg_t, axis=1),
            jnp.max(seg_t, axis=1),
        )
        return first, pos, seg, limits

    q_first, q_pos, q_seg, (q_pos_min, q_pos_max, q_seg_min, q_seg_max) = ranges_of(plane_rank)
    tile_ids = jnp.arange(nb, dtype=I32)

    def bucket_of(distance):
        return jnp.sum((distance[:, :, None] >= edges[None, None, 1:]).astype(I32), axis=2)

    scal_of, key_info = [], []
    for k in range(planes):
        plane = plane_rank - k
        k_first, k_pos, k_seg, (k_pos_min, k_pos_max, k_seg_min, k_seg_max) = ranges_of(plane)
        causal = (k_first + tile_ids * tile)[:, None] <= (q_first + tile_ids * tile + tile - 1)[
            None, :
        ]
        own = jnp.logical_or(
            (k_seg_min == 0)[:, None],
            jnp.logical_and(
                k_seg_min[:, None] <= q_seg_max[None, :], k_seg_max[:, None] >= q_seg_min[None, :]
            ),
        )
        flags = jnp.logical_and(jnp.logical_and(causal, own), plane >= 0).astype(I32)
        least = bucket_of(jnp.maximum(q_pos_min[None, :] - k_pos_max[:, None], 0))
        most = bucket_of(jnp.maximum(q_pos_max[None, :] - k_pos_min[:, None], 0))
        beyond = jnp.logical_and(k == 0, tile_ids[:, None] > tile_ids[None, :])
        full = jnp.min(jnp.where(beyond, 1, flags), axis=0)
        scal_of.append(
            jnp.concatenate(
                [
                    flags.reshape(-1),
                    least.reshape(-1),
                    most.reshape(-1),
                    full,
                    edges,
                    jnp.full((EDGE_GROUP,), 1 << 30, I32),
                    jnp.stack([q_first, k_first]).astype(I32),
                ]
            )
        )
        key_info.append((k_pos, k_seg))
    bucket_idx = buckets_of(
        jnp.stack(scal_of),
        q_pos[None, :],
        q_seg[None, :],
        jnp.broadcast_to(
            jnp.stack([info[0] for info in key_info])[:, :, None], (planes, rows, 128)
        ),
        jnp.broadcast_to(
            jnp.stack([info[1] for info in key_info])[:, :, None], (planes, rows, 128)
        ),
        tile,
    )

    qkv_got, bucket_idx = lax.optimization_barrier((qkv_got, bucket_idx))
    w_heads = join_parts(qkv_got[:, :, :pay_cols])
    half_cols = pay_cols + width // 2
    gathered_out = jnp.concatenate(
        [
            join_parts(qkv_got[:, :, pay_cols:half_cols]),
            join_parts(qkv_got[:, :, half_cols : pay_cols + width]),
        ],
        axis=1,
    )
    small_got = qkv_got[:, :, pay_cols + width :].reshape(devices, -1)
    router_size = w_rows * expert_count
    full_router = small_got[:, :router_size].reshape(width, expert_count)
    at = router_size
    gain_attn_full = small_got[:, at : at + w_rows].reshape(width).astype(F32)
    at += w_rows
    gain_moe_full = small_got[:, at : at + w_rows].reshape(width).astype(F32)
    at += w_rows
    bias_full = small_got[:, at : at + bias_share].reshape(HEADS, NBUCKET).astype(F32)
    at += bias_share
    other_arrived = small_got[:, at : at + capacity].reshape(slot_count).astype(F32)
    w_query = w_heads[:, :head_cols]
    w_keyval = w_heads[:, head_cols:]

    plane_wide = plane_input.astype(F32)
    plane_inverse = norm_inverse(plane_wide)
    attn_in = (plane_wide * plane_inverse * gain_attn_full).astype(BF16)
    q_t = lax.dot_general(
        w_query, attn_in, (((0,), (1,)), ((), ())), preferred_element_type=F32
    ).astype(BF16)
    keyval = jnp.dot(attn_in, w_keyval, preferred_element_type=F32).astype(BF16)
    bias_local = lax.dynamic_slice_in_dim(bias_full, place * heads, heads, 0) * LOG2E
    bias_table = jnp.concatenate(
        [bias_local, jnp.full((heads, 128 - NBUCKET), NEGATIVE, F32)], axis=1
    )
    bias_table = jnp.broadcast_to(bias_table[:, None, :], (heads, 8, 128))

    upward = [(i, i + 1) for i in range(planes - 1)]
    downward = [(i + 1, i) for i in range(planes - 1)]
    grad_send = jnp.dot(slot_table, out_grad, preferred_element_type=F32).astype(BF16)
    kv_pieces, probs, tops, state = [keyval], [], [], None
    travelling = lax.ppermute(keyval, "pl", upward) if planes > 1 else None
    for k in range(planes):
        made = forward_piece(
            k,
            k == planes - 1,
            scal_of[k],
            q_t,
            kv_pieces[k],
            bias_table,
            bucket_idx,
            state,
            tile,
        )
        probs.append(made[0])
        state = made[1:4]
        tops.append(made[1])
        if k == planes - 1:
            break
        if k == planes - 2:
            travelling, state, grad_send, gathered_out = lax.optimization_barrier(
                (travelling, state, grad_send, gathered_out)
            )
        else:
            travelling, state = lax.optimization_barrier((travelling, state))
        kv_pieces.append(travelling)
        if k + 2 < planes:
            travelling = lax.ppermute(travelling, "pl", upward)
    grad_raw = exchange(grad_send.reshape(expert_count, capacity, width)).reshape(
        slot_count, width
    )
    final_top, final_sum, out_sum = state
    mixed_own = made[4].reshape(group, tok_rows, head_cols)
    mixed = jnp.concatenate(
        plane_send(lambda j: lax.dynamic_index_in_dim(mixed_own, (place + j) % group, 0, False)),
        axis=1,
    )
    turned_out = lax.dynamic_slice_in_dim(
        jnp.concatenate([gathered_out, gathered_out], axis=0), place * head_cols, width, 0
    )

    input_wide = block_input.astype(F32)
    residual = input_wide + jnp.dot(mixed, turned_out, preferred_element_type=F32)
    inverse_moe = norm_inverse(residual)
    moe_in = (residual * inverse_moe * gain_moe_full).astype(BF16)
    outgoing = jnp.dot(slot_table, moe_in, preferred_element_type=F32).astype(BF16)
    outgoing, grad_raw = lax.optimization_barrier((outgoing, grad_raw))
    arrived = lax.all_to_all(
        outgoing.reshape(expert_count, capacity, width), ALL, split_axis=0, concat_axis=0, tiled=True
    ).reshape(slot_count, width)
    logits = jnp.dot(moe_in, full_router, preferred_element_type=F32)
    chosen = jnp.sum(jnp.where(route_hits, logits[:, None, :], 0.0), axis=2)
    gate_probs = jax.nn.softmax(chosen, axis=1)

    expert_in = w_in[0]
    expert_out = w_out[0]
    row_logits = jnp.dot(arrived, full_router, preferred_element_type=F32)
    own_logit = jnp.sum(jnp.where(expert_ids[None, :] == device_rank, row_logits, 0.0), axis=1)
    other_logit = jnp.sum(
        jnp.where(expert_ids[None, :].astype(F32) == other_arrived[:, None], row_logits, 0.0), axis=1
    )
    top_logit = jnp.maximum(own_logit, other_logit)
    own_part_exp = jnp.exp(own_logit - top_logit)
    row_gate = own_part_exp / (own_part_exp + jnp.exp(other_logit - top_logit))
    grad_wide = grad_raw.astype(F32)
    made_grad = (row_gate[:, None] * grad_wide).astype(BF16)

    signs = (expert_ids[None, :] == device_rank).astype(F32) - (
        expert_ids[None, :].astype(F32) == other_arrived[:, None]
    ).astype(F32)
    hidden, pre_grad, row_grad, row_slope = expert_pass(
        arrived, grad_raw, row_gate[:, None], signs, full_router, expert_in, expert_out
    )
    row_logit_grad = row_slope * signs
    logit_high = row_logit_grad.astype(BF16)
    logit_low = (row_logit_grad - logit_high.astype(F32)).astype(BF16)
    row_logit_grad = jnp.concatenate([logit_high, logit_low], axis=1)
    returned_grads = lax.all_to_all(
        row_grad.reshape(expert_count, capacity, width),
        ALL,
        split_axis=0,
        concat_axis=0,
        tiled=True,
    ).reshape(slot_count, width)
    hidden_late, made_late, row_grad = lax.optimization_barrier((hidden, made_grad, row_grad))
    expert_made = jnp.dot(hidden_late, expert_out, preferred_element_type=F32).astype(BF16)
    w_out_grad = lax.dot_general(
        hidden_late, made_late, (((0,), (0,)), ((), ())), preferred_element_type=F32
    )[None]
    router_pair = lax.dot_general(
        arrived, row_logit_grad, (((0,), (0,)), ((), ())), preferred_element_type=F32
    )
    router_grad = router_pair[:, :expert_count] + router_pair[:, expert_count:]
    returned_grads, expert_made, w_out_grad = lax.optimization_barrier(
        (returned_grads, expert_made, w_out_grad)
    )
    returned = exchange(expert_made.reshape(expert_count, capacity, width)).reshape(
        slot_count, width
    )

    moe_in_grad = lax.dot_general(
        slot_table, returned_grads, (((0,), (0,)), ((), ())), preferred_element_type=F32
    )
    grad_out = out_grad.astype(F32)
    residual_grad = grad_out + norm_input_grad(residual, inverse_moe, gain_moe_full, moe_in_grad)
    branch_grad = residual_grad.astype(BF16)
    mixed_grad = lax.dot_general(
        branch_grad, turned_out, (((1,), (1,)), ((), ())), preferred_element_type=F32
    ).astype(BF16)
    grad_t = in_place_order(
        plane_send(lambda j: mixed_grad[:, j * head_cols : (j + 1) * head_cols])
    ).T

    head_out_t = out_sum / final_sum
    delta = jnp.sum(
        grad_t.astype(F32).reshape(heads, HEAD_DIM, rows) * head_out_t, axis=1, keepdims=True
    )
    query_grad, carried, bias_parts = None, None, []
    for k in reversed(range(planes)):
        factor = jnp.exp2(tops[k] - final_top) / final_sum
        dkv, query_grad, bias_part, *query_rows = backward_piece(
            k,
            scal_of[k],
            q_t,
            grad_t,
            kv_pieces[k],
            probs[k],
            bucket_idx,
            factor,
            delta,
            query_grad,
            tile,
        )
        bias_parts.append(bias_part)
        if carried is None:
            total = dkv
        else:
            carried, dkv, query_grad, query_rows = lax.optimization_barrier(
                (carried, dkv, query_grad, query_rows)
            )
            total = dkv.astype(F32) + carried.astype(F32)
        if k == 0:
            break
        sent = total.astype(BF16)
        if k == planes - 1:
            sent, query_grad, returned, branch_late = lax.optimization_barrier(
                (sent, query_grad, returned, branch_grad)
            )
        carried = lax.ppermute(sent, "pl", downward)
        if k == planes - 1:
            attn_out_part = lax.dot_general(
                mixed, branch_late, (((0,), (0,)), ((), ())), preferred_element_type=F32
            )
            attn_out_part = lax.dynamic_slice_in_dim(
                jnp.concatenate([attn_out_part, attn_out_part], axis=0),
                width - place * head_cols,
                width,
                0,
            )
            attn_out_part = attn_out_part.astype(BF16).reshape(planes, group, w_rows, width)
            attn_out_part = sum(
                block.astype(F32)
                for block in plane_send(
                    lambda j: lax.dynamic_index_in_dim(
                        attn_out_part, (place + j) % group, 1, False
                    )
                )
            ).astype(BF16)
            gain_moe_grad = jnp.sum(moe_in_grad * residual * inverse_moe, axis=0)
    scale_row = jnp.tile(
        jnp.concatenate([jnp.full((HEAD_DIM,), 0.125, F32), jnp.ones((HEAD_DIM,), F32)]), heads
    )
    keyval_grad = (total * scale_row[None, :]).astype(BF16)
    query_grad = query_rows[0]
    bias_rows_at = -(-bias_share // w_rows)
    bias_rows = sum(bias_parts)
    band_rows = jnp.roll(jnp.sum(bias_rows[:, NBUCKET:], axis=1), 1, axis=1)[:, :BAND]
    bias_grad = jnp.sum(bias_rows[:, :NBUCKET], axis=2) + jnp.pad(
        band_rows, ((0, 0), (0, NBUCKET - BAND))
    )

    w_query_part = lax.dot_general(
        attn_in, query_grad, (((0,), (0,)), ((), ())), preferred_element_type=F32
    )
    w_keyval_part = lax.dot_general(
        attn_in, keyval_grad, (((0,), (0,)), ((), ())), preferred_element_type=F32
    )
    gain_attn_grad = (
        jnp.sum(w_query_part * w_query.astype(F32), axis=1, keepdims=True)
        + jnp.sum(w_keyval_part * w_keyval.astype(F32), axis=1, keepdims=True)
    ) / gain_attn_full[:, None]
    bias_all = lax.dynamic_update_slice_in_dim(
        jnp.zeros((HEADS, NBUCKET), F32), bias_grad, place * heads, 0
    ).reshape(devices, bias_share)
    bias_all = jnp.pad(bias_all, ((0, 0), (0, bias_rows_at * w_rows - bias_share)))
    bias_all = jnp.transpose(bias_all.reshape(devices, bias_rows_at, w_rows), (0, 2, 1))
    small_grads = jnp.concatenate(
        [
            router_grad,
            gain_moe_grad[:, None],
            gain_attn_grad,
            bias_all.reshape(width, bias_rows_at),
        ],
        axis=1,
    )
    small_high = small_grads.astype(BF16)
    small_low = (small_grads - small_high.astype(F32)).astype(BF16)
    w_parts = jnp.concatenate(
        [w_query_part.astype(BF16), w_keyval_part.astype(BF16), small_high, small_low], axis=1
    ).reshape(devices, w_rows, -1)
    w_parts, query_grad, keyval_grad = lax.optimization_barrier(
        (w_parts, query_grad, keyval_grad)
    )
    w_got = exchange(w_parts)

    attn_in_grad = lax.dot_general(
        query_grad, w_query, (((1,), (1,)), ((), ())), preferred_element_type=F32
    ) + lax.dot_general(
        keyval_grad, w_keyval, (((1,), (1,)), ((), ())), preferred_element_type=F32
    )
    attn_in_grad = attn_in_grad.reshape(group, tok_rows, width)
    pre_late, attn_out_part, w_parts = lax.optimization_barrier(
        (pre_grad, attn_out_part, w_parts)
    )
    attn_out_came = [lax.dynamic_index_in_dim(attn_out_part, plane_rank, 0, False)]
    for j in range(1, planes):
        onward = [(i, (i + j) % planes) for i in range(planes)]
        block = lax.dynamic_index_in_dim(attn_out_part, (plane_rank + j) % planes, 0, False)
        attn_out_came.append(lax.ppermute(block, "pl", onward))
    w_in_grad = lax.dot_general(
        arrived, pre_late, (((0,), (0,)), ((), ())), preferred_element_type=F32
    )[None]
    attn_in_grad, w_in_grad = lax.optimization_barrier((attn_in_grad, w_in_grad))
    came = plane_send(
        lambda j: lax.dynamic_index_in_dim(attn_in_grad, (place + j) % group, 0, False).astype(BF16)
    )
    attn_in_grad = sum(block.astype(F32) for block in came)
    attn_out_grad = sum(block.astype(F32) for block in attn_out_came)
    inverse_attn = norm_inverse(input_wide)
    input_grad = residual_grad + norm_input_grad(
        input_wide, inverse_attn, gain_attn_full, attn_in_grad
    )


    picked_first = lax.dot_general(
        table_first, returned, (((0,), (0,)), ((), ())), preferred_element_type=F32
    )
    picked_second = lax.dot_general(
        table_second, returned, (((0,), (0,)), ((), ())), preferred_element_type=F32
    )
    block_output = (
        residual + (gate_probs[:, 0:1] * picked_first + gate_probs[:, 1:2] * picked_second)
    ).astype(BF16)
    w_got, w_in_grad, block_output = lax.optimization_barrier((w_got, w_in_grad, block_output))

    w_wide = w_got.astype(F32)
    w_sum = jnp.sum(w_wide[:, :, :pay_cols].reshape(planes, group, w_rows, pay_cols), axis=0)
    q_sum = jnp.transpose(w_sum[:, :, :head_cols], (1, 0, 2)).reshape(1, w_rows, width)
    kv_sum = w_sum[:, :, head_cols:].reshape(group, w_rows, heads, 2, HEAD_DIM)
    kv_sum = jnp.transpose(kv_sum, (3, 1, 0, 2, 4)).reshape(2, w_rows, width)
    qkv_grad = jnp.concatenate([q_sum, kv_sum], axis=0)
    small_sum = jnp.sum(w_wide[:, :, pay_cols:], axis=0)
    columns = expert_count + 2 + bias_rows_at
    small_sum = small_sum[:, :columns] + small_sum[:, columns:]
    bias_sum = jnp.transpose(small_sum[:, expert_count + 2 :]).reshape(-1)[:bias_share]
    return (
        block_output,
        input_grad,
        qkv_grad,
        attn_out_grad,
        small_sum[:, :expert_count],
        small_sum[:, expert_count + 1],
        small_sum[:, expert_count],
        bias_sum,
        w_in_grad,
        w_out_grad,
    )


def solution(mesh):
    devices = mesh.devices
    grp, seq, wsh = devices.shape
    inner = Mesh(devices.reshape(grp, seq // 2, 2, wsh), ("grp",) + ALL)
    every = ("grp",) + ALL
    in_specs = (
        P(every, None),
        P(None, ALL, None),
        P(ALL, None),
        P(ALL, None),
        P(ALL),
        P(ALL),
        P(ALL),
        P(ALL, None, None),
        P(ALL, None, None),
        P(every, None),
        P("grp"),
        P(),
        P(every, None),
    )
    out_specs = (
        P(every, None),
        P(every, None),
        P("grp", ALL, None),
        P(every, None),
        P(every, None),
        P(every),
        P(every),
        P(every),
        P(every, None, None),
        P(every, None, None),
    )
    return jax.shard_map(
        shards, mesh=inner, in_specs=in_specs, out_specs=out_specs, check_vma=False
    )
```

```python
import functools
import math

import jax
import jax.numpy as jnp
from jax import lax
from jax.experimental import pallas as pl
from jax.experimental.pallas import tpu as pltpu
from jax.sharding import Mesh
from jax.sharding import PartitionSpec as P

HEADS = 12
HEAD_DIM = 64
NBUCKET = 32

EPSILON = 1e-06
NEGATIVE = -1e30
LOG2E = 1.4426950408889634
SCALE2 = 0.125 * LOG2E

PLANE = ("fx", "wsh")
ALL = ("pl", "fx", "wsh")
F32 = jnp.float32
BF16 = jnp.bfloat16
I32 = jnp.int32


def positions_of(segment_ids):
    total_rows = segment_ids.shape[0]
    numbers = jnp.arange(total_rows, dtype=jnp.int32)
    fresh_start = jnp.logical_or(numbers == 0, segment_ids != jnp.roll(segment_ids, 1))
    begins = lax.cummax(jnp.where(fresh_start, numbers, 0), axis=0)
    return jnp.where(segment_ids == 0, numbers, numbers - begins + total_rows // 2)


def norm_inverse(values):
    return lax.rsqrt(jnp.mean(values * values, axis=-1, keepdims=True) + EPSILON)


def norm_input_grad(values, inverse, gain_vec, grad_in):
    scaled = grad_in * gain_vec
    inner_mean = jnp.mean(scaled * values, axis=-1, keepdims=True)
    return inverse * scaled - values * inverse * inverse * inverse * inner_mean


BAND = 16
EDGE_GROUP = 4
EDGES = NBUCKET + EDGE_GROUP
VMEM_LIMIT = 60 << 20


def bucket_kernel(nb, tile, scal, qpos, qseg, kpos, kseg, idx_ref):
    piece = pl.program_id(0)
    n2 = nb * nb
    at = 3 * n2 + nb
    step = 128 if tile % 128 == 0 else tile
    q_first = scal[piece, at + EDGES]
    k_first = scal[piece, at + EDGES + 1]
    for jb in range(nb):
        for ib in range(nb):
            t = jb * nb + ib

            @pl.when(scal[piece, t] > 0)
            def _(jb=jb, ib=ib, t=t):
                low_bucket = scal[piece, n2 + t]
                high_bucket = scal[piece, 2 * n2 + t]
                cols = slice(ib * tile, (ib + 1) * tile)
                for r in range(tile // step):
                    rows = slice(jb * tile + r * step, jb * tile + (r + 1) * step)
                    key_pos = jnp.concatenate([kpos[0, rows, :]] * (tile // 128), axis=1)
                    key_seg = jnp.concatenate([kseg[0, rows, :]] * (tile // 128), axis=1)
                    distance = qpos[0:1, cols] - key_pos

                    def more(trip, count, distance=distance):
                        start = low_bucket + 1 + trip * EDGE_GROUP
                        for b in range(EDGE_GROUP):
                            count = count + jnp.where(distance >= scal[piece, at + start + b], 1, 0)
                        return count

                    count = more(0, jnp.full((step, tile), low_bucket, I32))
                    trips = lax.div(high_bucket - low_bucket + EDGE_GROUP - 1, EDGE_GROUP)
                    count = lax.fori_loop(1, trips, more, count)
                    key_row = lax.broadcasted_iota(I32, (step, tile), 0) + (k_first + rows.start)
                    query_row = lax.broadcasted_iota(I32, (step, tile), 1) + (q_first + cols.start)
                    own = jnp.logical_or(key_seg == 0, key_seg == qseg[0:1, cols])
                    seen = jnp.logical_and(key_row <= query_row, own)
                    idx_ref[0, rows, cols] = jnp.where(seen, count, NBUCKET)


def forward_kernel(first, last, nb, tile, heads, *refs):
    if first:
        (scal, q_ref, kv_ref, tbl_ref, idx_ref) = refs[:5]
        refs = refs[5:]
    else:
        (scal, q_ref, kv_ref, tbl_ref, idx_ref, m_in, l_in, o_in) = refs[:8]
        refs = refs[8:]
    if last:
        (p_ref, m_ref, l_ref, o_ref, mixed_ref, s_scr, kvt_scr, mixed_scr) = refs
    else:
        (p_ref, m_ref, l_ref, o_ref, s_scr, kvt_scr) = refs
    ib = pl.program_id(0)
    n2 = nb * nb
    full = scal[3 * n2 + ib] > 0
    wide = 2 * HEAD_DIM

    @pl.when(ib == 0)
    def _():
        kvt_scr[...] = kv_ref[...].T

    def one_head(head, carry):
        lanes_of = pl.ds(pl.multiple_of(head * wide, wide), wide)
        value_rows = pl.ds(pl.multiple_of(head * wide + HEAD_DIM, HEAD_DIM), HEAD_DIM)
        query = q_ref[pl.ds(pl.multiple_of(head * HEAD_DIM, HEAD_DIM), HEAD_DIM), :]
        query = jnp.concatenate([query, jnp.zeros_like(query)], axis=0)
        table = jnp.broadcast_to(tbl_ref[head, 0:1, :], (tile, 128))
        if first:
            m_old = jnp.full((1, tile), -3e38, F32)
            l_old = jnp.zeros((1, tile), F32)
            o_old = jnp.zeros((HEAD_DIM, tile), F32)
        else:
            m_old = m_in[head]
            l_old = l_in[head]
            o_old = o_in[head]

        def scores_of(rows):
            raw = jnp.dot(kv_ref[rows, lanes_of], query, preferred_element_type=F32)
            tops = []
            for c in range(tile // 128):
                lanes = slice(c * 128, (c + 1) * 128)
                score = raw[:, lanes] * SCALE2 + jnp.take_along_axis(
                    table, idx_ref[0, rows, lanes], axis=1
                )
                s_scr[rows, lanes] = score
                tops.append(jnp.max(score, axis=0, keepdims=True))
            return jnp.concatenate(tops, axis=1)

        def dense(blocks):
            m_new = m_old
            for jb in range(blocks):
                m_new = jnp.maximum(m_new, scores_of(slice(jb * tile, (jb + 1) * tile)))
            factor = jnp.exp2(m_old - m_new)
            total = l_old * factor
            for jb in range(blocks):
                rows = slice(jb * tile, (jb + 1) * tile)
                weight = jnp.exp2(s_scr[rows, :] - m_new)
                total = total + jnp.sum(weight, axis=0, keepdims=True)
                p_ref[head, rows, :] = weight.astype(BF16)
            made = jnp.dot(
                kvt_scr[value_rows, : blocks * tile],
                p_ref[head, : blocks * tile, :],
                preferred_element_type=F32,
            )
            m_ref[head] = m_new
            l_ref[head] = total
            o_ref[head] = o_old * factor + made

        if first:
            for blocks in range(1, nb + 1):

                @pl.when(jnp.logical_and(full, ib == blocks - 1))
                def _(blocks=blocks):
                    dense(blocks)

        else:

            @pl.when(full)
            def _():
                dense(nb)

        @pl.when(jnp.logical_not(full))
        def _():
            m_ref[head] = m_old
            for jb in range(nb):

                @pl.when(scal[jb * nb + ib] > 0)
                def _(jb=jb):
                    m_ref[head] = jnp.maximum(
                        m_ref[head], scores_of(slice(jb * tile, (jb + 1) * tile))
                    )

            m_new = m_ref[head]
            factor = jnp.exp2(m_old - m_new)
            l_ref[head] = l_old * factor
            o_ref[head] = o_old * factor
            for jb in range(nb):

                @pl.when(scal[jb * nb + ib] > 0)
                def _(jb=jb):
                    rows = slice(jb * tile, (jb + 1) * tile)
                    weight = jnp.exp2(s_scr[rows, :] - m_new)
                    l_ref[head] += jnp.sum(weight, axis=0, keepdims=True)
                    weight_low = weight.astype(BF16)
                    p_ref[head, rows, :] = weight_low
                    o_ref[head] += jnp.dot(
                        kvt_scr[value_rows, rows], weight_low, preferred_element_type=F32
                    )

        if last:
            at = pl.multiple_of(head * HEAD_DIM, HEAD_DIM)
            mixed_scr[pl.ds(at, HEAD_DIM), :] = (o_ref[head] / l_ref[head]).astype(BF16)
        return carry

    lax.fori_loop(0, heads, one_head, 0)
    if last:
        mixed_ref[...] = mixed_scr[...].T


def backward_kernel(start, own, nb, tile, heads, *refs):
    (scal, q_ref, do_ref, kv_ref, p_ref, idx_ref, f_ref, delta_ref) = refs[:8]
    refs = refs[8:]
    if not start:
        dq_in, refs = refs[0], refs[1:]
    if own:
        (dkv_out, dq_ref, bias_ref, qg_ref) = refs[:4]
        (ds_scr, low_scr, acc_scr, kvt_scr, band_scr, dkv_scr, qg_scr) = refs[4:]
    else:
        (dkv_out, dq_ref, bias_ref) = refs[:3]
        (ds_scr, low_scr, acc_scr, kvt_scr, dkv_scr) = refs[3:]
    ib = pl.program_id(0)
    n2 = nb * nb
    full = scal[3 * n2 + ib] > 0
    wide = 2 * HEAD_DIM
    pair = (((1,), (1,)), ((), ()))

    @pl.when(ib == 0)
    def _():
        kvt_scr[...] = kv_ref[...].T
        acc_scr[...] = jnp.zeros_like(acc_scr)
        dkv_scr[...] = jnp.zeros_like(dkv_scr)
        if own:
            band_scr[...] = jnp.zeros_like(band_scr)

    def one_head(head, carry):
        lanes_of = pl.ds(pl.multiple_of(head * wide, wide), wide)
        key_rows = pl.ds(pl.multiple_of(head * wide, wide), HEAD_DIM)
        head_rows = pl.ds(pl.multiple_of(head * HEAD_DIM, HEAD_DIM), HEAD_DIM)
        query = q_ref[head_rows, :]
        query = jnp.concatenate([query, jnp.zeros_like(query)], axis=0)
        out_grad = do_ref[head_rows, :]
        zeros = jnp.zeros_like(out_grad)
        grad_pad = jnp.concatenate([zeros, out_grad], axis=0)
        factor = f_ref[head]
        scaled = (out_grad.astype(F32) * factor).astype(BF16)
        scaled_pad = jnp.concatenate([zeros, scaled], axis=0)
        delta = delta_ref[head]
        dq_old = jnp.zeros((HEAD_DIM, tile), F32) if start else dq_in[head]

        def grads_of(rows):
            weight_grad = jnp.dot(kv_ref[rows, lanes_of], grad_pad, preferred_element_type=F32)
            score_grad = (p_ref[head, rows, :].astype(F32) * factor) * (weight_grad - delta)
            ds_scr[head, rows, :] = score_grad
            low_scr[rows, :] = score_grad.astype(BF16)

        def products_of(rows):
            dkv_scr[rows, lanes_of] += lax.dot_general(
                p_ref[head, rows, :], scaled_pad, pair, preferred_element_type=F32
            ) + lax.dot_general(low_scr[rows, :], query, pair, preferred_element_type=F32)
            return jnp.dot(kvt_scr[key_rows, rows], low_scr[rows, :], preferred_element_type=F32)

        def dense(blocks):
            for jb in range(blocks):
                grads_of(slice(jb * tile, (jb + 1) * tile))
            dq_ref[head] = dq_old + products_of(slice(0, blocks * tile))

        if own:
            for blocks in range(1, nb + 1):

                @pl.when(jnp.logical_and(full, ib == blocks - 1))
                def _(blocks=blocks):
                    dense(blocks)

        else:

            @pl.when(full)
            def _():
                dense(nb)

        @pl.when(jnp.logical_not(full))
        def _():
            dq_ref[head] = dq_old
            for jb in range(nb):

                @pl.when(scal[jb * nb + ib] > 0)
                def _(jb=jb):
                    rows = slice(jb * tile, (jb + 1) * tile)
                    grads_of(rows)
                    dq_ref[head] += products_of(rows)

        if own:
            qg_scr[head_rows, :] = (dq_ref[head] * 0.125).astype(BF16)
        return carry

    lax.fori_loop(0, heads, one_head, 0)
    if own:
        qg_ref[...] = qg_scr[...].T

    for jb in range(nb):
        t = jb * nb + ib

        @pl.when(scal[t] > 0)
        def _(jb=jb, t=t):
            least = scal[n2 + t]
            most = scal[2 * n2 + t]
            spots = range(jb * tile, (jb + 1) * tile, 32)

            def some(b):
                totals = [jnp.zeros((8, tile), F32) for _ in range(heads)]
                for r in spots:
                    hit = idx_ref[0, r : r + 32, :] == b
                    for head in range(heads):
                        part = jnp.where(hit, ds_scr[head, r : r + 32, :], 0.0)
                        totals[head] += jnp.sum(part.reshape(4, 8, tile), axis=0)
                for head in range(heads):
                    acc_scr[head, b] += totals[head]
                return totals

            if own:

                @pl.loop(jnp.maximum(least, BAND), most + 1)
                def _(b):
                    some(b)

            else:
                rest = [jnp.zeros((8, tile), F32) for _ in range(heads)]
                for head in range(heads):
                    for r in spots:
                        rest[head] += jnp.sum(
                            ds_scr[head, r : r + 32, :].reshape(4, 8, tile), axis=0
                        )

                def less(b, left):
                    return tuple(one - other for one, other in zip(left, some(b)))

                rest = lax.fori_loop(least + 1, most + 1, less, tuple(rest))
                for head in range(heads):
                    acc_scr[head, least] += rest[head]

    if own:
        def band_of(key_at, keys, lane_at):
            here = pl.ds(pl.multiple_of(key_at, BAND), keys)
            near = idx_ref[0, here, lane_at : lane_at + 128] < BAND
            for head in range(heads):
                band_scr[head, 128 - keys :, :] += jnp.where(
                    near, ds_scr[head, here, lane_at : lane_at + 128], 0.0
                )

        for lane_at in range(0, tile, 128):
            band_of(ib * tile + lane_at, 128, lane_at)
            if lane_at > 0:
                band_of(ib * tile + lane_at - BAND, BAND, lane_at)

        @pl.when(ib > 0)
        def _():
            @pl.when(scal[jnp.maximum(ib - 1, 0) * nb + ib] > 0)
            def _():
                band_of(ib * tile - BAND, BAND, 0)

    @pl.when(ib == nb - 1)
    def _():
        dkv_out[...] = dkv_scr[...].astype(dkv_out.dtype)
        for head in range(heads):
            folded = jnp.sum(acc_scr[head], axis=1)
            bias = folded[:, :128]
            for c in range(1, tile // 128):
                bias = bias + folded[:, c * 128 : (c + 1) * 128]
            bias_ref[head, :NBUCKET, :] = bias
            if own:
                square = (128, 128)
                reverse = (
                    lax.broadcasted_iota(I32, square, 0) + lax.broadcasted_iota(I32, square, 1)
                    == 127
                ).astype(BF16)
                band = band_scr[head]
                upper = band.astype(BF16)
                lower = (band - upper.astype(F32)).astype(BF16)
                turned = jnp.dot(reverse, upper, preferred_element_type=F32) + jnp.dot(
                    reverse, lower, preferred_element_type=F32
                )
                turned = pltpu.roll(turned, 0, 1, stride=1, stride_axis=0)
                bias_ref[head, NBUCKET:, :] = jnp.sum(turned.reshape(16, 8, 128), axis=0)
            else:
                bias_ref[head, NBUCKET:, :] = jnp.zeros((8, 128), F32)


def buckets_of(scal, qpos, qseg, kpos, kseg, tile):
    planes, rows = kpos.shape[:2]
    nb = rows // tile
    return pl.pallas_call(
        functools.partial(bucket_kernel, nb, tile),
        grid=(planes,),
        in_specs=[
            pl.BlockSpec(memory_space=pltpu.SMEM),
            pl.BlockSpec((1, rows), lambda p: (0, 0)),
            pl.BlockSpec((1, rows), lambda p: (0, 0)),
            pl.BlockSpec((1, rows, 128), lambda p: (p, 0, 0)),
            pl.BlockSpec((1, rows, 128), lambda p: (p, 0, 0)),
        ],
        out_specs=pl.BlockSpec((1, rows, rows), lambda p: (p, 0, 0)),
        out_shape=jax.ShapeDtypeStruct((planes, rows, rows), I32),
        compiler_params=pltpu.CompilerParams(
            dimension_semantics=("arbitrary",), vmem_limit_bytes=VMEM_LIMIT
        ),
        cost_estimate=pl.CostEstimate(
            flops=planes * rows * rows * 16,
            bytes_accessed=planes * rows * rows * 4,
            transcendentals=0,
        ),
    )(scal, qpos, qseg, kpos, kseg)


def forward_piece(k, last, scal, q_t, kv, table, idx, state, tile):
    heads = table.shape[0]
    rows = kv.shape[0]
    nb = rows // tile
    head_cols = heads * HEAD_DIM
    column = lambda *shape: pl.BlockSpec(
        shape + (tile,), lambda i: (0,) * len(shape) + (i,)
    )
    in_specs = [
        pl.BlockSpec(memory_space=pltpu.SMEM),
        column(head_cols),
        pl.BlockSpec((rows, 2 * head_cols), lambda i: (0, 0)),
        pl.BlockSpec((heads, 8, 128), lambda i: (0, 0, 0)),
        pl.BlockSpec((1, rows, tile), lambda i: (k, 0, i)),
    ]
    args = [scal, q_t, kv, table, idx]
    if k > 0:
        in_specs += [column(heads, 1), column(heads, 1), column(heads, HEAD_DIM)]
        args += list(state)
    pairs = heads * rows * rows
    out_specs = [column(heads, rows), column(heads, 1), column(heads, 1), column(heads, HEAD_DIM)]
    out_shape = [
        jax.ShapeDtypeStruct((heads, rows, rows), BF16),
        jax.ShapeDtypeStruct((heads, 1, rows), F32),
        jax.ShapeDtypeStruct((heads, 1, rows), F32),
        jax.ShapeDtypeStruct((heads, HEAD_DIM, rows), F32),
    ]
    scratch_shapes = [
        pltpu.VMEM((rows, tile), F32),
        pltpu.VMEM((2 * head_cols, rows), BF16),
    ]
    if last:
        out_specs.append(pl.BlockSpec((tile, head_cols), lambda i: (i, 0)))
        out_shape.append(jax.ShapeDtypeStruct((rows, head_cols), BF16))
        scratch_shapes.append(pltpu.VMEM((head_cols, tile), BF16))
    return pl.pallas_call(
        functools.partial(forward_kernel, k == 0, last, nb, tile, heads),
        grid=(nb,),
        in_specs=in_specs,
        out_specs=out_specs,
        out_shape=out_shape,
        scratch_shapes=scratch_shapes,
        compiler_params=pltpu.CompilerParams(
            dimension_semantics=("arbitrary",), vmem_limit_bytes=VMEM_LIMIT
        ),
        cost_estimate=pl.CostEstimate(
            flops=pairs * 4 * 128, bytes_accessed=pairs * 4, transcendentals=pairs
        ),
    )(*args)


def backward_piece(k, scal, q_t, do_t, kv, probs, idx, factor, delta, dq, tile):
    heads = probs.shape[0]
    rows = kv.shape[0]
    nb = rows // tile
    start = dq is None
    own = k == 0
    head_cols = heads * HEAD_DIM
    column = lambda *shape: pl.BlockSpec(
        shape + (tile,), lambda i: (0,) * len(shape) + (i,)
    )
    in_specs = [
        pl.BlockSpec(memory_space=pltpu.SMEM),
        column(head_cols),
        column(head_cols),
        pl.BlockSpec((rows, 2 * head_cols), lambda i: (0, 0)),
        column(heads, rows),
        pl.BlockSpec((1, rows, tile), lambda i: (k, 0, i)),
        column(heads, 1),
        column(heads, 1),
    ]
    args = [scal, q_t, do_t, kv, probs, idx, factor, delta]
    if not start:
        in_specs += [column(heads, HEAD_DIM)]
        args += [dq]
    pairs = heads * rows * rows
    out_specs = [
        pl.BlockSpec((rows, 2 * head_cols), lambda i: (0, 0)),
        column(heads, HEAD_DIM),
        pl.BlockSpec((heads, NBUCKET + 8, 128), lambda i: (0, 0, 0)),
    ]
    out_shape = [
        jax.ShapeDtypeStruct((rows, 2 * head_cols), F32 if own else BF16),
        jax.ShapeDtypeStruct((heads, HEAD_DIM, rows), F32),
        jax.ShapeDtypeStruct((heads, NBUCKET + 8, 128), F32),
    ]
    scratch_shapes = [
        pltpu.VMEM((heads, rows, tile), F32),
        pltpu.VMEM((rows, tile), BF16),
        pltpu.VMEM((heads, NBUCKET, 8, tile), F32),
        pltpu.VMEM((2 * head_cols, rows), BF16),
    ]
    if own:
        out_specs.append(pl.BlockSpec((tile, head_cols), lambda i: (i, 0)))
        out_shape.append(jax.ShapeDtypeStruct((rows, head_cols), BF16))
        scratch_shapes.append(pltpu.VMEM((heads, 128, 128), F32))
    scratch_shapes.append(pltpu.VMEM((rows, 2 * head_cols), F32))
    if own:
        scratch_shapes.append(pltpu.VMEM((head_cols, tile), BF16))
    return pl.pallas_call(
        functools.partial(backward_kernel, start, own, nb, tile, heads),
        grid=(nb,),
        in_specs=in_specs,
        out_specs=out_specs,
        out_shape=out_shape,
        scratch_shapes=scratch_shapes,
        compiler_params=pltpu.CompilerParams(
            dimension_semantics=("arbitrary",), vmem_limit_bytes=VMEM_LIMIT
        ),
        cost_estimate=pl.CostEstimate(
            flops=pairs * 8 * 128, bytes_accessed=pairs * 4, transcendentals=0
        ),
    )(*args)


GELU_SCALE = 0.7978845608028654
GELU_CUBE = 0.044715


def expert_kernel(
    steps,
    blocks,
    rows_ref,
    grads_ref,
    gate_ref,
    signs_ref,
    router_ref,
    win_ref,
    wout_ref,
    hidden_ref,
    pre_ref,
    row_ref,
    slope_ref,
    acc_scr,
    gate_scr,
):
    step = pl.program_id(0)

    @pl.when(step == 0)
    def _():
        acc_scr[...] = jnp.zeros_like(acc_scr)
        gate_scr[...] = jnp.zeros_like(gate_scr)

    size = rows_ref.shape[0] // blocks
    pair = (((1,), (1,)), ((), ()))
    for block in range(blocks):
        here = slice(block * size, (block + 1) * size)
        pre = jnp.dot(rows_ref[here, :], win_ref[...], preferred_element_type=F32)
        raw = lax.dot_general(
            grads_ref[here, :], wout_ref[...], pair, preferred_element_type=F32
        )
        square = pre * pre
        turn = jnp.tanh(GELU_SCALE * pre * (1.0 + GELU_CUBE * square))
        half = 0.5 + 0.5 * turn
        hidden = (pre * half).astype(BF16)
        hidden_ref[here, :] = hidden
        gate_scr[here, :] += jnp.sum(raw * hidden.astype(F32), axis=1, keepdims=True)
        slope = half + (0.5 * GELU_SCALE) * pre * (1.0 - turn * turn) * (
            1.0 + (3.0 * GELU_CUBE) * square
        )
        pre_grad = (raw * gate_ref[here, :] * slope).astype(BF16)
        pre_ref[here, :] = pre_grad
        acc_scr[here, :] += lax.dot_general(
            pre_grad, win_ref[...], pair, preferred_element_type=F32
        )

    @pl.when(step == steps - 1)
    def _():
        gate = gate_ref[...]
        slope = gate * (1.0 - gate) * gate_scr[...]
        logit = slope * signs_ref[...]
        high = logit.astype(BF16)
        low = (logit - high.astype(F32)).astype(BF16)
        routed = lax.dot_general(high, router_ref[...], pair, preferred_element_type=F32)
        routed += lax.dot_general(low, router_ref[...], pair, preferred_element_type=F32)
        row_ref[...] = (acc_scr[...] + routed).astype(BF16)
        slope_ref[...] = slope


def expert_pass(rows, grads, gate, signs, router, w_in, w_out):
    count, width = rows.shape
    units = w_in.shape[1]
    experts = router.shape[1]
    tile = 512 if units % 512 == 0 else units
    steps = units // tile
    blocks = 3 if count % 48 == 0 else 1
    whole = lambda *shape: pl.BlockSpec(shape, lambda f: (0,) * len(shape))
    return pl.pallas_call(
        functools.partial(expert_kernel, steps, blocks),
        grid=(steps,),
        in_specs=[
            whole(count, width),
            whole(count, width),
            whole(count, 1),
            whole(count, experts),
            whole(width, experts),
            pl.BlockSpec((width, tile), lambda f: (0, f)),
            pl.BlockSpec((tile, width), lambda f: (f, 0)),
        ],
        out_specs=[
            pl.BlockSpec((count, tile), lambda f: (0, f)),
            pl.BlockSpec((count, tile), lambda f: (0, f)),
            whole(count, width),
            whole(count, 1),
        ],
        out_shape=[
            jax.ShapeDtypeStruct((count, units), BF16),
            jax.ShapeDtypeStruct((count, units), BF16),
            jax.ShapeDtypeStruct((count, width), BF16),
            jax.ShapeDtypeStruct((count, 1), F32),
        ],
        scratch_shapes=[pltpu.VMEM((count, width), F32), pltpu.VMEM((count, 1), F32)],
        compiler_params=pltpu.CompilerParams(
            dimension_semantics=("arbitrary",), vmem_limit_bytes=VMEM_LIMIT
        ),
        cost_estimate=pl.CostEstimate(
            flops=6 * count * width * units,
            bytes_accessed=4 * width * units + 4 * count * units + 6 * count * width,
            transcendentals=count * units,
        ),
    )(rows, grads, gate, signs, router, w_in, w_out)


def shards(
    block_input,
    w_qkv,
    w_attn_out,
    w_router,
    gain_attn,
    gain_moe,
    rel_bias,
    w_in,
    w_out,
    routes,
    segment_ids,
    bucket_table,
    out_grad,
):
    tok_rows, width = block_input.shape
    planes = lax.axis_size("pl")
    group = lax.axis_size("fx") * lax.axis_size("wsh")
    devices = planes * group
    cores = lax.axis_size("grp")
    plane_rank = lax.axis_index("pl")
    place = lax.axis_index(PLANE)
    device_rank = plane_rank * group + place
    core_rank = lax.axis_index("grp")
    heads = HEADS // group
    head_cols = heads * HEAD_DIM
    rows = tok_rows * group
    w_rows = w_qkv.shape[1]
    expert_count = w_router.shape[1]
    bias_share = rel_bias.shape[0]

    split = cores if w_rows % cores == 0 else 1
    part_rows = w_rows // split

    def own_part(array, axis):
        if split == 1:
            return array
        return lax.dynamic_slice_in_dim(array, core_rank * part_rows, part_rows, axis)

    def join_parts(array):
        if split > 1:
            both = lax.all_gather(array, "grp", axis=0, tiled=False)
            array = jnp.transpose(both, (1, 0, 2, 3))
        return array.reshape(devices * w_rows, array.shape[-1])

    def exchange(array, axes=ALL):
        return lax.all_to_all(array, axes, split_axis=0, concat_axis=0, tiled=True)

    def plane_send(block_of):
        came = [block_of(0)]
        for j in range(1, group):
            onward = [(i, (i + j) % group) for i in range(group)]
            came.append(lax.ppermute(block_of(j), PLANE, onward))
        return [came[-i % group] for i in range(group)]

    def in_place_order(blocks):
        size = blocks[0].shape[0]
        twice = jnp.concatenate(blocks + blocks[:-1], axis=0)
        return lax.dynamic_slice_in_dim(twice, (-place % group) * size, size * group, 0)

    capacity = max(2, 4 * tok_rows // expert_count)
    expert_ids = jnp.arange(expert_count, dtype=I32)
    route_hits = routes[:, :, None] == expert_ids[None, None, :]
    flat_hits = route_hits.reshape(tok_rows * 2, expert_count)
    order = jnp.arange(tok_rows * 2, dtype=I32)
    earlier = (order[:, None] > order[None, :]).astype(BF16)
    ranks = jnp.dot(earlier, flat_hits.astype(BF16), preferred_element_type=F32)
    slot_ranks = jnp.sum(jnp.where(flat_hits, ranks, 0.0), axis=1).astype(I32)
    slot_ids = routes * capacity + slot_ranks.reshape(tok_rows, 2)
    slot_count = expert_count * capacity
    slot_numbers = jnp.arange(slot_count, dtype=I32)
    hit_first = slot_numbers[:, None] == slot_ids[None, :, 0]
    hit_second = slot_numbers[:, None] == slot_ids[None, :, 1]
    table_first = hit_first.astype(BF16)
    table_second = hit_second.astype(BF16)
    slot_table = table_first + table_second
    other_expert = jnp.sum(
        jnp.where(hit_first, routes[None, :, 1], 0) + jnp.where(hit_second, routes[None, :, 0], 0),
        axis=1,
    )

    plane_input = in_place_order(plane_send(lambda j: block_input))

    def join_small(rows_of, small_of):
        count, height = rows_of.shape[:2]
        spare = -(-small_of.shape[1] // height)
        small_of = jnp.pad(small_of, ((0, 0), (0, spare * height - small_of.shape[1])))
        return jnp.concatenate([rows_of, small_of.reshape(count, height, spare)], axis=2)

    qkv_part = own_part(w_qkv, 1)
    q_part = qkv_part[0].reshape(part_rows, group, head_cols)
    kv_part = qkv_part[1:].reshape(2, part_rows, group, heads, HEAD_DIM)
    kv_part = jnp.transpose(kv_part, (1, 2, 3, 0, 4)).reshape(part_rows, group, 2 * head_cols)
    qkv_pay = jnp.transpose(jnp.concatenate([q_part, kv_part], axis=2), (1, 0, 2))
    small = jnp.concatenate([w_router.reshape(-1), gain_attn, gain_moe, rel_bias])
    pay_cols = 3 * head_cols
    small_count = small.shape[0]
    small = jnp.concatenate(
        [
            jnp.broadcast_to(small[None], (devices, small_count)),
            other_expert.astype(BF16).reshape(devices, capacity),
        ],
        axis=1,
    )
    qkv_pay = jnp.broadcast_to(qkv_pay[None], (planes,) + qkv_pay.shape)
    qkv_pay = qkv_pay.reshape(devices, part_rows, pay_cols)
    out_pay = jnp.broadcast_to(own_part(w_attn_out, 0)[None], (devices, part_rows, width))
    qkv_pay = join_small(jnp.concatenate([qkv_pay, out_pay], axis=2), small)
    qkv_got = lax.all_to_all(qkv_pay, ALL, split_axis=0, concat_axis=0, tiled=True)
    positions = positions_of(segment_ids)
    bucket_ids = jnp.arange(NBUCKET, dtype=I32)
    edges = jnp.sum((bucket_table[None, :] < bucket_ids[:, None]).astype(I32), axis=1)
    tile = 256 if rows % 256 == 0 else rows
    nb = rows // tile

    def ranges_of(plane):
        first = jnp.maximum(plane, 0) * rows
        pos = lax.dynamic_slice_in_dim(positions, first, rows)
        seg = lax.dynamic_slice_in_dim(segment_ids, first, rows)
        pos_t, seg_t = pos.reshape(nb, tile), seg.reshape(nb, tile)
        limits = (
            jnp.min(pos_t, axis=1),
            jnp.max(pos_t, axis=1),
            jnp.min(seg_t, axis=1),
            jnp.max(seg_t, axis=1),
        )
        return first, pos, seg, limits

    q_first, q_pos, q_seg, (q_pos_min, q_pos_max, q_seg_min, q_seg_max) = ranges_of(plane_rank)
    tile_ids = jnp.arange(nb, dtype=I32)

    def bucket_of(distance):
        return jnp.sum((distance[:, :, None] >= edges[None, None, 1:]).astype(I32), axis=2)

    scal_of, key_info = [], []
    for k in range(planes):
        plane = plane_rank - k
        k_first, k_pos, k_seg, (k_pos_min, k_pos_max, k_seg_min, k_seg_max) = ranges_of(plane)
        causal = (k_first + tile_ids * tile)[:, None] <= (q_first + tile_ids * tile + tile - 1)[
            None, :
        ]
        own = jnp.logical_or(
            (k_seg_min == 0)[:, None],
            jnp.logical_and(
                k_seg_min[:, None] <= q_seg_max[None, :], k_seg_max[:, None] >= q_seg_min[None, :]
            ),
        )
        flags = jnp.logical_and(jnp.logical_and(causal, own), plane >= 0).astype(I32)
        least = bucket_of(jnp.maximum(q_pos_min[None, :] - k_pos_max[:, None], 0))
        most = bucket_of(jnp.maximum(q_pos_max[None, :] - k_pos_min[:, None], 0))
        beyond = jnp.logical_and(k == 0, tile_ids[:, None] > tile_ids[None, :])
        full = jnp.min(jnp.where(beyond, 1, flags), axis=0)
        scal_of.append(
            jnp.concatenate(
                [
                    flags.reshape(-1),
                    least.reshape(-1),
                    most.reshape(-1),
                    full,
                    edges,
                    jnp.full((EDGE_GROUP,), 1 << 30, I32),
                    jnp.stack([q_first, k_first]).astype(I32),
                ]
            )
        )
        key_info.append((k_pos, k_seg))
    plane_inverse = norm_inverse(plane_input.astype(F32))
    scal_all, plane_input, plane_inverse = lax.optimization_barrier(
        (jnp.stack(scal_of), plane_input, plane_inverse)
    )
    plane_wide = plane_input.astype(F32)
    bucket_idx = buckets_of(
        scal_all,
        q_pos[None, :],
        q_seg[None, :],
        jnp.broadcast_to(
            jnp.stack([info[0] for info in key_info])[:, :, None], (planes, rows, 128)
        ),
        jnp.broadcast_to(
            jnp.stack([info[1] for info in key_info])[:, :, None], (planes, rows, 128)
        ),
        tile,
    )

    qkv_got, bucket_idx = lax.optimization_barrier((qkv_got, bucket_idx))
    w_heads = join_parts(qkv_got[:, :, :pay_cols])
    half_cols = pay_cols + width // 2
    gathered_out = jnp.concatenate(
        [
            join_parts(qkv_got[:, :, pay_cols:half_cols]),
            join_parts(qkv_got[:, :, half_cols : pay_cols + width]),
        ],
        axis=1,
    )
    small_got = qkv_got[:, :, pay_cols + width :].reshape(devices, -1)
    router_size = w_rows * expert_count
    full_router = small_got[:, :router_size].reshape(width, expert_count)
    at = router_size
    gain_attn_full = small_got[:, at : at + w_rows].reshape(width).astype(F32)
    at += w_rows
    gain_moe_full = small_got[:, at : at + w_rows].reshape(width).astype(F32)
    at += w_rows
    bias_full = small_got[:, at : at + bias_share].reshape(HEADS, NBUCKET).astype(F32)
    at += bias_share
    other_arrived = small_got[:, at : at + capacity].reshape(slot_count).astype(F32)
    w_query = w_heads[:, :head_cols]
    w_keyval = w_heads[:, head_cols:]

    attn_in = (plane_wide * plane_inverse * gain_attn_full).astype(BF16)
    q_t = lax.dot_general(
        w_query, attn_in, (((0,), (1,)), ((), ())), preferred_element_type=F32
    ).astype(BF16)
    keyval = jnp.dot(attn_in, w_keyval, preferred_element_type=F32).astype(BF16)
    bias_local = lax.dynamic_slice_in_dim(bias_full, place * heads, heads, 0) * LOG2E
    bias_table = jnp.concatenate(
        [bias_local, jnp.full((heads, 128 - NBUCKET), NEGATIVE, F32)], axis=1
    )
    bias_table = jnp.broadcast_to(bias_table[:, None, :], (heads, 8, 128))

    upward = [(i, i + 1) for i in range(planes - 1)]
    downward = [(i + 1, i) for i in range(planes - 1)]
    grad_send = jnp.dot(slot_table, out_grad, preferred_element_type=F32).astype(BF16)
    kv_pieces, probs, tops, state = [keyval], [], [], None
    travelling = lax.ppermute(keyval, "pl", upward) if planes > 1 else None
    for k in range(planes):
        made = forward_piece(
            k,
            k == planes - 1,
            scal_of[k],
            q_t,
            kv_pieces[k],
            bias_table,
            bucket_idx,
            state,
            tile,
        )
        probs.append(made[0])
        state = made[1:4]
        tops.append(made[1])
        if k == planes - 1:
            break
        if k == planes - 2:
            travelling, state, grad_send, gathered_out = lax.optimization_barrier(
                (travelling, state, grad_send, gathered_out)
            )
        else:
            travelling, state = lax.optimization_barrier((travelling, state))
        kv_pieces.append(travelling)
        if k + 2 < planes:
            travelling = lax.ppermute(travelling, "pl", upward)
    grad_raw = exchange(grad_send.reshape(expert_count, capacity, width)).reshape(
        slot_count, width
    )
    final_top, final_sum, out_sum = state
    mixed_own = made[4].reshape(group, tok_rows, head_cols)
    mixed = jnp.concatenate(
        plane_send(lambda j: lax.dynamic_index_in_dim(mixed_own, (place + j) % group, 0, False)),
        axis=1,
    )
    turned_out = lax.dynamic_slice_in_dim(
        jnp.concatenate([gathered_out, gathered_out], axis=0), place * head_cols, width, 0
    )

    input_wide = block_input.astype(F32)
    residual = input_wide + jnp.dot(mixed, turned_out, preferred_element_type=F32)
    inverse_moe = norm_inverse(residual)
    moe_in = (residual * inverse_moe * gain_moe_full).astype(BF16)
    outgoing = jnp.dot(slot_table, moe_in, preferred_element_type=F32).astype(BF16)
    outgoing, grad_raw = lax.optimization_barrier((outgoing, grad_raw))
    arrived = lax.all_to_all(
        outgoing.reshape(expert_count, capacity, width), ALL, split_axis=0, concat_axis=0, tiled=True
    ).reshape(slot_count, width)
    logits = jnp.dot(moe_in, full_router, preferred_element_type=F32)
    chosen = jnp.sum(jnp.where(route_hits, logits[:, None, :], 0.0), axis=2)
    gate_probs = jax.nn.softmax(chosen, axis=1)

    expert_in = w_in[0]
    expert_out = w_out[0]
    row_logits = jnp.dot(arrived, full_router, preferred_element_type=F32)
    own_logit = jnp.sum(jnp.where(expert_ids[None, :] == device_rank, row_logits, 0.0), axis=1)
    other_logit = jnp.sum(
        jnp.where(expert_ids[None, :].astype(F32) == other_arrived[:, None], row_logits, 0.0), axis=1
    )
    top_logit = jnp.maximum(own_logit, other_logit)
    own_part_exp = jnp.exp(own_logit - top_logit)
    row_gate = own_part_exp / (own_part_exp + jnp.exp(other_logit - top_logit))
    grad_wide = grad_raw.astype(F32)
    made_grad = (row_gate[:, None] * grad_wide).astype(BF16)

    signs = (expert_ids[None, :] == device_rank).astype(F32) - (
        expert_ids[None, :].astype(F32) == other_arrived[:, None]
    ).astype(F32)
    hidden, pre_grad, row_grad, row_slope = expert_pass(
        arrived, grad_raw, row_gate[:, None], signs, full_router, expert_in, expert_out
    )
    row_logit_grad = row_slope * signs
    logit_high = row_logit_grad.astype(BF16)
    logit_low = (row_logit_grad - logit_high.astype(F32)).astype(BF16)
    row_logit_grad = jnp.concatenate([logit_high, logit_low], axis=1)
    returned_grads = lax.all_to_all(
        row_grad.reshape(expert_count, capacity, width),
        ALL,
        split_axis=0,
        concat_axis=0,
        tiled=True,
    ).reshape(slot_count, width)
    hidden_late, made_late, row_grad = lax.optimization_barrier((hidden, made_grad, row_grad))
    expert_made = jnp.dot(hidden_late, expert_out, preferred_element_type=F32).astype(BF16)
    w_out_grad = lax.dot_general(
        hidden_late, made_late, (((0,), (0,)), ((), ())), preferred_element_type=F32
    )[None]
    router_pair = lax.dot_general(
        arrived, row_logit_grad, (((0,), (0,)), ((), ())), preferred_element_type=F32
    )
    router_grad = router_pair[:, :expert_count] + router_pair[:, expert_count:]
    returned_grads, expert_made, w_out_grad = lax.optimization_barrier(
        (returned_grads, expert_made, w_out_grad)
    )
    returned = exchange(expert_made.reshape(expert_count, capacity, width)).reshape(
        slot_count, width
    )

    moe_in_grad = lax.dot_general(
        slot_table, returned_grads, (((0,), (0,)), ((), ())), preferred_element_type=F32
    )
    grad_out = out_grad.astype(F32)
    residual_grad = grad_out + norm_input_grad(residual, inverse_moe, gain_moe_full, moe_in_grad)
    branch_grad = residual_grad.astype(BF16)
    mixed_grad = lax.dot_general(
        branch_grad, turned_out, (((1,), (1,)), ((), ())), preferred_element_type=F32
    ).astype(BF16)
    grad_t = in_place_order(
        plane_send(lambda j: mixed_grad[:, j * head_cols : (j + 1) * head_cols])
    ).T

    head_out_t = out_sum / final_sum
    delta = jnp.sum(
        grad_t.astype(F32).reshape(heads, HEAD_DIM, rows) * head_out_t, axis=1, keepdims=True
    )
    query_grad, carried, bias_parts = None, None, []
    for k in reversed(range(planes)):
        factor = jnp.exp2(tops[k] - final_top) / final_sum
        dkv, query_grad, bias_part, *query_rows = backward_piece(
            k,
            scal_of[k],
            q_t,
            grad_t,
            kv_pieces[k],
            probs[k],
            bucket_idx,
            factor,
            delta,
            query_grad,
            tile,
        )
        bias_parts.append(bias_part)
        if carried is None:
            total = dkv
        else:
            carried, dkv, query_grad, query_rows = lax.optimization_barrier(
                (carried, dkv, query_grad, query_rows)
            )
            total = dkv.astype(F32) + carried.astype(F32)
        if k == 0:
            break
        sent = total.astype(BF16)
        if k == planes - 1:
            sent, query_grad, returned, branch_late = lax.optimization_barrier(
                (sent, query_grad, returned, branch_grad)
            )
        carried = lax.ppermute(sent, "pl", downward)
        if k == planes - 1:
            attn_out_part = lax.dot_general(
                mixed, branch_late, (((0,), (0,)), ((), ())), preferred_element_type=F32
            )
            attn_out_part = lax.dynamic_slice_in_dim(
                jnp.concatenate([attn_out_part, attn_out_part], axis=0),
                width - place * head_cols,
                width,
                0,
            )
            attn_out_part = attn_out_part.astype(BF16).reshape(planes, group, w_rows, width)
            attn_out_part = sum(
                block.astype(F32)
                for block in plane_send(
                    lambda j: lax.dynamic_index_in_dim(
                        attn_out_part, (place + j) % group, 1, False
                    )
                )
            ).astype(BF16)
            gain_moe_grad = jnp.sum(moe_in_grad * residual * inverse_moe, axis=0)
    scale_row = jnp.tile(
        jnp.concatenate([jnp.full((HEAD_DIM,), 0.125, F32), jnp.ones((HEAD_DIM,), F32)]), heads
    )
    keyval_grad = (total * scale_row[None, :]).astype(BF16)
    query_grad = query_rows[0]
    bias_rows_at = -(-bias_share // w_rows)
    bias_rows = sum(bias_parts)
    band_rows = jnp.roll(jnp.sum(bias_rows[:, NBUCKET:], axis=1), 1, axis=1)[:, :BAND]
    bias_grad = jnp.sum(bias_rows[:, :NBUCKET], axis=2) + jnp.pad(
        band_rows, ((0, 0), (0, NBUCKET - BAND))
    )

    w_query_part = lax.dot_general(
        attn_in, query_grad, (((0,), (0,)), ((), ())), preferred_element_type=F32
    )
    w_keyval_part = lax.dot_general(
        attn_in, keyval_grad, (((0,), (0,)), ((), ())), preferred_element_type=F32
    )
    gain_attn_grad = (
        jnp.sum(w_query_part * w_query.astype(F32), axis=1, keepdims=True)
        + jnp.sum(w_keyval_part * w_keyval.astype(F32), axis=1, keepdims=True)
    ) / gain_attn_full[:, None]
    bias_all = lax.dynamic_update_slice_in_dim(
        jnp.zeros((HEADS, NBUCKET), F32), bias_grad, place * heads, 0
    ).reshape(devices, bias_share)
    bias_all = jnp.pad(bias_all, ((0, 0), (0, bias_rows_at * w_rows - bias_share)))
    bias_all = jnp.transpose(bias_all.reshape(devices, bias_rows_at, w_rows), (0, 2, 1))
    small_grads = jnp.concatenate(
        [
            router_grad,
            gain_moe_grad[:, None],
            gain_attn_grad,
            bias_all.reshape(width, bias_rows_at),
        ],
        axis=1,
    )
    small_high = small_grads.astype(BF16)
    small_low = (small_grads - small_high.astype(F32)).astype(BF16)
    w_parts = jnp.concatenate(
        [w_query_part.astype(BF16), w_keyval_part.astype(BF16), small_high, small_low], axis=1
    ).reshape(devices, w_rows, -1)
    w_parts, query_grad, keyval_grad = lax.optimization_barrier(
        (w_parts, query_grad, keyval_grad)
    )
    w_got = exchange(w_parts)

    attn_in_grad = lax.dot_general(
        query_grad, w_query, (((1,), (1,)), ((), ())), preferred_element_type=F32
    ) + lax.dot_general(
        keyval_grad, w_keyval, (((1,), (1,)), ((), ())), preferred_element_type=F32
    )
    attn_in_grad = attn_in_grad.reshape(group, tok_rows, width)
    pre_late, attn_out_part, w_parts = lax.optimization_barrier(
        (pre_grad, attn_out_part, w_parts)
    )
    attn_out_came = [lax.dynamic_index_in_dim(attn_out_part, plane_rank, 0, False)]
    for j in range(1, planes):
        onward = [(i, (i + j) % planes) for i in range(planes)]
        block = lax.dynamic_index_in_dim(attn_out_part, (plane_rank + j) % planes, 0, False)
        attn_out_came.append(lax.ppermute(block, "pl", onward))
    w_in_grad = lax.dot_general(
        arrived, pre_late, (((0,), (0,)), ((), ())), preferred_element_type=F32
    )[None]
    attn_in_grad, w_in_grad = lax.optimization_barrier((attn_in_grad, w_in_grad))
    came = plane_send(
        lambda j: lax.dynamic_index_in_dim(attn_in_grad, (place + j) % group, 0, False).astype(BF16)
    )
    attn_in_grad = sum(block.astype(F32) for block in came)
    attn_out_grad = sum(block.astype(F32) for block in attn_out_came)
    inverse_attn = norm_inverse(input_wide)
    input_grad = residual_grad + norm_input_grad(
        input_wide, inverse_attn, gain_attn_full, attn_in_grad
    )


    picked_first = lax.dot_general(
        table_first, returned, (((0,), (0,)), ((), ())), preferred_element_type=F32
    )
    picked_second = lax.dot_general(
        table_second, returned, (((0,), (0,)), ((), ())), preferred_element_type=F32
    )
    block_output = (
        residual + (gate_probs[:, 0:1] * picked_first + gate_probs[:, 1:2] * picked_second)
    ).astype(BF16)
    w_got, w_in_grad, block_output = lax.optimization_barrier((w_got, w_in_grad, block_output))

    w_wide = w_got.astype(F32)
    w_sum = jnp.sum(w_wide[:, :, :pay_cols].reshape(planes, group, w_rows, pay_cols), axis=0)
    q_sum = jnp.transpose(w_sum[:, :, :head_cols], (1, 0, 2)).reshape(1, w_rows, width)
    kv_sum = w_sum[:, :, head_cols:].reshape(group, w_rows, heads, 2, HEAD_DIM)
    kv_sum = jnp.transpose(kv_sum, (3, 1, 0, 2, 4)).reshape(2, w_rows, width)
    qkv_grad = jnp.concatenate([q_sum, kv_sum], axis=0)
    small_sum = jnp.sum(w_wide[:, :, pay_cols:], axis=0)
    columns = expert_count + 2 + bias_rows_at
    small_sum = small_sum[:, :columns] + small_sum[:, columns:]
    bias_sum = jnp.transpose(small_sum[:, expert_count + 2 :]).reshape(-1)[:bias_share]
    return (
        block_output,
        input_grad,
        qkv_grad,
        attn_out_grad,
        small_sum[:, :expert_count],
        small_sum[:, expert_count + 1],
        small_sum[:, expert_count],
        bias_sum,
        w_in_grad,
        w_out_grad,
    )


def solution(mesh):
    devices = mesh.devices
    grp, seq, wsh = devices.shape
    inner = Mesh(devices.reshape(grp, seq // 2, 2, wsh), ("grp",) + ALL)
    every = ("grp",) + ALL
    in_specs = (
        P(every, None),
        P(None, ALL, None),
        P(ALL, None),
        P(ALL, None),
        P(ALL),
        P(ALL),
        P(ALL),
        P(ALL, None, None),
        P(ALL, None, None),
        P(every, None),
        P("grp"),
        P(),
        P(every, None),
    )
    out_specs = (
        P(every, None),
        P(every, None),
        P("grp", ALL, None),
        P(every, None),
        P(every, None),
        P(every),
        P(every),
        P(every),
        P(every, None, None),
        P(every, None, None),
    )
    return jax.shard_map(
        shards, mesh=inner, in_specs=in_specs, out_specs=out_specs, check_vma=False
    )
```

```python
import functools
import math

import jax
import jax.numpy as jnp
from jax import lax
from jax.experimental import pallas as pl
from jax.experimental.pallas import tpu as pltpu
from jax.sharding import Mesh
from jax.sharding import PartitionSpec as P

HEADS = 12
HEAD_DIM = 64
NBUCKET = 32

EPSILON = 1e-06
NEGATIVE = -1e30
LOG2E = 1.4426950408889634
SCALE2 = 0.125 * LOG2E

PLANE = ("fx", "wsh")
ALL = ("pl", "fx", "wsh")
F32 = jnp.float32
BF16 = jnp.bfloat16
I32 = jnp.int32


def positions_of(segment_ids):
    total_rows = segment_ids.shape[0]
    numbers = jnp.arange(total_rows, dtype=jnp.int32)
    fresh_start = jnp.logical_or(numbers == 0, segment_ids != jnp.roll(segment_ids, 1))
    begins = lax.cummax(jnp.where(fresh_start, numbers, 0), axis=0)
    return jnp.where(segment_ids == 0, numbers, numbers - begins + total_rows // 2)


def norm_inverse(values):
    return lax.rsqrt(jnp.mean(values * values, axis=-1, keepdims=True) + EPSILON)


def norm_input_grad(values, inverse, gain_vec, grad_in):
    scaled = grad_in * gain_vec
    inner_mean = jnp.mean(scaled * values, axis=-1, keepdims=True)
    return inverse * scaled - values * inverse * inverse * inverse * inner_mean


BAND = 16
EDGE_GROUP = 4
EDGES = NBUCKET + EDGE_GROUP
VMEM_LIMIT = 60 << 20


def bucket_kernel(nb, tile, scal, qpos, qseg, kpos, kseg, idx_ref):
    piece = pl.program_id(0)
    n2 = nb * nb
    at = 3 * n2 + nb
    step = 128 if tile % 128 == 0 else tile
    q_first = scal[piece, at + EDGES]
    k_first = scal[piece, at + EDGES + 1]
    for jb in range(nb):
        for ib in range(nb):
            t = jb * nb + ib

            @pl.when(scal[piece, t] > 0)
            def _(jb=jb, ib=ib, t=t):
                low_bucket = scal[piece, n2 + t]
                high_bucket = scal[piece, 2 * n2 + t]
                cols = slice(ib * tile, (ib + 1) * tile)
                for r in range(tile // step):
                    rows = slice(jb * tile + r * step, jb * tile + (r + 1) * step)
                    key_pos = jnp.concatenate([kpos[0, rows, :]] * (tile // 128), axis=1)
                    key_seg = jnp.concatenate([kseg[0, rows, :]] * (tile // 128), axis=1)
                    distance = qpos[0:1, cols] - key_pos

                    def more(trip, count, distance=distance):
                        start = low_bucket + 1 + trip * EDGE_GROUP
                        for b in range(EDGE_GROUP):
                            count = count + jnp.where(distance >= scal[piece, at + start + b], 1, 0)
                        return count

                    count = more(0, jnp.full((step, tile), low_bucket, I32))
                    trips = lax.div(high_bucket - low_bucket + EDGE_GROUP - 1, EDGE_GROUP)
                    count = lax.fori_loop(1, trips, more, count)
                    key_row = lax.broadcasted_iota(I32, (step, tile), 0) + (k_first + rows.start)
                    query_row = lax.broadcasted_iota(I32, (step, tile), 1) + (q_first + cols.start)
                    own = jnp.logical_or(key_seg == 0, key_seg == qseg[0:1, cols])
                    seen = jnp.logical_and(key_row <= query_row, own)
                    idx_ref[0, rows, cols] = jnp.where(seen, count, NBUCKET)


def forward_kernel(first, last, nb, tile, heads, *refs):
    if first:
        (scal, q_ref, kv_ref, tbl_ref, idx_ref) = refs[:5]
        refs = refs[5:]
    else:
        (scal, q_ref, kv_ref, tbl_ref, idx_ref, m_in, l_in, o_in) = refs[:8]
        refs = refs[8:]
    if last:
        (p_ref, m_ref, l_ref, o_ref, mixed_ref, s_scr, kvt_scr, mixed_scr) = refs
    else:
        (p_ref, m_ref, l_ref, o_ref, s_scr, kvt_scr) = refs
    ib = pl.program_id(0)
    n2 = nb * nb
    full = scal[3 * n2 + ib] > 0
    wide = 2 * HEAD_DIM

    @pl.when(ib == 0)
    def _():
        kvt_scr[...] = kv_ref[...].T

    def one_head(head, carry):
        lanes_of = pl.ds(pl.multiple_of(head * wide, wide), wide)
        value_rows = pl.ds(pl.multiple_of(head * wide + HEAD_DIM, HEAD_DIM), HEAD_DIM)
        query = q_ref[pl.ds(pl.multiple_of(head * HEAD_DIM, HEAD_DIM), HEAD_DIM), :]
        query = jnp.concatenate([query, jnp.zeros_like(query)], axis=0)
        table = jnp.broadcast_to(tbl_ref[head, 0:1, :], (tile, 128))
        if first:
            m_old = jnp.full((1, tile), -3e38, F32)
            l_old = jnp.zeros((1, tile), F32)
            o_old = jnp.zeros((HEAD_DIM, tile), F32)
        else:
            m_old = m_in[head]
            l_old = l_in[head]
            o_old = o_in[head]

        def scores_of(rows):
            raw = jnp.dot(kv_ref[rows, lanes_of], query, preferred_element_type=F32)
            tops = []
            for c in range(tile // 128):
                lanes = slice(c * 128, (c + 1) * 128)
                score = raw[:, lanes] * SCALE2 + jnp.take_along_axis(
                    table, idx_ref[0, rows, lanes], axis=1
                )
                s_scr[rows, lanes] = score
                tops.append(jnp.max(score, axis=0, keepdims=True))
            return jnp.concatenate(tops, axis=1)

        def dense(blocks):
            m_new = m_old
            for jb in range(blocks):
                m_new = jnp.maximum(m_new, scores_of(slice(jb * tile, (jb + 1) * tile)))
            factor = jnp.exp2(m_old - m_new)
            total = l_old * factor
            for jb in range(blocks):
                rows = slice(jb * tile, (jb + 1) * tile)
                weight = jnp.exp2(s_scr[rows, :] - m_new)
                total = total + jnp.sum(weight, axis=0, keepdims=True)
                p_ref[head, rows, :] = weight.astype(BF16)
            made = jnp.dot(
                kvt_scr[value_rows, : blocks * tile],
                p_ref[head, : blocks * tile, :],
                preferred_element_type=F32,
            )
            m_ref[head] = m_new
            l_ref[head] = total
            o_ref[head] = o_old * factor + made

        if first:
            for blocks in range(1, nb + 1):

                @pl.when(jnp.logical_and(full, ib == blocks - 1))
                def _(blocks=blocks):
                    dense(blocks)

        else:

            @pl.when(full)
            def _():
                dense(nb)

        @pl.when(jnp.logical_not(full))
        def _():
            m_ref[head] = m_old
            for jb in range(nb):

                @pl.when(scal[jb * nb + ib] > 0)
                def _(jb=jb):
                    m_ref[head] = jnp.maximum(
                        m_ref[head], scores_of(slice(jb * tile, (jb + 1) * tile))
                    )

            m_new = m_ref[head]
            factor = jnp.exp2(m_old - m_new)
            l_ref[head] = l_old * factor
            o_ref[head] = o_old * factor
            for jb in range(nb):

                @pl.when(scal[jb * nb + ib] > 0)
                def _(jb=jb):
                    rows = slice(jb * tile, (jb + 1) * tile)
                    weight = jnp.exp2(s_scr[rows, :] - m_new)
                    l_ref[head] += jnp.sum(weight, axis=0, keepdims=True)
                    weight_low = weight.astype(BF16)
                    p_ref[head, rows, :] = weight_low
                    o_ref[head] += jnp.dot(
                        kvt_scr[value_rows, rows], weight_low, preferred_element_type=F32
                    )

        if last:
            at = pl.multiple_of(head * HEAD_DIM, HEAD_DIM)
            mixed_scr[pl.ds(at, HEAD_DIM), :] = (o_ref[head] / l_ref[head]).astype(BF16)
        return carry

    lax.fori_loop(0, heads, one_head, 0)
    if last:
        mixed_ref[...] = mixed_scr[...].T


def backward_kernel(start, own, nb, tile, heads, *refs):
    (scal, q_ref, do_ref, kv_ref, p_ref, idx_ref, f_ref, delta_ref) = refs[:8]
    refs = refs[8:]
    if not start:
        dq_in, refs = refs[0], refs[1:]
    if own:
        (dkv_out, dq_ref, bias_ref, qg_ref) = refs[:4]
        (ds_scr, low_scr, acc_scr, kvt_scr, band_scr, dkv_scr, qg_scr) = refs[4:]
    else:
        (dkv_out, dq_ref, bias_ref) = refs[:3]
        (ds_scr, low_scr, acc_scr, kvt_scr, dkv_scr) = refs[3:]
    ib = pl.program_id(0)
    n2 = nb * nb
    full = scal[3 * n2 + ib] > 0
    wide = 2 * HEAD_DIM
    pair = (((1,), (1,)), ((), ()))

    @pl.when(ib == 0)
    def _():
        kvt_scr[...] = kv_ref[...].T
        acc_scr[...] = jnp.zeros_like(acc_scr)
        dkv_scr[...] = jnp.zeros_like(dkv_scr)
        if own:
            band_scr[...] = jnp.zeros_like(band_scr)

    def one_head(head, carry):
        lanes_of = pl.ds(pl.multiple_of(head * wide, wide), wide)
        key_rows = pl.ds(pl.multiple_of(head * wide, wide), HEAD_DIM)
        head_rows = pl.ds(pl.multiple_of(head * HEAD_DIM, HEAD_DIM), HEAD_DIM)
        query = q_ref[head_rows, :]
        query = jnp.concatenate([query, jnp.zeros_like(query)], axis=0)
        out_grad = do_ref[head_rows, :]
        zeros = jnp.zeros_like(out_grad)
        grad_pad = jnp.concatenate([zeros, out_grad], axis=0)
        factor = f_ref[head]
        scaled = (out_grad.astype(F32) * factor).astype(BF16)
        scaled_pad = jnp.concatenate([zeros, scaled], axis=0)
        delta = delta_ref[head]
        dq_old = jnp.zeros((HEAD_DIM, tile), F32) if start else dq_in[head]

        def grads_of(rows):
            weight_grad = jnp.dot(kv_ref[rows, lanes_of], grad_pad, preferred_element_type=F32)
            score_grad = (p_ref[head, rows, :].astype(F32) * factor) * (weight_grad - delta)
            ds_scr[head, rows, :] = score_grad
            low_scr[rows, :] = score_grad.astype(BF16)

        def products_of(rows):
            dkv_scr[rows, lanes_of] += lax.dot_general(
                p_ref[head, rows, :], scaled_pad, pair, preferred_element_type=F32
            ) + lax.dot_general(low_scr[rows, :], query, pair, preferred_element_type=F32)
            return jnp.dot(kvt_scr[key_rows, rows], low_scr[rows, :], preferred_element_type=F32)

        def dense(blocks):
            for jb in range(blocks):
                grads_of(slice(jb * tile, (jb + 1) * tile))
            dq_ref[head] = dq_old + products_of(slice(0, blocks * tile))

        if own:
            for blocks in range(1, nb + 1):

                @pl.when(jnp.logical_and(full, ib == blocks - 1))
                def _(blocks=blocks):
                    dense(blocks)

        else:

            @pl.when(full)
            def _():
                dense(nb)

        @pl.when(jnp.logical_not(full))
        def _():
            dq_ref[head] = dq_old
            for jb in range(nb):

                @pl.when(scal[jb * nb + ib] > 0)
                def _(jb=jb):
                    rows = slice(jb * tile, (jb + 1) * tile)
                    grads_of(rows)
                    dq_ref[head] += products_of(rows)

        if own:
            qg_scr[head_rows, :] = (dq_ref[head] * 0.125).astype(BF16)
        return carry

    lax.fori_loop(0, heads, one_head, 0)
    if own:
        qg_ref[...] = qg_scr[...].T

    for jb in range(nb):
        t = jb * nb + ib

        @pl.when(scal[t] > 0)
        def _(jb=jb, t=t):
            least = scal[n2 + t]
            most = scal[2 * n2 + t]
            spots = range(jb * tile, (jb + 1) * tile, 32)

            def some(b):
                totals = [jnp.zeros((8, tile), F32) for _ in range(heads)]
                for r in spots:
                    hit = idx_ref[0, r : r + 32, :] == b
                    for head in range(heads):
                        part = jnp.where(hit, ds_scr[head, r : r + 32, :], 0.0)
                        totals[head] += jnp.sum(part.reshape(4, 8, tile), axis=0)
                for head in range(heads):
                    acc_scr[head, b] += totals[head]
                return totals

            if own:

                @pl.loop(jnp.maximum(least, BAND), most + 1)
                def _(b):
                    some(b)

            else:
                rest = [jnp.zeros((8, tile), F32) for _ in range(heads)]
                for head in range(heads):
                    for r in spots:
                        rest[head] += jnp.sum(
                            ds_scr[head, r : r + 32, :].reshape(4, 8, tile), axis=0
                        )

                def less(b, left):
                    return tuple(one - other for one, other in zip(left, some(b)))

                rest = lax.fori_loop(least + 1, most + 1, less, tuple(rest))
                for head in range(heads):
                    acc_scr[head, least] += rest[head]

    if own:
        def band_of(key_at, keys, lane_at):
            here = pl.ds(pl.multiple_of(key_at, BAND), keys)
            near = idx_ref[0, here, lane_at : lane_at + 128] < BAND
            for head in range(heads):
                band_scr[head, 128 - keys :, :] += jnp.where(
                    near, ds_scr[head, here, lane_at : lane_at + 128], 0.0
                )

        for lane_at in range(0, tile, 128):
            band_of(ib * tile + lane_at, 128, lane_at)
            if lane_at > 0:
                band_of(ib * tile + lane_at - BAND, BAND, lane_at)

        @pl.when(ib > 0)
        def _():
            @pl.when(scal[jnp.maximum(ib - 1, 0) * nb + ib] > 0)
            def _():
                band_of(ib * tile - BAND, BAND, 0)

    @pl.when(ib == nb - 1)
    def _():
        dkv_out[...] = dkv_scr[...].astype(dkv_out.dtype)
        for head in range(heads):
            folded = jnp.sum(acc_scr[head], axis=1)
            bias = folded[:, :128]
            for c in range(1, tile // 128):
                bias = bias + folded[:, c * 128 : (c + 1) * 128]
            bias_ref[head, :NBUCKET, :] = bias
            if own:
                square = (128, 128)
                reverse = (
                    lax.broadcasted_iota(I32, square, 0) + lax.broadcasted_iota(I32, square, 1)
                    == 127
                ).astype(BF16)
                band = band_scr[head]
                upper = band.astype(BF16)
                lower = (band - upper.astype(F32)).astype(BF16)
                turned = jnp.dot(reverse, upper, preferred_element_type=F32) + jnp.dot(
                    reverse, lower, preferred_element_type=F32
                )
                turned = pltpu.roll(turned, 0, 1, stride=1, stride_axis=0)
                bias_ref[head, NBUCKET:, :] = jnp.sum(turned.reshape(16, 8, 128), axis=0)
            else:
                bias_ref[head, NBUCKET:, :] = jnp.zeros((8, 128), F32)


def buckets_of(scal, qpos, qseg, kpos, kseg, tile):
    planes, rows = kpos.shape[:2]
    nb = rows // tile
    return pl.pallas_call(
        functools.partial(bucket_kernel, nb, tile),
        grid=(planes,),
        in_specs=[
            pl.BlockSpec(memory_space=pltpu.SMEM),
            pl.BlockSpec((1, rows), lambda p: (0, 0)),
            pl.BlockSpec((1, rows), lambda p: (0, 0)),
            pl.BlockSpec((1, rows, 128), lambda p: (p, 0, 0)),
            pl.BlockSpec((1, rows, 128), lambda p: (p, 0, 0)),
        ],
        out_specs=pl.BlockSpec((1, rows, rows), lambda p: (p, 0, 0)),
        out_shape=jax.ShapeDtypeStruct((planes, rows, rows), I32),
        compiler_params=pltpu.CompilerParams(
            dimension_semantics=("arbitrary",), vmem_limit_bytes=VMEM_LIMIT
        ),
        cost_estimate=pl.CostEstimate(
            flops=planes * rows * rows * 16,
            bytes_accessed=planes * rows * rows * 4,
            transcendentals=0,
        ),
    )(scal, qpos, qseg, kpos, kseg)


def forward_piece(k, last, scal, q_t, kv, table, idx, state, tile):
    heads = table.shape[0]
    rows = kv.shape[0]
    nb = rows // tile
    head_cols = heads * HEAD_DIM
    column = lambda *shape: pl.BlockSpec(
        shape + (tile,), lambda i: (0,) * len(shape) + (i,)
    )
    in_specs = [
        pl.BlockSpec(memory_space=pltpu.SMEM),
        column(head_cols),
        pl.BlockSpec((rows, 2 * head_cols), lambda i: (0, 0)),
        pl.BlockSpec((heads, 8, 128), lambda i: (0, 0, 0)),
        pl.BlockSpec((1, rows, tile), lambda i: (k, 0, i)),
    ]
    args = [scal, q_t, kv, table, idx]
    if k > 0:
        in_specs += [column(heads, 1), column(heads, 1), column(heads, HEAD_DIM)]
        args += list(state)
    pairs = heads * rows * rows
    out_specs = [column(heads, rows), column(heads, 1), column(heads, 1), column(heads, HEAD_DIM)]
    out_shape = [
        jax.ShapeDtypeStruct((heads, rows, rows), BF16),
        jax.ShapeDtypeStruct((heads, 1, rows), F32),
        jax.ShapeDtypeStruct((heads, 1, rows), F32),
        jax.ShapeDtypeStruct((heads, HEAD_DIM, rows), F32),
    ]
    scratch_shapes = [
        pltpu.VMEM((rows, tile), F32),
        pltpu.VMEM((2 * head_cols, rows), BF16),
    ]
    if last:
        out_specs.append(pl.BlockSpec((tile, head_cols), lambda i: (i, 0)))
        out_shape.append(jax.ShapeDtypeStruct((rows, head_cols), BF16))
        scratch_shapes.append(pltpu.VMEM((head_cols, tile), BF16))
    return pl.pallas_call(
        functools.partial(forward_kernel, k == 0, last, nb, tile, heads),
        grid=(nb,),
        in_specs=in_specs,
        out_specs=out_specs,
        out_shape=out_shape,
        scratch_shapes=scratch_shapes,
        compiler_params=pltpu.CompilerParams(
            dimension_semantics=("arbitrary",), vmem_limit_bytes=VMEM_LIMIT
        ),
        cost_estimate=pl.CostEstimate(
            flops=pairs * 4 * 128, bytes_accessed=pairs * 4, transcendentals=pairs
        ),
    )(*args)


def backward_piece(k, scal, q_t, do_t, kv, probs, idx, factor, delta, dq, tile):
    heads = probs.shape[0]
    rows = kv.shape[0]
    nb = rows // tile
    start = dq is None
    own = k == 0
    head_cols = heads * HEAD_DIM
    column = lambda *shape: pl.BlockSpec(
        shape + (tile,), lambda i: (0,) * len(shape) + (i,)
    )
    in_specs = [
        pl.BlockSpec(memory_space=pltpu.SMEM),
        column(head_cols),
        column(head_cols),
        pl.BlockSpec((rows, 2 * head_cols), lambda i: (0, 0)),
        column(heads, rows),
        pl.BlockSpec((1, rows, tile), lambda i: (k, 0, i)),
        column(heads, 1),
        column(heads, 1),
    ]
    args = [scal, q_t, do_t, kv, probs, idx, factor, delta]
    if not start:
        in_specs += [column(heads, HEAD_DIM)]
        args += [dq]
    pairs = heads * rows * rows
    out_specs = [
        pl.BlockSpec((rows, 2 * head_cols), lambda i: (0, 0)),
        column(heads, HEAD_DIM),
        pl.BlockSpec((heads, NBUCKET + 8, 128), lambda i: (0, 0, 0)),
    ]
    out_shape = [
        jax.ShapeDtypeStruct((rows, 2 * head_cols), F32 if own else BF16),
        jax.ShapeDtypeStruct((heads, HEAD_DIM, rows), F32),
        jax.ShapeDtypeStruct((heads, NBUCKET + 8, 128), F32),
    ]
    scratch_shapes = [
        pltpu.VMEM((heads, rows, tile), F32),
        pltpu.VMEM((rows, tile), BF16),
        pltpu.VMEM((heads, NBUCKET, 8, tile), F32),
        pltpu.VMEM((2 * head_cols, rows), BF16),
    ]
    if own:
        out_specs.append(pl.BlockSpec((tile, head_cols), lambda i: (i, 0)))
        out_shape.append(jax.ShapeDtypeStruct((rows, head_cols), BF16))
        scratch_shapes.append(pltpu.VMEM((heads, 128, 128), F32))
    scratch_shapes.append(pltpu.VMEM((rows, 2 * head_cols), F32))
    if own:
        scratch_shapes.append(pltpu.VMEM((head_cols, tile), BF16))
    return pl.pallas_call(
        functools.partial(backward_kernel, start, own, nb, tile, heads),
        grid=(nb,),
        in_specs=in_specs,
        out_specs=out_specs,
        out_shape=out_shape,
        scratch_shapes=scratch_shapes,
        compiler_params=pltpu.CompilerParams(
            dimension_semantics=("arbitrary",), vmem_limit_bytes=VMEM_LIMIT
        ),
        cost_estimate=pl.CostEstimate(
            flops=pairs * 8 * 128, bytes_accessed=pairs * 4, transcendentals=0
        ),
    )(*args)


GELU_SCALE = 0.7978845608028654
GELU_CUBE = 0.044715


def expert_kernel(
    steps,
    blocks,
    rows_ref,
    grads_ref,
    gate_ref,
    signs_ref,
    router_ref,
    win_ref,
    wout_ref,
    hidden_ref,
    pre_ref,
    row_ref,
    slope_ref,
    acc_scr,
    gate_scr,
):
    step = pl.program_id(0)

    @pl.when(step == 0)
    def _():
        acc_scr[...] = jnp.zeros_like(acc_scr)
        gate_scr[...] = jnp.zeros_like(gate_scr)

    size = rows_ref.shape[0] // blocks
    pair = (((1,), (1,)), ((), ()))
    for block in range(blocks):
        here = slice(block * size, (block + 1) * size)
        pre = jnp.dot(rows_ref[here, :], win_ref[...], preferred_element_type=F32)
        raw = lax.dot_general(
            grads_ref[here, :], wout_ref[...], pair, preferred_element_type=F32
        )
        square = pre * pre
        turn = jnp.tanh(pre * (GELU_SCALE + (GELU_SCALE * GELU_CUBE) * square))
        half = 0.5 + 0.5 * turn
        hidden = (pre * half).astype(BF16)
        hidden_ref[here, :] = hidden
        product = raw * hidden.astype(F32)
        lanes = gate_scr.shape[1]
        gate_scr[here, :] += sum(
            product[:, at : at + lanes] for at in range(0, product.shape[1], lanes)
        )
        slope = half + (pre * (1.0 - turn * turn)) * (
            0.5 * GELU_SCALE + (1.5 * GELU_SCALE * GELU_CUBE) * square
        )
        pre_grad = (raw * gate_ref[here, :] * slope).astype(BF16)
        pre_ref[here, :] = pre_grad
        acc_scr[here, :] += lax.dot_general(
            pre_grad, win_ref[...], pair, preferred_element_type=F32
        )

    @pl.when(step == steps - 1)
    def _():
        gate = gate_ref[...]
        slope = gate * (1.0 - gate) * jnp.sum(gate_scr[...], axis=1, keepdims=True)
        logit = slope * signs_ref[...]
        high = logit.astype(BF16)
        low = (logit - high.astype(F32)).astype(BF16)
        routed = lax.dot_general(high, router_ref[...], pair, preferred_element_type=F32)
        routed += lax.dot_general(low, router_ref[...], pair, preferred_element_type=F32)
        row_ref[...] = (acc_scr[...] + routed).astype(BF16)
        slope_ref[...] = slope


def expert_pass(rows, grads, gate, signs, router, w_in, w_out):
    count, width = rows.shape
    units = w_in.shape[1]
    experts = router.shape[1]
    tile = 768 if units % 768 == 0 else units
    steps = units // tile
    blocks = 1
    whole = lambda *shape: pl.BlockSpec(shape, lambda f: (0,) * len(shape))
    return pl.pallas_call(
        functools.partial(expert_kernel, steps, blocks),
        grid=(steps,),
        in_specs=[
            whole(count, width),
            whole(count, width),
            whole(count, 1),
            whole(count, experts),
            whole(width, experts),
            pl.BlockSpec((width, tile), lambda f: (0, f)),
            pl.BlockSpec((tile, width), lambda f: (f, 0)),
        ],
        out_specs=[
            pl.BlockSpec((count, tile), lambda f: (0, f)),
            pl.BlockSpec((count, tile), lambda f: (0, f)),
            whole(count, width),
            whole(count, 1),
        ],
        out_shape=[
            jax.ShapeDtypeStruct((count, units), BF16),
            jax.ShapeDtypeStruct((count, units), BF16),
            jax.ShapeDtypeStruct((count, width), BF16),
            jax.ShapeDtypeStruct((count, 1), F32),
        ],
        scratch_shapes=[
            pltpu.VMEM((count, width), F32),
            pltpu.VMEM((count, 128 if tile % 128 == 0 else tile), F32),
        ],
        compiler_params=pltpu.CompilerParams(
            dimension_semantics=("arbitrary",), vmem_limit_bytes=VMEM_LIMIT
        ),
        cost_estimate=pl.CostEstimate(
            flops=6 * count * width * units,
            bytes_accessed=4 * width * units + 4 * count * units + 6 * count * width,
            transcendentals=count * units,
        ),
    )(rows, grads, gate, signs, router, w_in, w_out)


def shards(
    block_input,
    w_qkv,
    w_attn_out,
    w_router,
    gain_attn,
    gain_moe,
    rel_bias,
    w_in,
    w_out,
    routes,
    segment_ids,
    bucket_table,
    out_grad,
):
    tok_rows, width = block_input.shape
    planes = lax.axis_size("pl")
    group = lax.axis_size("fx") * lax.axis_size("wsh")
    devices = planes * group
    cores = lax.axis_size("grp")
    plane_rank = lax.axis_index("pl")
    place = lax.axis_index(PLANE)
    device_rank = plane_rank * group + place
    core_rank = lax.axis_index("grp")
    heads = HEADS // group
    head_cols = heads * HEAD_DIM
    rows = tok_rows * group
    w_rows = w_qkv.shape[1]
    expert_count = w_router.shape[1]
    bias_share = rel_bias.shape[0]

    split = cores if w_rows % cores == 0 else 1
    part_rows = w_rows // split

    def own_part(array, axis):
        if split == 1:
            return array
        return lax.dynamic_slice_in_dim(array, core_rank * part_rows, part_rows, axis)

    def join_parts(array):
        if split > 1:
            both = lax.all_gather(array, "grp", axis=0, tiled=False)
            array = jnp.transpose(both, (1, 0, 2, 3))
        return array.reshape(devices * w_rows, array.shape[-1])

    def exchange(array, axes=ALL):
        return lax.all_to_all(array, axes, split_axis=0, concat_axis=0, tiled=True)

    def plane_send(block_of):
        came = [block_of(0)]
        for j in range(1, group):
            onward = [(i, (i + j) % group) for i in range(group)]
            came.append(lax.ppermute(block_of(j), PLANE, onward))
        return [came[-i % group] for i in range(group)]

    def in_place_order(blocks):
        size = blocks[0].shape[0]
        twice = jnp.concatenate(blocks + blocks[:-1], axis=0)
        return lax.dynamic_slice_in_dim(twice, (-place % group) * size, size * group, 0)

    capacity = max(2, 4 * tok_rows // expert_count)
    expert_ids = jnp.arange(expert_count, dtype=I32)
    route_hits = routes[:, :, None] == expert_ids[None, None, :]
    flat_hits = route_hits.reshape(tok_rows * 2, expert_count)
    order = jnp.arange(tok_rows * 2, dtype=I32)
    earlier = (order[:, None] > order[None, :]).astype(BF16)
    ranks = jnp.dot(earlier, flat_hits.astype(BF16), preferred_element_type=F32)
    slot_ranks = jnp.sum(jnp.where(flat_hits, ranks, 0.0), axis=1).astype(I32)
    slot_ids = routes * capacity + slot_ranks.reshape(tok_rows, 2)
    slot_count = expert_count * capacity
    slot_numbers = jnp.arange(slot_count, dtype=I32)
    hit_first = slot_numbers[:, None] == slot_ids[None, :, 0]
    hit_second = slot_numbers[:, None] == slot_ids[None, :, 1]
    table_first = hit_first.astype(BF16)
    table_second = hit_second.astype(BF16)
    slot_table = table_first + table_second
    other_expert = jnp.sum(
        jnp.where(hit_first, routes[None, :, 1], 0) + jnp.where(hit_second, routes[None, :, 0], 0),
        axis=1,
    )

    plane_input = in_place_order(plane_send(lambda j: block_input))

    def join_small(rows_of, small_of):
        count, height = rows_of.shape[:2]
        spare = -(-small_of.shape[1] // height)
        small_of = jnp.pad(small_of, ((0, 0), (0, spare * height - small_of.shape[1])))
        return jnp.concatenate([rows_of, small_of.reshape(count, height, spare)], axis=2)

    qkv_part = own_part(w_qkv, 1)
    q_part = qkv_part[0].reshape(part_rows, group, head_cols)
    kv_part = qkv_part[1:].reshape(2, part_rows, group, heads, HEAD_DIM)
    kv_part = jnp.transpose(kv_part, (1, 2, 3, 0, 4)).reshape(part_rows, group, 2 * head_cols)
    qkv_pay = jnp.transpose(jnp.concatenate([q_part, kv_part], axis=2), (1, 0, 2))
    small = jnp.concatenate([w_router.reshape(-1), gain_attn, gain_moe, rel_bias])
    pay_cols = 3 * head_cols
    small_count = small.shape[0]
    small = jnp.concatenate(
        [
            jnp.broadcast_to(small[None], (devices, small_count)),
            other_expert.astype(BF16).reshape(devices, capacity),
        ],
        axis=1,
    )
    qkv_pay = jnp.broadcast_to(qkv_pay[None], (planes,) + qkv_pay.shape)
    qkv_pay = qkv_pay.reshape(devices, part_rows, pay_cols)
    out_pay = jnp.broadcast_to(own_part(w_attn_out, 0)[None], (devices, part_rows, width))
    qkv_pay = join_small(jnp.concatenate([qkv_pay, out_pay], axis=2), small)
    qkv_got = lax.all_to_all(qkv_pay, ALL, split_axis=0, concat_axis=0, tiled=True)
    positions = positions_of(segment_ids)
    bucket_ids = jnp.arange(NBUCKET, dtype=I32)
    edges = jnp.sum((bucket_table[None, :] < bucket_ids[:, None]).astype(I32), axis=1)
    tile = 256 if rows % 256 == 0 else rows
    nb = rows // tile

    def ranges_of(plane):
        first = jnp.maximum(plane, 0) * rows
        pos = lax.dynamic_slice_in_dim(positions, first, rows)
        seg = lax.dynamic_slice_in_dim(segment_ids, first, rows)
        pos_t, seg_t = pos.reshape(nb, tile), seg.reshape(nb, tile)
        limits = (
            jnp.min(pos_t, axis=1),
            jnp.max(pos_t, axis=1),
            jnp.min(seg_t, axis=1),
            jnp.max(seg_t, axis=1),
        )
        return first, pos, seg, limits

    q_first, q_pos, q_seg, (q_pos_min, q_pos_max, q_seg_min, q_seg_max) = ranges_of(plane_rank)
    tile_ids = jnp.arange(nb, dtype=I32)

    def bucket_of(distance):
        return jnp.sum((distance[:, :, None] >= edges[None, None, 1:]).astype(I32), axis=2)

    scal_of, key_info = [], []
    for k in range(planes):
        plane = plane_rank - k
        k_first, k_pos, k_seg, (k_pos_min, k_pos_max, k_seg_min, k_seg_max) = ranges_of(plane)
        causal = (k_first + tile_ids * tile)[:, None] <= (q_first + tile_ids * tile + tile - 1)[
            None, :
        ]
        own = jnp.logical_or(
            (k_seg_min == 0)[:, None],
            jnp.logical_and(
                k_seg_min[:, None] <= q_seg_max[None, :], k_seg_max[:, None] >= q_seg_min[None, :]
            ),
        )
        flags = jnp.logical_and(jnp.logical_and(causal, own), plane >= 0).astype(I32)
        least = bucket_of(jnp.maximum(q_pos_min[None, :] - k_pos_max[:, None], 0))
        most = bucket_of(jnp.maximum(q_pos_max[None, :] - k_pos_min[:, None], 0))
        beyond = jnp.logical_and(k == 0, tile_ids[:, None] > tile_ids[None, :])
        full = jnp.min(jnp.where(beyond, 1, flags), axis=0)
        scal_of.append(
            jnp.concatenate(
                [
                    flags.reshape(-1),
                    least.reshape(-1),
                    most.reshape(-1),
                    full,
                    edges,
                    jnp.full((EDGE_GROUP,), 1 << 30, I32),
                    jnp.stack([q_first, k_first]).astype(I32),
                ]
            )
        )
        key_info.append((k_pos, k_seg))
    plane_inverse = norm_inverse(plane_input.astype(F32))
    scal_all, plane_input, plane_inverse = lax.optimization_barrier(
        (jnp.stack(scal_of), plane_input, plane_inverse)
    )
    plane_wide = plane_input.astype(F32)
    bucket_idx = buckets_of(
        scal_all,
        q_pos[None, :],
        q_seg[None, :],
        jnp.broadcast_to(
            jnp.stack([info[0] for info in key_info])[:, :, None], (planes, rows, 128)
        ),
        jnp.broadcast_to(
            jnp.stack([info[1] for info in key_info])[:, :, None], (planes, rows, 128)
        ),
        tile,
    )

    qkv_got, bucket_idx = lax.optimization_barrier((qkv_got, bucket_idx))
    w_heads = join_parts(qkv_got[:, :, :pay_cols])
    half_cols = pay_cols + width // 2
    gathered_out = jnp.concatenate(
        [
            join_parts(qkv_got[:, :, pay_cols:half_cols]),
            join_parts(qkv_got[:, :, half_cols : pay_cols + width]),
        ],
        axis=1,
    )
    small_got = qkv_got[:, :, pay_cols + width :].reshape(devices, -1)
    router_size = w_rows * expert_count
    full_router = small_got[:, :router_size].reshape(width, expert_count)
    at = router_size
    gain_attn_full = small_got[:, at : at + w_rows].reshape(width).astype(F32)
    at += w_rows
    gain_moe_full = small_got[:, at : at + w_rows].reshape(width).astype(F32)
    at += w_rows
    bias_full = small_got[:, at : at + bias_share].reshape(HEADS, NBUCKET).astype(F32)
    at += bias_share
    other_arrived = small_got[:, at : at + capacity].reshape(slot_count).astype(F32)
    w_query = w_heads[:, :head_cols]
    w_keyval = w_heads[:, head_cols:]

    attn_in = (plane_wide * plane_inverse * gain_attn_full).astype(BF16)
    q_t = lax.dot_general(
        w_query, attn_in, (((0,), (1,)), ((), ())), preferred_element_type=F32
    ).astype(BF16)
    keyval = jnp.dot(attn_in, w_keyval, preferred_element_type=F32).astype(BF16)
    bias_local = lax.dynamic_slice_in_dim(bias_full, place * heads, heads, 0) * LOG2E
    bias_table = jnp.concatenate(
        [bias_local, jnp.full((heads, 128 - NBUCKET), NEGATIVE, F32)], axis=1
    )
    bias_table = jnp.broadcast_to(bias_table[:, None, :], (heads, 8, 128))

    upward = [(i, i + 1) for i in range(planes - 1)]
    downward = [(i + 1, i) for i in range(planes - 1)]
    grad_send = jnp.dot(slot_table, out_grad, preferred_element_type=F32).astype(BF16)
    kv_pieces, probs, tops, state = [keyval], [], [], None
    travelling = lax.ppermute(keyval, "pl", upward) if planes > 1 else None
    for k in range(planes):
        made = forward_piece(
            k,
            k == planes - 1,
            scal_of[k],
            q_t,
            kv_pieces[k],
            bias_table,
            bucket_idx,
            state,
            tile,
        )
        probs.append(made[0])
        state = made[1:4]
        tops.append(made[1])
        if k == planes - 1:
            break
        if k == planes - 2:
            travelling, state, grad_send, gathered_out = lax.optimization_barrier(
                (travelling, state, grad_send, gathered_out)
            )
        else:
            travelling, state = lax.optimization_barrier((travelling, state))
        kv_pieces.append(travelling)
        if k + 2 < planes:
            travelling = lax.ppermute(travelling, "pl", upward)
    grad_raw = exchange(grad_send.reshape(expert_count, capacity, width)).reshape(
        slot_count, width
    )
    final_top, final_sum, out_sum = state
    mixed_own = made[4].reshape(group, tok_rows, head_cols)
    mixed = jnp.concatenate(
        plane_send(lambda j: lax.dynamic_index_in_dim(mixed_own, (place + j) % group, 0, False)),
        axis=1,
    )
    turned_out = lax.dynamic_slice_in_dim(
        jnp.concatenate([gathered_out, gathered_out], axis=0), place * head_cols, width, 0
    )

    input_wide = block_input.astype(F32)
    residual = input_wide + jnp.dot(mixed, turned_out, preferred_element_type=F32)
    inverse_moe = norm_inverse(residual)
    moe_in = (residual * inverse_moe * gain_moe_full).astype(BF16)
    outgoing = jnp.dot(slot_table, moe_in, preferred_element_type=F32).astype(BF16)
    outgoing, grad_raw = lax.optimization_barrier((outgoing, grad_raw))
    arrived = lax.all_to_all(
        outgoing.reshape(expert_count, capacity, width), ALL, split_axis=0, concat_axis=0, tiled=True
    ).reshape(slot_count, width)
    logits = jnp.dot(moe_in, full_router, preferred_element_type=F32)
    chosen = jnp.sum(jnp.where(route_hits, logits[:, None, :], 0.0), axis=2)
    gate_probs = jax.nn.softmax(chosen, axis=1)

    expert_in = w_in[0]
    expert_out = w_out[0]
    row_logits = jnp.dot(arrived, full_router, preferred_element_type=F32)
    own_logit = jnp.sum(jnp.where(expert_ids[None, :] == device_rank, row_logits, 0.0), axis=1)
    other_logit = jnp.sum(
        jnp.where(expert_ids[None, :].astype(F32) == other_arrived[:, None], row_logits, 0.0), axis=1
    )
    top_logit = jnp.maximum(own_logit, other_logit)
    own_part_exp = jnp.exp(own_logit - top_logit)
    row_gate = own_part_exp / (own_part_exp + jnp.exp(other_logit - top_logit))
    grad_wide = grad_raw.astype(F32)
    made_grad = (row_gate[:, None] * grad_wide).astype(BF16)

    signs = (expert_ids[None, :] == device_rank).astype(F32) - (
        expert_ids[None, :].astype(F32) == other_arrived[:, None]
    ).astype(F32)
    hidden, pre_grad, row_grad, row_slope = expert_pass(
        arrived, grad_raw, row_gate[:, None], signs, full_router, expert_in, expert_out
    )
    row_logit_grad = row_slope * signs
    logit_high = row_logit_grad.astype(BF16)
    logit_low = (row_logit_grad - logit_high.astype(F32)).astype(BF16)
    row_logit_grad = jnp.concatenate([logit_high, logit_low], axis=1)
    returned_grads = lax.all_to_all(
        row_grad.reshape(expert_count, capacity, width),
        ALL,
        split_axis=0,
        concat_axis=0,
        tiled=True,
    ).reshape(slot_count, width)
    hidden_late, made_late, row_grad = lax.optimization_barrier((hidden, made_grad, row_grad))
    expert_made = jnp.dot(hidden_late, expert_out, preferred_element_type=F32).astype(BF16)
    w_out_grad = lax.dot_general(
        hidden_late, made_late, (((0,), (0,)), ((), ())), preferred_element_type=F32
    )[None]
    router_pair = lax.dot_general(
        arrived, row_logit_grad, (((0,), (0,)), ((), ())), preferred_element_type=F32
    )
    router_grad = router_pair[:, :expert_count] + router_pair[:, expert_count:]
    returned_grads, expert_made, w_out_grad = lax.optimization_barrier(
        (returned_grads, expert_made, w_out_grad)
    )
    moe_in_grad = lax.dot_general(
        slot_table, returned_grads, (((0,), (0,)), ((), ())), preferred_element_type=F32
    )
    grad_out = out_grad.astype(F32)
    residual_grad = grad_out + norm_input_grad(residual, inverse_moe, gain_moe_full, moe_in_grad)
    branch_grad = residual_grad.astype(BF16)
    mixed_grad = lax.dot_general(
        branch_grad, turned_out, (((1,), (1,)), ((), ())), preferred_element_type=F32
    ).astype(BF16)
    grad_rows = plane_send(lambda j: mixed_grad[:, j * head_cols : (j + 1) * head_cols])
    grad_rows, expert_made = lax.optimization_barrier((grad_rows, expert_made))
    grad_t = in_place_order(grad_rows).T
    returned = exchange(expert_made.reshape(expert_count, capacity, width)).reshape(
        slot_count, width
    )

    head_out_t = out_sum / final_sum
    delta = jnp.sum(
        grad_t.astype(F32).reshape(heads, HEAD_DIM, rows) * head_out_t, axis=1, keepdims=True
    )
    query_grad, carried, bias_parts = None, None, []
    for k in reversed(range(planes)):
        factor = jnp.exp2(tops[k] - final_top) / final_sum
        dkv, query_grad, bias_part, *query_rows = backward_piece(
            k,
            scal_of[k],
            q_t,
            grad_t,
            kv_pieces[k],
            probs[k],
            bucket_idx,
            factor,
            delta,
            query_grad,
            tile,
        )
        bias_parts.append(bias_part)
        if carried is None:
            total = dkv
        else:
            carried, dkv, query_grad, query_rows = lax.optimization_barrier(
                (carried, dkv, query_grad, query_rows)
            )
            total = dkv.astype(F32) + carried.astype(F32)
        if k == 0:
            break
        sent = total.astype(BF16)
        if k == planes - 1:
            sent, query_grad, branch_late = lax.optimization_barrier(
                (sent, query_grad, branch_grad)
            )
        elif k == planes - 2:
            sent, query_grad, returned = lax.optimization_barrier((sent, query_grad, returned))
        carried = lax.ppermute(sent, "pl", downward)
        if k == planes - 1:
            attn_out_part = lax.dot_general(
                mixed, branch_late, (((0,), (0,)), ((), ())), preferred_element_type=F32
            )
            attn_out_part = lax.dynamic_slice_in_dim(
                jnp.concatenate([attn_out_part, attn_out_part], axis=0),
                width - place * head_cols,
                width,
                0,
            )
            attn_out_part = attn_out_part.astype(BF16).reshape(planes, group, w_rows, width)
            attn_out_part = sum(
                block.astype(F32)
                for block in plane_send(
                    lambda j: lax.dynamic_index_in_dim(
                        attn_out_part, (place + j) % group, 1, False
                    )
                )
            ).astype(BF16)
            gain_moe_grad = jnp.sum(moe_in_grad * residual * inverse_moe, axis=0)
    scale_row = jnp.tile(
        jnp.concatenate([jnp.full((HEAD_DIM,), 0.125, F32), jnp.ones((HEAD_DIM,), F32)]), heads
    )
    keyval_grad = (total * scale_row[None, :]).astype(BF16)
    query_grad = query_rows[0]
    bias_rows_at = -(-bias_share // w_rows)
    bias_rows = sum(bias_parts)
    band_rows = jnp.roll(jnp.sum(bias_rows[:, NBUCKET:], axis=1), 1, axis=1)[:, :BAND]
    bias_grad = jnp.sum(bias_rows[:, :NBUCKET], axis=2) + jnp.pad(
        band_rows, ((0, 0), (0, NBUCKET - BAND))
    )

    w_query_part = lax.dot_general(
        attn_in, query_grad, (((0,), (0,)), ((), ())), preferred_element_type=F32
    )
    w_keyval_part = lax.dot_general(
        attn_in, keyval_grad, (((0,), (0,)), ((), ())), preferred_element_type=F32
    )
    gain_attn_grad = (
        jnp.sum(w_query_part * w_query.astype(F32), axis=1, keepdims=True)
        + jnp.sum(w_keyval_part * w_keyval.astype(F32), axis=1, keepdims=True)
    ) / gain_attn_full[:, None]
    bias_all = lax.dynamic_update_slice_in_dim(
        jnp.zeros((HEADS, NBUCKET), F32), bias_grad, place * heads, 0
    ).reshape(devices, bias_share)
    bias_all = jnp.pad(bias_all, ((0, 0), (0, bias_rows_at * w_rows - bias_share)))
    bias_all = jnp.transpose(bias_all.reshape(devices, bias_rows_at, w_rows), (0, 2, 1))
    small_grads = jnp.concatenate(
        [
            router_grad,
            gain_moe_grad[:, None],
            gain_attn_grad,
            bias_all.reshape(width, bias_rows_at),
        ],
        axis=1,
    )
    small_high = small_grads.astype(BF16)
    small_low = (small_grads - small_high.astype(F32)).astype(BF16)
    w_parts = jnp.concatenate(
        [w_query_part.astype(BF16), w_keyval_part.astype(BF16), small_high, small_low], axis=1
    ).reshape(devices, w_rows, -1)
    w_parts, query_grad, keyval_grad = lax.optimization_barrier(
        (w_parts, query_grad, keyval_grad)
    )
    w_got = exchange(w_parts)

    attn_in_grad = lax.dot_general(
        query_grad, w_query, (((1,), (1,)), ((), ())), preferred_element_type=F32
    ) + lax.dot_general(
        keyval_grad, w_keyval, (((1,), (1,)), ((), ())), preferred_element_type=F32
    )
    attn_in_grad = attn_in_grad.reshape(group, tok_rows, width)
    pre_late, attn_out_part, w_parts = lax.optimization_barrier(
        (pre_grad, attn_out_part, w_parts)
    )
    attn_out_came = [lax.dynamic_index_in_dim(attn_out_part, plane_rank, 0, False)]
    for j in range(1, planes):
        onward = [(i, (i + j) % planes) for i in range(planes)]
        block = lax.dynamic_index_in_dim(attn_out_part, (plane_rank + j) % planes, 0, False)
        attn_out_came.append(lax.ppermute(block, "pl", onward))
    w_in_grad = lax.dot_general(
        arrived, pre_late, (((0,), (0,)), ((), ())), preferred_element_type=F32
    )[None]
    attn_in_grad, w_in_grad = lax.optimization_barrier((attn_in_grad, w_in_grad))
    came = plane_send(
        lambda j: lax.dynamic_index_in_dim(attn_in_grad, (place + j) % group, 0, False).astype(BF16)
    )
    attn_in_grad = sum(block.astype(F32) for block in came)
    attn_out_grad = sum(block.astype(F32) for block in attn_out_came)
    inverse_attn = norm_inverse(input_wide)
    input_grad = residual_grad + norm_input_grad(
        input_wide, inverse_attn, gain_attn_full, attn_in_grad
    )


    picked_first = lax.dot_general(
        table_first, returned, (((0,), (0,)), ((), ())), preferred_element_type=F32
    )
    picked_second = lax.dot_general(
        table_second, returned, (((0,), (0,)), ((), ())), preferred_element_type=F32
    )
    block_output = (
        residual + (gate_probs[:, 0:1] * picked_first + gate_probs[:, 1:2] * picked_second)
    ).astype(BF16)
    w_got, w_in_grad, block_output = lax.optimization_barrier((w_got, w_in_grad, block_output))

    w_wide = w_got.astype(F32)
    w_sum = jnp.sum(w_wide[:, :, :pay_cols].reshape(planes, group, w_rows, pay_cols), axis=0)
    q_sum = jnp.transpose(w_sum[:, :, :head_cols], (1, 0, 2)).reshape(1, w_rows, width)
    kv_sum = w_sum[:, :, head_cols:].reshape(group, w_rows, heads, 2, HEAD_DIM)
    kv_sum = jnp.transpose(kv_sum, (3, 1, 0, 2, 4)).reshape(2, w_rows, width)
    qkv_grad = jnp.concatenate([q_sum, kv_sum], axis=0)
    small_sum = jnp.sum(w_wide[:, :, pay_cols:], axis=0)
    columns = expert_count + 2 + bias_rows_at
    small_sum = small_sum[:, :columns] + small_sum[:, columns:]
    bias_sum = jnp.transpose(small_sum[:, expert_count + 2 :]).reshape(-1)[:bias_share]
    return (
        block_output,
        input_grad,
        qkv_grad,
        attn_out_grad,
        small_sum[:, :expert_count],
        small_sum[:, expert_count + 1],
        small_sum[:, expert_count],
        bias_sum,
        w_in_grad,
        w_out_grad,
    )


def solution(mesh):
    devices = mesh.devices
    grp, seq, wsh = devices.shape
    inner = Mesh(devices.reshape(grp, seq // 2, 2, wsh), ("grp",) + ALL)
    every = ("grp",) + ALL
    in_specs = (
        P(every, None),
        P(None, ALL, None),
        P(ALL, None),
        P(ALL, None),
        P(ALL),
        P(ALL),
        P(ALL),
        P(ALL, None, None),
        P(ALL, None, None),
        P(every, None),
        P("grp"),
        P(),
        P(every, None),
    )
    out_specs = (
        P(every, None),
        P(every, None),
        P("grp", ALL, None),
        P(every, None),
        P(every, None),
        P(every),
        P(every),
        P(every),
        P(every, None, None),
        P(every, None, None),
    )
    return jax.shard_map(
        shards, mesh=inner, in_specs=in_specs, out_specs=out_specs, check_vma=False
    )
```
